32 devices in a mesh: dp: 8 (over z, y), seq: 4 (over x, core).
Axes of the slice: x: 2, y: 2, z: 4, core: 2. Of those that a mesh axis runs over, the one named last changes fastest.
Arguments:
- tokens: bfloat16 [8, 4096, 1024], P('dp', 'seq'), may hold values from -6 to 6
- lengths: int32 [8, 8], P('dp'), may hold values from 1 to 2048, 3584 in all within a row
- cotangent: bfloat16 [8, 4096, 1024], P('dp', 'seq'), may hold values from -6 to 6
- norm_gain: float32 [1024], P(('dp', 'seq')), may hold values from 0.5 to 1.5
- norm_shift: float32 [1024], P(('dp', 'seq')), may hold values from -1.75 to 1.75
- value_weight: float32 [1024, 3072], P(('dp', 'seq')), may hold values from -0.1875 to 0.1875
- value_bias: float32 [3072], P(('dp', 'seq')), may hold values from -1.75 to 1.75
- reduce_weight: float32 [1024, 512], P(('dp', 'seq')), may hold values from -0.1875 to 0.1875
- reduce_bias: float32 [512], P(('dp', 'seq')), may hold values from -1.75 to 1.75
- decay_rates: float32 [512], P(('dp', 'seq')), may hold values from 6e-05 to 0.034
- skip_gain: float32 [512], P(('dp', 'seq')), may hold values from -6 to 6
- state_weight: float32 [512, 512], P(('dp', 'seq')), may hold values from -0.25 to 0.25
- expand_weight: float32 [512, 3072], P(('dp', 'seq')), may hold values from -0.25 to 0.25
- expand_bias: float32 [3072], P(('dp', 'seq')), may hold values from -1.75 to 1.75
- out_weight: float32 [3072, 1024], P(('dp', 'seq')), may hold values from -0.21875 to 0.21875
- out_bias: float32 [1024], P(('dp', 'seq')), may hold values from -1.75 to 1.75
Outputs:
- output: bfloat16 [8, 4096, 1024], P('dp', 'seq')
- grad_tokens: bfloat16 [8, 4096, 1024], P('dp', 'seq')
- grad_norm_gain: float32 [1024], P(('dp', 'seq'))
- grad_norm_shift: float32 [1024], P(('dp', 'seq'))
- grad_value_weight: float32 [1024, 3072], P(('dp', 'seq'))
- grad_value_bias: float32 [3072], P(('dp', 'seq'))
- grad_reduce_weight: float32 [1024, 512], P(('dp', 'seq'))
- grad_reduce_bias: float32 [512], P(('dp', 'seq'))
- grad_decay_rates: float32 [512], P(('dp', 'seq'))
- grad_skip_gain: float32 [512], P(('dp', 'seq'))
- grad_state_weight: float32 [512, 512], P(('dp', 'seq'))
- grad_expand_weight: float32 [512, 3072], P(('dp', 'seq'))
- grad_expand_bias: float32 [3072], P(('dp', 'seq'))
- grad_out_weight: float32 [3072, 1024], P(('dp', 'seq'))
- grad_out_bias: float32 [1024], P(('dp', 'seq'))
The draws below stay inside these ranges and needn't reach their ends.
Inputs may be any that keep to these rules, and one draw needn't show every extreme that they name: Each row's 8 lengths sum to 3584 and the rest of the row is padding; the largest length of each row is 2048.
All inputs are finite; a program needn't handle non-finite values.
Results may differ from the reference program's by a relative error of at most 0.011.
Values may be sent and summed in bfloat16 or wider, within the bound.
No kernel may reach another device: no remote copies, remote signals or barrier semaphores. Data moves between devices by JAX's collectives and lax.ppermute only.
A program may use at most 192 MiB of HBM per device.

```python
import math
import jax
import jax.numpy as jnp
import numpy as np
from jax import lax

D = 1024
GATE = 3072
RED = 512
LEN = 4096
NDOC = 8
ROWS = 8


def draw_decay_rates(key, part):
    uniform_part = jax.random.uniform(key, (RED,), jnp.float32)
    lower = jnp.log(0.5 / LEN)
    upper = jnp.log(1.0 / 30.0)
    return jnp.exp(lower + uniform_part * (upper - lower))


def shard_levels(key, dims, cuts, least, top_value):
    def one(position, parts):
        steps = jax.random.uniform(jax.random.fold_in(jax.random.fold_in(key, 6), position), (parts,), jnp.float32, least / len(cuts), top_value / len(cuts))
        return jnp.repeat(jnp.exp(steps), dims[position] // parts).reshape((-1,) + (1,) * (len(dims) - position - 1))

    loudness = one(*cuts[0])
    for cut in cuts[1:]:
        loudness = loudness * one(*cut)
    return loudness


def split_up(count, total, bound, skew):
    loads = [(1 << 20) // math.isqrt(grade ** skew) + 1 for grade in range(2, count + 1)]
    surplus, counts = total - bound - (count - 1), [1] * (count - 1)
    while surplus > 0:
        movable = [i for i in range(count - 1) if counts[i] < bound]
        pool, left = sum([loads[i] for i in movable]), surplus
        for i in movable:
            more = min(bound - counts[i], max(1, left * loads[i] // pool), surplus)
            counts[i] = counts[i] + more
            surplus = surplus - more
    return np.array([bound] + counts)


def ragged(stream_key, count, total, bound, skew):
    if count == 2:
        one = jax.random.randint(stream_key, (), max(1, total - bound), min(bound, total - 1) + 1)
        return jnp.stack([one, total - one])
    sizes = jnp.asarray(split_up(count, total, bound, skew), jnp.int32)
    twos = (count - 1) // 2
    source_of, sink = sizes[1:1 + 2 * twos:2], sizes[2:2 + 2 * twos:2]
    slack = jnp.minimum(source_of - 1, bound - sink)
    shifted = jax.random.randint(jax.random.fold_in(stream_key, 1), (twos,), 0, 1 << 20) % (slack + 1)
    sizes = sizes.at[1:1 + 2 * twos:2].set(source_of - shifted).at[2:2 + 2 * twos:2].set(sink + shifted)
    return sizes[jax.random.permutation(jax.random.fold_in(stream_key, 2), count)]


def normal_values(rng, shape, scale, bound, pieces=(), held_as=jnp.bfloat16):
    values = scale * jax.random.normal(rng, shape, jnp.float32)
    if pieces:
        values = values * shard_levels(rng, shape, pieces, -0.22, 0.18)
    return jnp.clip(values, -bound, bound).astype(held_as)


def setup_inputs(seed: int = 0) -> dict:
    keys = jax.random.split(jax.random.key(seed), 17)
    tokens = normal_values(keys[0], (ROWS, LEN, D), 1.0, 6.0, ((0, 8), (1, 4)))
    lengths = jax.vmap(lambda own: ragged(own, NDOC, LEN - LEN // 8, LEN // 2, 2))(jax.random.split(keys[1], ROWS)).reshape((ROWS, NDOC)).astype(jnp.int32)
    cotangent = normal_values(keys[2], (ROWS, LEN, D), 1.0, 6.0, ((0, 8), (1, 4)))
    norm_gain = jnp.clip(1.0 + 0.1 * jax.random.normal(keys[3], (D,), jnp.float32), 0.5, 1.5)
    norm_shift = normal_values(keys[4], (D,), 0.3, 1.75, ((0, 32),), jnp.float32)
    value_weight = normal_values(keys[5], (D, GATE), D ** -0.5, 0.1875, ((0, 32),), jnp.float32)
    value_bias = normal_values(keys[6], (GATE,), 0.3, 1.75, ((0, 32),), jnp.float32)
    reduce_weight = normal_values(keys[7], (D, RED), D ** -0.5, 0.1875, ((0, 32),), jnp.float32)
    reduce_bias = normal_values(keys[8], (RED,), 0.3, 1.75, ((0, 32),), jnp.float32)
    decay_rates = draw_decay_rates(jax.random.fold_in(keys[16], 71), 0)
    skip_gain = normal_values(keys[10], (RED,), 1.0, 6.0, ((0, 32),), jnp.float32)
    state_weight = normal_values(keys[11], (RED, RED), RED ** -0.5, 0.25, ((0, 32),), jnp.float32)
    expand_weight = normal_values(keys[12], (RED, GATE), RED ** -0.5, 0.25, ((0, 32),), jnp.float32)
    expand_bias = normal_values(keys[13], (GATE,), 0.3, 1.75, ((0, 32),), jnp.float32)
    out_weight = normal_values(keys[14], (GATE, D), (GATE // 4) ** -0.5, 0.21875, ((0, 32),), jnp.float32)
    out_bias = normal_values(keys[15], (D,), 0.3, 1.75, ((0, 32),), jnp.float32)
    return dict(tokens=tokens, lengths=lengths, cotangent=cotangent, norm_gain=norm_gain, norm_shift=norm_shift, value_weight=value_weight, value_bias=value_bias, reduce_weight=reduce_weight, reduce_bias=reduce_bias, decay_rates=decay_rates, skip_gain=skip_gain, state_weight=state_weight, expand_weight=expand_weight, expand_bias=expand_bias, out_weight=out_weight, out_bias=out_bias)


@jax.custom_vjp
def low(v):
    return lax.optimization_barrier(v.astype(jnp.bfloat16)).astype(jnp.float32)

@jax.custom_vjp
def low_back(v):
    return v

def low_keep(v):
    return (low(v), None)

def low_pass(kept, grad):
    return (grad,)

def back_keep(v):
    return (v, None)

def back_low(kept, grad):
    return (low(grad),)
low.defvjp(low_keep, low_pass)
low_back.defvjp(back_keep, back_low)
EPSILON = 1e-05

def matmul_high(left, right):
    return jnp.dot(left, right, precision=lax.Precision.HIGHEST, preferred_element_type=jnp.float32)

def compose(earlier, latter):
    return (earlier[0] * latter[0], latter[0] * earlier[1] + latter[1])

def layer_norm(token_rows, scale, offset):
    center = token_rows - lax.optimization_barrier(jnp.mean(token_rows, axis=-1, keepdims=True))
    inverse = lax.rsqrt(lax.optimization_barrier(jnp.mean(center * center, axis=-1, keepdims=True)) + EPSILON)
    return center * inverse * scale + offset

def decay_terms(rates):
    return (jnp.exp(-rates), jnp.sqrt(-jnp.expm1(-2.0 * rates)))

def row_flags(row_lengths, positions):
    doc_ends = jnp.cumsum(row_lengths, axis=-1)
    starts = jnp.any(positions[..., None] == doc_ends[..., None, :-1], axis=-1) | (positions == 0)
    live_mask = positions < doc_ends[..., -1:]
    return (starts, live_mask)

def forward(row_tokens, param_set, starts, live_mask):
    scale, offset, value_mat, value_add, reduce_mat, reduce_add, rate_vec, skip_vec, state_mat, expand_mat, expand_add, out_mat, out_add = [low(entry) for entry in param_set]
    normed = low(layer_norm(row_tokens, scale, offset))
    value_pre = low_back(matmul_high(normed, value_mat) + value_add)
    reduce_pre = low_back(matmul_high(normed, reduce_mat) + reduce_add)
    values_act = jax.nn.gelu(value_pre)
    reduced = jax.nn.gelu(reduce_pre)
    decays, inflow = decay_terms(rate_vec)
    retain = decays * (1.0 - starts.astype(jnp.float32))[:, None]
    states = lax.associative_scan(compose, (retain, inflow * reduced), axis=0)[1]
    ssm_out = low_back(matmul_high(low(states), state_mat) + skip_vec * reduced)
    expand_pre = low_back(matmul_high(low(ssm_out), expand_mat) + expand_add)
    gated_prod = low(values_act * expand_pre)
    branch = matmul_high(gated_prod, out_mat) + out_add
    return row_tokens + live_mask.astype(jnp.float32)[:, None] * branch

def reference(tokens, lengths, cotangent, norm_gain, norm_shift, value_weight, value_bias, reduce_weight, reduce_bias, decay_rates, skip_gain, state_weight, expand_weight, expand_bias, out_weight, out_bias):
    params = (norm_gain, norm_shift, value_weight, value_bias, reduce_weight, reduce_bias, decay_rates, skip_gain, state_weight, expand_weight, expand_bias, out_weight, out_bias)
    positions = jnp.arange(LEN, dtype=jnp.int32)

    def one_row(totals, inputs):
        row_tokens, row_lengths, row_cot = inputs
        starts, live_mask = row_flags(row_lengths, positions)

        def inner(row_vals, param_set):
            return forward(row_vals, param_set, starts, live_mask)
        result, pullback = jax.vjp(inner, row_tokens.astype(jnp.float32), params)
        grad_row, grad_params = pullback(row_cot.astype(jnp.float32))
        totals = jax.tree.map(lambda first, second: first + second, totals, grad_params)
        return (totals, (result.astype(jnp.bfloat16), grad_row.astype(jnp.bfloat16)))
    initial = tuple((jnp.zeros_like(entry) for entry in params))
    totals, (output, grad_tokens) = lax.scan(one_row, initial, (tokens, lengths, cotangent))
    return (output, grad_tokens, totals[0], totals[1], totals[2], totals[3], totals[4], totals[5], totals[6], totals[7], totals[8], totals[9], totals[10], totals[11], totals[12])
```

```python
import jax
import jax.numpy as jnp
from jax import lax
from jax.experimental import pallas as pl
from jax.experimental.pallas import tpu as pltpu
from jax.sharding import PartitionSpec as P

EPSILON = 1e-05
HALF = jnp.bfloat16
SINGLE = jnp.float32
MAIN = 5
SEGMENTS = 8
MIB = 1 << 20


def log2(n):
    return n.bit_length() - 1


def device_number():
    return lax.axis_index("dp") * lax.axis_size("seq") + lax.axis_index("seq")


def low_bits():
    return log2(lax.axis_size("dp") * lax.axis_size("seq")) - MAIN


def exchange(values, bit):
    inner = log2(lax.axis_size("seq"))
    axis, place = ("seq", bit) if bit < inner else ("dp", bit - inner)
    count = lax.axis_size(axis)
    return lax.ppermute(values, axis, [(i, i ^ (1 << place)) for i in range(count)])


def gather_low(values):
    for bit in range(low_bits()):
        other = exchange(values, bit)
        upper = (device_number() >> bit) & 1
        values = jnp.where(
            upper == 1, jnp.concatenate([other, values]), jnp.concatenate([values, other])
        )
    return values


def reduce_low(values):
    for bit in reversed(range(low_bits())):
        upper = (device_number() >> bit) & 1
        halves = values.reshape((2, values.shape[0] // 2) + values.shape[1:])
        mine = lax.dynamic_index_in_dim(halves, upper, 0, False)
        theirs = lax.dynamic_index_in_dim(halves, 1 - upper, 0, False)
        values = mine + exchange(theirs, bit)
    return values


def join(own, other):
    return jnp.concatenate([own, other])


def gather_chunk(rows, split):
    base = low_bits()
    core, bit_x, bit_y, bit_z, bit_far = (base + i for i in range(MAIN))
    held = rows[None]
    held = join(held, exchange(held, bit_far))
    held = join(held, exchange(held, bit_z))
    first, second = held[:, :split], held[:, split:]
    parts = []
    if split:
        from_y = exchange(first, bit_y)
        from_x = exchange(second, bit_x)
        first, second = join(first, from_y), join(second, from_x)
        from_x = exchange(first, bit_x)
        from_y = exchange(second, bit_y)
        first, second = join(first, from_x), join(second, from_y)
        parts = [first, exchange(first, core), second, exchange(second, core)]
    else:
        second = join(second, exchange(second, bit_y))
        second = join(second, exchange(second, bit_x))
        parts = [second, exchange(second, core)]
    return parts


def spot(rel, x_first):
    core = rel & 1
    bit_x, bit_y = (rel >> 1) & 1, (rel >> 2) & 1
    bit_z, bit_far = (rel >> 3) & 1, (rel >> 4) & 1
    if x_first:
        return core, bit_x * 8 + bit_y * 4 + bit_z * 2 + bit_far
    return core, bit_y * 8 + bit_x * 4 + bit_z * 2 + bit_far


def place_weights(parts, pieces, shapes, me):
    width = parts[0].shape[-1]
    pairs = len(parts) // 2

    def body(me_ref, *refs):
        ins, outs, sems = refs[: 2 * pairs], refs[2 * pairs : -1], refs[-1]
        mine = me_ref[0]

        def one(shard, carry):
            rel = shard ^ mine
            for which, row, rows, out, held, to_row, to_col in pieces:
                core, k = spot(rel, which == 0)
                target = outs[out].at[
                    pl.ds(pl.multiple_of(shard * held + to_row, 8), rows), pl.ds(to_col, width)
                ]

                @pl.when(core == 0)
                def _():
                    pltpu.make_async_copy(
                        ins[2 * which].at[k, pl.ds(row, rows)], target, sems.at[out]
                    ).start()

                @pl.when(core == 1)
                def _():
                    pltpu.make_async_copy(
                        ins[2 * which + 1].at[k, pl.ds(row, rows)], target, sems.at[out]
                    ).start()

            return carry

        lax.fori_loop(0, 1 << MAIN, one, 0)
        for i, out in enumerate(outs):
            pltpu.make_async_copy(out, out, sems.at[i]).wait()

    return pl.pallas_call(
        body,
        out_shape=[jax.ShapeDtypeStruct(s, HALF) for s in shapes],
        in_specs=[pl.BlockSpec(memory_space=pltpu.SMEM)]
        + [pl.BlockSpec(memory_space=pl.ANY)] * len(parts),
        out_specs=[pl.BlockSpec(memory_space=pl.ANY)] * len(shapes),
        scratch_shapes=[pltpu.SemaphoreType.DMA((len(shapes),))],
    )(me, *parts)


def weight_grad(left, right, shard_rows, column_block, row_block, me, name):
    tokens, height = left.shape
    width = right.shape[1]
    column_blocks, row_blocks = width // column_block, height // row_block
    per_block = row_block // shard_rows
    half = 1 << (MAIN - 1)

    def body(me_ref, left_ref, right_ref, send_ref, keep_ref):
        mine = me_ref[0]
        product = lax.dot_general(
            left_ref[...], right_ref[...], (((0,), (0,)), ((), ())), preferred_element_type=SINGLE
        ).astype(HALF)
        for s in range(per_block):
            shard = pl.program_id(1) * per_block + s
            core, k = spot(shard ^ mine, True)
            part = product[s * shard_rows : (s + 1) * shard_rows]

            @pl.when(core == 1)
            def _():
                send_ref[k] = part

            @pl.when(core == 0)
            def _():
                keep_ref[k] = part

    shape = jax.ShapeDtypeStruct((half, column_blocks * shard_rows, column_block), HALF)
    spec = pl.BlockSpec((half, shard_rows, column_block), lambda j, i: (0, j, 0))
    return pl.pallas_call(
        body,
        name=name,
        out_shape=[shape, shape],
        grid=(column_blocks, row_blocks),
        in_specs=[
            pl.BlockSpec(memory_space=pltpu.SMEM),
            pl.BlockSpec((tokens, row_block), lambda j, i: (0, i)),
            pl.BlockSpec((tokens, column_block), lambda j, i: (0, j)),
        ],
        out_specs=[spec, spec],
        compiler_params=pltpu.CompilerParams(vmem_limit_bytes=48 * MIB),
        cost_estimate=pl.CostEstimate(
            flops=2 * tokens * height * width,
            bytes_accessed=2 * tokens * (height + width) + 2 * height * width,
            transcendentals=0,
        ),
    )(me, left, right)


def add_low(first, second):
    return (first.astype(SINGLE) + second.astype(SINGLE)).astype(HALF)


def reduce_chunk(send, keep, split):
    base = low_bits()
    core, bit_x, bit_y, bit_z, bit_far = (base + i for i in range(MAIN))
    rows, width = send.shape[1:]
    total = add_low(keep, exchange(send, core)).reshape(2, 2, 4, rows, width)
    second = total[:, :, :, split:]
    if split:
        first = total[:, :, :, :split]
        from_x = exchange(first[1], bit_x)
        from_y = exchange(second[:, 1], bit_y)
        first, second = add_low(first[0], from_x), add_low(second[:, 0], from_y)
        from_y = exchange(first[1], bit_y)
        from_x = exchange(second[1], bit_x)
        first, second = add_low(first[0], from_y), add_low(second[0], from_x)
        total = jnp.concatenate([first, second], axis=1)
    else:
        second = add_low(second[0], exchange(second[1], bit_x))
        total = add_low(second[0], exchange(second[1], bit_y))
    total = add_low(total[:2], exchange(total[2:], bit_z))
    return total[0].astype(SINGLE) + exchange(total[1], bit_far).astype(SINGLE)


def keep_mask(ends_ref, first, shape, span):
    place = first + lax.broadcasted_iota(jnp.int32, shape, 0) * span
    start = place == 0
    for i in range(7):
        start = start | (place == ends_ref[i])
    return jnp.where(start, 0.0, 1.0)


def scan_states(ends, base, inputs, decays, reverse, name):
    block, channels = inputs.shape
    span = block // SEGMENTS
    lanes = 128

    def body(ends_ref, base_ref, in_ref, decay_ref, state_ref, product_ref):
        decay = jnp.broadcast_to(decay_ref[...], (SEGMENTS, lanes))
        first = base_ref[0]

        def at(k):
            return pl.ds(k, SEGMENTS, stride=span)

        def one(lap, carry):
            k = span - 1 - lap if reverse else lap
            state, product = carry
            a = decay * keep_mask(ends_ref, first + (k + 1 if reverse else k), (SEGMENTS, lanes), span)
            state, product = a * state + in_ref[at(k), :], product * a
            state_ref[at(k), :] = state
            product_ref[at(k), :] = product
            return (state, product)

        zero = jnp.zeros((SEGMENTS, lanes), SINGLE)
        state, product = lax.fori_loop(0, span, one, (zero, zero + 1.0), unroll=8)
        carry, through = zero[:1], zero[:1] + 1.0
        carries, throughs = [None] * SEGMENTS, [None] * SEGMENTS
        order = range(SEGMENTS)[::-1] if reverse else range(SEGMENTS)
        for s in order:
            carries[s], throughs[s] = carry, through
            carry = product[s : s + 1] * carry + state[s : s + 1]
            through = product[s : s + 1] * through
        carry_in = jnp.concatenate(carries, axis=0)
        through_in = jnp.concatenate(throughs, axis=0)

        def two(k, carry):
            product = product_ref[at(k), :]
            state_ref[at(k), :] = state_ref[at(k), :] + product * carry_in
            product_ref[at(k), :] = product * through_in
            return carry

        lax.fori_loop(0, span, two, 0, unroll=8)

    shape = jax.ShapeDtypeStruct((block, channels), SINGLE)
    spec = pl.BlockSpec((block, lanes), lambda i: (0, i))
    return pl.pallas_call(
        body,
        name=name,
        out_shape=[shape, shape],
        grid=(channels // lanes,),
        in_specs=[
            pl.BlockSpec(memory_space=pltpu.SMEM),
            pl.BlockSpec(memory_space=pltpu.SMEM),
            spec,
            pl.BlockSpec((1, lanes), lambda i: (0, i)),
        ],
        out_specs=[spec, spec],
        compiler_params=pltpu.CompilerParams(vmem_limit_bytes=24 * MIB),
    )(ends, base, inputs, decays)


def carried_in(through, ending, reverse):
    count, place = lax.axis_size("seq"), lax.axis_index("seq")
    gathered = lax.all_gather(jnp.stack([through, ending]), "seq")
    state = jnp.zeros_like(ending)
    for lap in range(count):
        source = count - 1 - lap if reverse else lap
        before = source > place if reverse else source < place
        state = jnp.where(before, gathered[source, 0] * state + gathered[source, 1], state)
    return state


def layer_norm(token_rows, scale, offset):
    center = token_rows - jnp.mean(token_rows, axis=-1, keepdims=True)
    inverse = lax.rsqrt(jnp.mean(center * center, axis=-1, keepdims=True) + EPSILON)
    return center * inverse * scale + offset


def decay_terms(rates):
    return (jnp.exp(-rates), jnp.sqrt(-jnp.expm1(-2.0 * rates)))


def column_sum(values):
    return jnp.sum(values.astype(SINGLE), axis=0)


def column_blocks(shard, width):
    return jnp.concatenate(
        [shard[:, i : i + width] for i in range(0, shard.shape[1], width)], axis=0
    )


def from_column_blocks(rows, count):
    height = rows.shape[0] // count
    return jnp.concatenate([rows[i * height : (i + 1) * height] for i in range(count)], axis=1)


def on_device(
    tokens,
    lengths,
    cotangent,
    norm_gain,
    norm_shift,
    value_weight,
    value_bias,
    reduce_weight,
    reduce_bias,
    decay_rates,
    skip_gain,
    state_weight,
    expand_weight,
    expand_bias,
    out_weight,
    out_bias,
):
    half, single = HALF, SINGLE
    shards = 1 << MAIN
    me = (device_number() >> low_bits()).reshape(1).astype(jnp.int32)
    low = lambda a: gather_low(a.astype(half))
    vectors = [
        low(v)
        for v in (
            norm_gain,
            norm_shift,
            value_bias,
            reduce_bias,
            decay_rates,
            skip_gain,
            expand_bias,
            out_bias,
        )
    ]
    sizes = [v.shape[0] for v in vectors]
    used = sum(sizes)
    reduce_shard, state_shard = low(reduce_weight), low(state_weight)
    value_shard, expand_shard, out_shard = low(value_weight), low(expand_weight), low(out_weight)
    channels = state_shard.shape[1]
    width = tokens.shape[-1]
    gate = value_shard.shape[1]
    blocks = gate // width

    vector_rows = jnp.pad(jnp.concatenate(vectors)[None], ((0, 7), (0, channels - used)))
    small = jnp.concatenate([reduce_shard, state_shard, vector_rows], axis=0)
    small_parts = gather_chunk(small, 0)
    value_parts = gather_chunk(column_blocks(value_shard, width), 48)
    expand_parts = gather_chunk(column_blocks(expand_shard, width), 24)
    out_parts = gather_chunk(out_shard, 48)

    reduce_mat, state_mat, vector_mat = place_weights(
        small_parts,
        [(0, 0, 32, 0, 32, 0, 0), (0, 32, 16, 1, 16, 0, 0), (0, 48, 8, 2, 8, 0, 0)],
        [(width, channels), (channels, channels), (8 * shards, channels)],
        me,
    )
    (value_mat,) = place_weights(
        value_parts,
        [
            (0, 0, 32, 0, 32, 0, 0),
            (0, 32, 16, 0, 32, 0, width),
            (1, 0, 16, 0, 32, 16, width),
            (1, 16, 32, 0, 32, 0, 2 * width),
        ],
        [(width, gate)],
        me,
    )
    (expand_mat,) = place_weights(
        expand_parts,
        [
            (0, 0, 16, 0, 16, 0, 0),
            (0, 16, 8, 0, 16, 0, width),
            (1, 0, 8, 0, 16, 8, width),
            (1, 8, 16, 0, 16, 0, 2 * width),
        ],
        [(channels, gate)],
        me,
    )
    (out_mat,) = place_weights(
        out_parts,
        [(0, 0, 48, 0, 96, 0, 0), (1, 0, 48, 0, 96, 48, 0)],
        [(gate, width)],
        me,
    )
    vector_table = vector_mat.reshape(shards, 8, channels)[:, 0].astype(single)
    places = [sum(sizes[:i]) for i in range(len(sizes))]
    (
        norm_scale,
        norm_offset,
        value_add,
        reduce_add,
        rate_vec,
        skip_vec,
        expand_add,
        out_add,
    ) = [vector_table[:, p : p + n].reshape(-1) for p, n in zip(places, sizes)]

    row_count, block, _ = tokens.shape
    base = (lax.axis_index("seq") * block).reshape(1).astype(jnp.int32)
    positions = base + jnp.arange(block, dtype=jnp.int32)
    doc_ends = jnp.cumsum(lengths, axis=-1).reshape(-1)
    starts = jnp.any(positions[:, None] == doc_ends[None, :-1], axis=-1) | (positions == 0)
    keep_flags = (1.0 - starts.astype(single))[:, None]
    live_rows = (positions < doc_ends[-1]).astype(single)[:, None]
    token_rows = tokens.reshape(block, width).astype(single)

    normed, norm_pull = jax.vjp(layer_norm, token_rows, norm_scale, norm_offset)
    normed_low = normed.astype(half)
    reduce_pre = jnp.dot(normed_low, reduce_mat, preferred_element_type=single) + reduce_add
    reduced_act, reduce_pull = jax.vjp(jax.nn.gelu, reduce_pre)
    (decays, inflow), decay_pull = jax.vjp(decay_terms, rate_vec)
    local_states, cumul = scan_states(
        doc_ends, base, inflow * reduced_act, decays[None], False, "forward_scan"
    )
    carried = carried_in(cumul[-1], local_states[-1], False)
    value_pre = jnp.dot(normed_low, value_mat, preferred_element_type=single) + value_add
    values_act, value_pull = jax.vjp(jax.nn.gelu, value_pre)
    states = local_states + cumul * carried[None]
    states_low = states.astype(half)
    ssm_out = jnp.dot(states_low, state_mat, preferred_element_type=single) + skip_vec * reduced_act
    ssm_low = ssm_out.astype(half)
    expand_pre = jnp.dot(ssm_low, expand_mat, preferred_element_type=single) + expand_add
    gated_low = (values_act * expand_pre).astype(half)

    cot_rows = cotangent.reshape(-1, width).astype(single)
    branch_grad = (live_rows * cot_rows).astype(half)
    out_grads = weight_grad(gated_low, branch_grad, 96, width, 768, me, "grad_out")
    out_sum = reduce_chunk(*out_grads, 48)

    branch = jnp.dot(gated_low, out_mat, preferred_element_type=single) + out_add
    output = (token_rows + live_rows * branch).astype(half).reshape(tokens.shape)
    grad_out_add = column_sum(branch_grad)
    gated_grad = jnp.einsum("td,gd->tg", branch_grad, out_mat, preferred_element_type=single)
    expand_grad = (gated_grad * values_act).astype(half)
    value_grad = gated_grad * expand_pre
    value_low = value_pull(value_grad)[0].astype(half)
    expand_grads = weight_grad(ssm_low, expand_grad, 16, width, 512, me, "grad_expand")
    expand_sum = reduce_chunk(*expand_grads, 24)
    value_grads = weight_grad(normed_low, value_low, 32, width, 512, me, "grad_value")
    value_sum = reduce_chunk(*value_grads, 48)
    grad_expand_add = column_sum(expand_grad)
    grad_value_add = column_sum(value_low)
    ssm_grad = jnp.einsum(
        "tg,rg->tr", expand_grad, expand_mat, preferred_element_type=single
    ).astype(half)
    grad_skip = jnp.sum(ssm_grad.astype(single) * reduced_act, axis=0)
    state_send, state_keep = weight_grad(states_low, ssm_grad, 16, channels, 512, me, "grad_state")
    state_grad = jnp.einsum("ts,rs->tr", ssm_grad, state_mat, preferred_element_type=single)
    local_total, suffix = scan_states(doc_ends, base, state_grad, decays[None], True, "reverse_scan")
    flow_in = carried_in(suffix[0], local_total[0], True)
    total_grad = local_total + suffix * flow_in[None]
    prev_states = jnp.concatenate([carried[None], states[:-1]], axis=0)
    grad_decays = jnp.sum(total_grad * keep_flags * prev_states, axis=0)
    grad_inflow = jnp.sum(total_grad * reduced_act, axis=0)
    grad_rates = decay_pull((grad_decays, grad_inflow))[0]
    reduced_grad = ssm_grad.astype(single) * skip_vec + inflow * total_grad
    reduce_low_grad = reduce_pull(reduced_grad)[0].astype(half)
    grad_reduce_add = column_sum(reduce_low_grad)
    reduce_send, reduce_keep = weight_grad(
        normed_low, reduce_low_grad, 32, channels, 512, me, "grad_reduce"
    )
    normed_grad = jnp.einsum(
        "tg,dg->td", value_low, value_mat, preferred_element_type=single
    ) + jnp.einsum("tr,dr->td", reduce_low_grad, reduce_mat, preferred_element_type=single)
    token_grad, grad_scale, grad_offset = norm_pull(normed_grad)
    grad_tokens = (cot_rows + token_grad).astype(half).reshape(tokens.shape)

    sums = (
        grad_scale,
        grad_offset,
        grad_value_add,
        grad_reduce_add,
        grad_rates,
        grad_skip,
        grad_expand_add,
        grad_out_add,
    )
    table = jnp.concatenate([v.reshape(shards, -1) for v in sums], axis=1).astype(half)
    table = jnp.pad(table[:, None], ((0, 0), (0, 7), (0, channels - used)))
    k = jnp.arange(shards // 2, dtype=jnp.int32)
    rel = ((k >> 3) & 1) * 2 + ((k >> 2) & 1) * 4 + ((k >> 1) & 1) * 8 + (k & 1) * 16
    small_sum = reduce_chunk(
        jnp.concatenate([reduce_send, state_send, table[(rel + 1) ^ me]], axis=1),
        jnp.concatenate([reduce_keep, state_keep, table[rel ^ me]], axis=1),
        0,
    )
    vector_sum = small_sum[48]
    vector_sums = [reduce_low(vector_sum[p : p + n]) for p, n in zip(places, sizes)]
    return (
        output,
        grad_tokens,
        vector_sums[0],
        vector_sums[1],
        reduce_low(from_column_blocks(value_sum, blocks)),
        vector_sums[2],
        reduce_low(small_sum[:32]),
        vector_sums[3],
        vector_sums[4],
        vector_sums[5],
        reduce_low(small_sum[32:48]),
        reduce_low(from_column_blocks(expand_sum, blocks)),
        vector_sums[6],
        reduce_low(out_sum),
        vector_sums[7],
    )


def solution(mesh):
    rows, vector, matrix = P("dp", "seq", None), P(("dp", "seq")), P(("dp", "seq"), None)
    return jax.shard_map(
        on_device,
        mesh=mesh,
        in_specs=(
            rows,
            P("dp", None),
            rows,
            vector,
            vector,
            matrix,
            vector,
            matrix,
            vector,
            vector,
            vector,
            matrix,
            matrix,
            vector,
            matrix,
            vector,
        ),
        out_specs=(
            rows,
            rows,
            vector,
            vector,
            matrix,
            vector,
            matrix,
            vector,
            vector,
            vector,
            matrix,
            matrix,
            vector,
            matrix,
            vector,
        ),
        check_vma=False,
    )
```

```python
import jax
import jax.numpy as jnp
from jax import lax
from jax.experimental import pallas as pl
from jax.experimental.pallas import tpu as pltpu
from jax.sharding import PartitionSpec as P

EPSILON = 1e-05
HALF = jnp.bfloat16
SINGLE = jnp.float32
MAIN = 5
SEGMENTS = 8
MIB = 1 << 20


def log2(n):
    return n.bit_length() - 1


def device_number():
    return lax.axis_index("dp") * lax.axis_size("seq") + lax.axis_index("seq")


def low_bits():
    return log2(lax.axis_size("dp") * lax.axis_size("seq")) - MAIN


def exchange(values, bit):
    inner = log2(lax.axis_size("seq"))
    axis, place = ("seq", bit) if bit < inner else ("dp", bit - inner)
    count = lax.axis_size(axis)
    return lax.ppermute(values, axis, [(i, i ^ (1 << place)) for i in range(count)])


def gather_low(values):
    for bit in range(low_bits()):
        other = exchange(values, bit)
        upper = (device_number() >> bit) & 1
        values = jnp.where(
            upper == 1, jnp.concatenate([other, values]), jnp.concatenate([values, other])
        )
    return values


def reduce_low(values):
    for bit in reversed(range(low_bits())):
        upper = (device_number() >> bit) & 1
        halves = values.reshape((2, values.shape[0] // 2) + values.shape[1:])
        mine = lax.dynamic_index_in_dim(halves, upper, 0, False)
        theirs = lax.dynamic_index_in_dim(halves, 1 - upper, 0, False)
        values = mine + exchange(theirs, bit)
    return values


def join(own, other):
    return jnp.concatenate([own, other])


def gather_chunk(rows, split):
    base = low_bits()
    core, bit_x, bit_y, bit_z, bit_far = (base + i for i in range(MAIN))
    held = rows[None]
    held = join(held, exchange(held, bit_far))
    held = join(held, exchange(held, bit_z))
    first, second = held[:, :split], held[:, split:]
    parts = []
    if split:
        from_y = exchange(first, bit_y)
        from_x = exchange(second, bit_x)
        first, second = join(first, from_y), join(second, from_x)
        from_x = exchange(first, bit_x)
        from_y = exchange(second, bit_y)
        first, second = join(first, from_x), join(second, from_y)
        parts = [first, exchange(first, core), second, exchange(second, core)]
    else:
        second = join(second, exchange(second, bit_y))
        second = join(second, exchange(second, bit_x))
        parts = [second, exchange(second, core)]
    return parts


def spot(rel, x_first):
    core = rel & 1
    bit_x, bit_y = (rel >> 1) & 1, (rel >> 2) & 1
    bit_z, bit_far = (rel >> 3) & 1, (rel >> 4) & 1
    if x_first:
        return core, bit_x * 8 + bit_y * 4 + bit_z * 2 + bit_far
    return core, bit_y * 8 + bit_x * 4 + bit_z * 2 + bit_far


def load_weights(mine, parts, target, pieces, sems):
    def one(shard, carry):
        rel = shard ^ mine
        for pair, row, rows, group, held, to_row in pieces:
            core, k = spot(rel, pair == 0)
            to = target.at[group, pl.ds(pl.multiple_of(shard * held + to_row, 16), rows)]
            for side in range(2):

                @pl.when(core == side)
                def _():
                    source = parts[2 * pair + side].at[k, pl.ds(row, rows)]
                    pltpu.make_async_copy(source, to, sems.at[group]).start()

        return carry

    lax.fori_loop(0, 1 << MAIN, one, 0)


def await_weights(target, group, sems):
    pltpu.make_async_copy(target.at[group], target.at[group], sems.at[group]).wait()


REDUCE_PIECES = [(0, 0, 32, 0, 32, 0)]
STATE_PIECES = [(0, 32, 16, 0, 16, 0)]
VALUE_PIECES = [
    (0, 0, 32, 0, 32, 0),
    (0, 32, 16, 1, 32, 0),
    (1, 0, 16, 1, 32, 16),
    (1, 16, 32, 2, 32, 0),
]
EXPAND_PIECES = [(0, 0, 16, 0, 16, 0), (0, 16, 16, 1, 16, 0), (1, 0, 16, 2, 16, 0)]
OUT_PIECES = [(0, 0, 48, 0, 96, 0), (1, 0, 48, 0, 96, 48)]

SMEM = pl.BlockSpec(memory_space=pltpu.SMEM)
ANY = pl.BlockSpec(memory_space=pl.ANY)


def whole(*shape):
    return pl.BlockSpec(shape, lambda *_: (0,) * len(shape))


def dot(left, right, left_dim=1, right_dim=0):
    return lax.dot_general(
        left, right, (((left_dim,), (right_dim,)), ((), ())), preferred_element_type=SINGLE
    )


def gelu_pair(v):
    c, d = 0.7978845608028654, 0.7978845608028654 * 0.044715
    square = v * v
    h = 0.5 + 0.5 * jnp.tanh(v * (c + d * square))
    act = v * h
    return act, h + 2.0 * act * (1.0 - h) * (c + 3.0 * d * square)


def norm_terms(x):
    center = x - jnp.mean(x, axis=-1, keepdims=True)
    inverse = lax.rsqrt(jnp.mean(center * center, axis=-1, keepdims=True) + EPSILON)
    return center * inverse, inverse


def lanes_joined(ref, rows):
    return jnp.concatenate([ref[c, rows, :] for c in range(ref.shape[0])], axis=1)


def scan_block(ends_ref, first, decay, value_ref, product_ref, reverse):
    columns, block, lanes = value_ref.shape
    span = block // SEGMENTS
    decays = [
        jnp.broadcast_to(decay[:, c * lanes : (c + 1) * lanes], (SEGMENTS, lanes))
        for c in range(columns)
    ]

    def one(lap, carry):
        k = span - 1 - lap if reverse else lap
        mask = keep_mask(ends_ref, first + (k + 1 if reverse else k), (SEGMENTS, lanes), span)
        at = pl.ds(k, SEGMENTS, stride=span)
        states, products = [], []
        for c in range(columns):
            a = decays[c] * mask
            states.append(a * carry[0][c] + value_ref[c, at, :])
            products.append(a * carry[1][c])
        for c in range(columns):
            value_ref[c, at, :] = states[c]
            product_ref[c, at, :] = products[c]
        return (states, products)

    zero = [jnp.zeros((SEGMENTS, lanes), SINGLE)] * columns
    ones = [jnp.ones((SEGMENTS, lanes), SINGLE)] * columns
    states, products = lax.fori_loop(0, span, one, (zero, ones), unroll=4)
    return jnp.concatenate(products, axis=1), jnp.concatenate(states, axis=1)


def span_carries(product, state, carry, reverse):
    carries = [None] * SEGMENTS
    for s in range(SEGMENTS)[::-1] if reverse else range(SEGMENTS):
        carries[s] = carry
        carry = product[s : s + 1] * carry + state[s : s + 1]
    return carries, carry


def block_carry(place, maps_ref, reverse):
    count = maps_ref.shape[0]
    carry = jnp.zeros((1, maps_ref.shape[2]), SINGLE)
    for s in range(count)[::-1] if reverse else range(count):
        rel = s ^ place
        inside = s > place if reverse else s < place
        moved = maps_ref[rel, 0:1, :] * carry + maps_ref[rel, 1:2, :]
        carry = jnp.where(inside, moved, carry)
    return carry


def whole_map(product, state, reverse):
    zero = jnp.zeros((1, product.shape[1]), SINGLE)
    _, ending = span_carries(product, state, zero, reverse)
    through = zero + 1.0
    for s in range(SEGMENTS):
        through = through * product[s : s + 1]
    return through, ending


def gather_maps(maps):
    held = maps[None]
    for bit in range(log2(lax.axis_size("seq"))):
        held = join(held, exchange(held, bit))
    return held


def reduce_kernel(scalars, tokens, gain, shift, bias, decay, inflow, parts):
    block, width = tokens.shape
    channels = bias.shape[1]
    tile = 256
    columns = channels // 128

    def body(me, ends, base, x_ref, gain_ref, shift_ref, bias_ref, decay_ref, inflow_ref, p0, p1,
             normed_ref, act_ref, slope_ref, state_ref, product_ref, span_ref, map_ref,
             weight, sems):
        load_weights(me[0], (p0, p1), weight, REDUCE_PIECES, sems)
        for t in range(block // tile):
            rows = pl.ds(t * tile, tile)
            n, _ = norm_terms(x_ref[rows, :].astype(SINGLE))
            normed_ref[rows, :] = (n * gain_ref[...] + shift_ref[...]).astype(HALF)
        await_weights(weight, 0, sems)
        for t in range(block // tile):
            rows = pl.ds(t * tile, tile)
            act, slope = gelu_pair(dot(normed_ref[rows, :], weight[0]) + bias_ref[...])
            act_ref[rows, :] = act
            slope_ref[rows, :] = slope.astype(HALF)
            flow = act * inflow_ref[...]
            for c in range(columns):
                state_ref[c, rows, :] = flow[:, c * 128 : (c + 1) * 128]
        product, state = scan_block(ends, base[0], decay_ref[...], state_ref, product_ref, False)
        span_ref[0], span_ref[1] = product, state
        map_ref[0:1, :], map_ref[1:2, :] = whole_map(product, state, False)

    vm = pl.BlockSpec(memory_space=pltpu.VMEM)
    return pl.pallas_call(
        body,
        name="reduce_forward",
        out_shape=[
            jax.ShapeDtypeStruct((block, width), HALF),
            jax.ShapeDtypeStruct((block, channels), SINGLE),
            jax.ShapeDtypeStruct((block, channels), HALF),
            jax.ShapeDtypeStruct((columns, block, 128), SINGLE),
            jax.ShapeDtypeStruct((columns, block, 128), SINGLE),
            jax.ShapeDtypeStruct((2, SEGMENTS, channels), SINGLE),
            jax.ShapeDtypeStruct((2, channels), SINGLE),
        ],
        in_specs=[SMEM] * 3 + [vm] * 6 + [ANY] * 2,
        out_specs=[vm] * 7,
        scratch_shapes=[
            pltpu.VMEM((1, width, channels), HALF),
            pltpu.SemaphoreType.DMA((1,)),
        ],
        compiler_params=pltpu.CompilerParams(vmem_limit_bytes=40 * MIB),
        cost_estimate=pl.CostEstimate(
            flops=2 * block * width * channels,
            bytes_accessed=16 * MIB,
            transcendentals=block * channels,
        ),
    )(*scalars[:3], tokens, gain, shift, bias, decay, inflow, *parts)


def value_kernel(me, normed, bias, parts):
    block, width = normed.shape
    gate = bias.shape[1]
    tile, sub = 256, 256
    groups = gate // width

    def body(me, x_ref, bias_ref, p0, p1, p2, p3, act_ref, slope_ref, weight, sems):
        j, t = pl.program_id(0), pl.program_id(1)

        @pl.when((j == 0) & (t == 0))
        def _():
            load_weights(me[0], (p0, p1, p2, p3), weight, VALUE_PIECES, sems)

        for g in range(groups):

            @pl.when((j == g) & (t == 0))
            def _():
                await_weights(weight, g, sems)

        for c in range(width // sub):
            cols = pl.ds(c * sub, sub)
            pre = dot(x_ref[...], weight[j, :, cols]) + bias_ref[:, cols]
            act, slope = gelu_pair(pre)
            act_ref[:, cols] = act.astype(HALF)
            slope_ref[:, cols] = slope.astype(HALF)

    shape = jax.ShapeDtypeStruct((block, gate), HALF)
    spec = pl.BlockSpec((tile, width), lambda j, t: (t, j))
    return pl.pallas_call(
        body,
        name="value_forward",
        out_shape=[shape, shape],
        grid=(groups, block // tile),
        in_specs=[
            SMEM,
            pl.BlockSpec((tile, width), lambda j, t: (t, 0)),
            pl.BlockSpec((1, width), lambda j, t: (0, j)),
        ]
        + [ANY] * 4,
        out_specs=[spec, spec],
        scratch_shapes=[
            pltpu.VMEM((groups, width, width), HALF),
            pltpu.SemaphoreType.DMA((groups,)),
        ],
        compiler_params=pltpu.CompilerParams(vmem_limit_bytes=40 * MIB),
        cost_estimate=pl.CostEstimate(
            flops=2 * block * width * gate,
            bytes_accessed=20 * MIB,
            transcendentals=block * gate,
        ),
    )(me, normed, bias, *parts)


def expand_kernel(me, place, maps, spans, states, products, act, skip, inflow, bias, va, vd,
                  small_parts, parts):
    columns, block, _ = states.shape
    channels = act.shape[1]
    gate = bias.shape[1]
    tile, sub = 256, 512
    groups, width = 3, gate // 3
    span = block // SEGMENTS

    def body(me, place_ref, maps_ref, span_ref, state_ref, product_ref, act_ref, skip_ref,
             inflow_ref, bias_ref, va_ref, vd_ref, s0, s1, p0, p1, p2, p3,
             gated_ref, slope_ref, low_ref, prior_ref, ssm_ref,
             carry_ref, small, weight, small_sems, sems):
        t = pl.program_id(0)

        @pl.when(t == 0)
        def _():
            load_weights(me[0], (s0, s1), small, STATE_PIECES, small_sems)
            load_weights(me[0], (p0, p1, p2, p3), weight, EXPAND_PIECES, sems)
            entering = block_carry(place_ref[0], maps_ref, False)
            carries, _ = span_carries(span_ref[0], span_ref[1], entering, False)
            for s in range(SEGMENTS):
                carry_ref[s] = jnp.broadcast_to(carries[s], (8, channels))
            await_weights(small, 0, small_sems)
            for g in range(groups):
                await_weights(weight, g, sems)

        pieces = []
        for s in range(tile // span):
            rows = pl.ds(s * span, span)
            carry = carry_ref[t * (tile // span) + s][:1]
            pieces.append(
                lanes_joined(state_ref, rows) + lanes_joined(product_ref, rows) * carry
            )
        state = jnp.concatenate(pieces, axis=0)
        low = state.astype(HALF)
        low_ref[...] = low
        prior_ref[...] = (state - inflow_ref[...] * act_ref[...]).astype(HALF)
        ssm = (dot(low, small[0]) + skip_ref[...] * act_ref[...]).astype(HALF)
        ssm_ref[...] = ssm
        for g in range(groups):
            for c in range(width // sub):
                cols = pl.ds(g * width + c * sub, sub)
                pre = dot(ssm, weight[g, :, c * sub : (c + 1) * sub]) + bias_ref[:, cols]
                gated_ref[:, cols] = (va_ref[:, cols].astype(SINGLE) * pre).astype(HALF)
                slope_ref[:, cols] = (vd_ref[:, cols].astype(SINGLE) * pre).astype(HALF)

    tall = pl.BlockSpec((columns, tile, 128), lambda t: (0, t, 0))
    narrow = pl.BlockSpec((tile, channels), lambda t: (t, 0))
    wide = pl.BlockSpec((tile, gate), lambda t: (t, 0))
    return pl.pallas_call(
        body,
        name="expand_forward",
        out_shape=[jax.ShapeDtypeStruct((block, gate), HALF)] * 2
        + [jax.ShapeDtypeStruct((block, channels), HALF)] * 3,
        grid=(block // tile,),
        in_specs=[
            SMEM,
            SMEM,
            whole(*maps.shape),
            whole(*spans.shape),
            tall,
            tall,
            narrow,
            whole(1, channels),
            whole(1, channels),
            whole(1, gate),
            wide,
            wide,
        ]
        + [ANY] * 6,
        out_specs=[wide, wide, narrow, narrow, narrow],
        scratch_shapes=[
            pltpu.VMEM((SEGMENTS, 8, channels), SINGLE),
            pltpu.VMEM((1, channels, channels), HALF),
            pltpu.VMEM((groups, channels, width), HALF),
            pltpu.SemaphoreType.DMA((1,)),
            pltpu.SemaphoreType.DMA((groups,)),
        ],
        compiler_params=pltpu.CompilerParams(vmem_limit_bytes=48 * MIB),
        cost_estimate=pl.CostEstimate(
            flops=2 * block * channels * (gate + channels),
            bytes_accessed=36 * MIB,
            transcendentals=0,
        ),
    )(me, place, maps, spans, states, products, act, skip, inflow, bias, va, vd,
      *small_parts, *parts)


def out_kernel(me, live, base, gated, tokens, bias, parts):
    block, gate = gated.shape
    width = tokens.shape[1]
    tile = 256

    def body(me, live_ref, base_ref, gated_ref, x_ref, bias_ref, p0, p1, p2, p3,
             out_ref, weight, sems):
        t = pl.program_id(0)

        @pl.when(t == 0)
        def _():
            load_weights(me[0], (p0, p1, p2, p3), weight, OUT_PIECES, sems)
            await_weights(weight, 0, sems)

        place = base_ref[0] + t * tile + lax.broadcasted_iota(jnp.int32, (tile, 1), 0)
        branch = dot(gated_ref[...], weight[0]) + bias_ref[...]
        branch = jnp.where(place < live_ref[0], branch, 0.0)
        out_ref[...] = (x_ref[...].astype(SINGLE) + branch).astype(HALF)

    return pl.pallas_call(
        body,
        name="out_forward",
        out_shape=jax.ShapeDtypeStruct((block, width), HALF),
        grid=(block // tile,),
        in_specs=[
            SMEM,
            SMEM,
            SMEM,
            pl.BlockSpec((tile, gate), lambda t: (t, 0)),
            pl.BlockSpec((tile, width), lambda t: (t, 0)),
            whole(1, width),
        ]
        + [ANY] * 4,
        out_specs=pl.BlockSpec((tile, width), lambda t: (t, 0)),
        scratch_shapes=[
            pltpu.VMEM((1, gate, width), HALF),
            pltpu.SemaphoreType.DMA((1,)),
        ],
        compiler_params=pltpu.CompilerParams(vmem_limit_bytes=40 * MIB),
        cost_estimate=pl.CostEstimate(
            flops=2 * block * width * gate, bytes_accessed=16 * MIB, transcendentals=0
        ),
    )(me, live, base, gated, tokens, bias, *parts)


def fold(values):
    return jnp.sum(values.reshape(values.shape[0] // 8, 8, values.shape[1]), axis=0)


def gate_kernel(me, branch_grad, va, slope, parts):
    block, width = branch_grad.shape
    gate = va.shape[1]
    tile, sub = 256, 512

    def body(me, grad_ref, va_ref, slope_ref, p0, p1, p2, p3,
             expand_ref, value_ref, expand_sum, value_sum, weight, sems):
        t = pl.program_id(0)

        @pl.when(t == 0)
        def _():
            load_weights(me[0], (p0, p1, p2, p3), weight, OUT_PIECES, sems)
            expand_sum[...] = jnp.zeros_like(expand_sum)
            value_sum[...] = jnp.zeros_like(value_sum)
            await_weights(weight, 0, sems)

        grad = grad_ref[...]
        for c in range(gate // sub):
            cols = pl.ds(c * sub, sub)
            gated_grad = dot(grad, weight[0, c * sub : (c + 1) * sub, :], 1, 1)
            expand = gated_grad * va_ref[:, cols].astype(SINGLE)
            value = gated_grad * slope_ref[:, cols].astype(SINGLE)
            expand_ref[:, cols] = expand.astype(HALF)
            value_ref[:, cols] = value.astype(HALF)
            expand_sum[:, cols] += fold(expand)
            value_sum[:, cols] += fold(value)

    wide = pl.BlockSpec((tile, gate), lambda t: (t, 0))
    return pl.pallas_call(
        body,
        name="gate_backward",
        out_shape=[jax.ShapeDtypeStruct((block, gate), HALF)] * 2
        + [jax.ShapeDtypeStruct((8, gate), SINGLE)] * 2,
        grid=(block // tile,),
        in_specs=[SMEM, pl.BlockSpec((tile, width), lambda t: (t, 0)), wide, wide] + [ANY] * 4,
        out_specs=[wide, wide, whole(8, gate), whole(8, gate)],
        scratch_shapes=[
            pltpu.VMEM((1, gate, width), HALF),
            pltpu.SemaphoreType.DMA((1,)),
        ],
        compiler_params=pltpu.CompilerParams(vmem_limit_bytes=48 * MIB),
        cost_estimate=pl.CostEstimate(
            flops=2 * block * width * gate, bytes_accessed=32 * MIB, transcendentals=0
        ),
    )(me, branch_grad, va, slope, *parts)


def state_kernel(me, ends, base, expand_grad, act, decay, small_parts, parts):
    block, gate = expand_grad.shape
    channels = act.shape[1]
    tile = 256
    groups, width = 3, gate // 3
    columns = channels // 128

    def body(me, ends_ref, base_ref, grad_ref, act_ref, decay_ref, s0, s1, p0, p1, p2, p3,
             ssm_ref, total_ref, product_ref, span_ref, map_ref, skip_sum,
             small, weight, small_sems, sems):
        t = pl.program_id(0)

        @pl.when(t == 0)
        def _():
            load_weights(me[0], (s0, s1), small, STATE_PIECES, small_sems)
            load_weights(me[0], (p0, p1, p2, p3), weight, EXPAND_PIECES, sems)
            skip_sum[...] = jnp.zeros_like(skip_sum)
            await_weights(small, 0, small_sems)
            for g in range(groups):
                await_weights(weight, g, sems)

        ssm = dot(grad_ref[:, :width], weight[0], 1, 1)
        for g in range(1, groups):
            ssm += dot(grad_ref[:, g * width : (g + 1) * width], weight[g], 1, 1)
        low = ssm.astype(HALF)
        ssm_ref[...] = low
        skip_sum[...] += fold(ssm * act_ref[...])
        state = dot(low, small[0], 1, 1)
        rows = pl.ds(pl.multiple_of(t * tile, tile), tile)
        for c in range(columns):
            total_ref[c, rows, :] = state[:, c * 128 : (c + 1) * 128]

        @pl.when(t == block // tile - 1)
        def _():
            product, state = scan_block(
                ends_ref, base_ref[0], decay_ref[...], total_ref, product_ref, True
            )
            span_ref[0], span_ref[1] = product, state
            map_ref[0:1, :], map_ref[1:2, :] = whole_map(product, state, True)

    narrow = pl.BlockSpec((tile, channels), lambda t: (t, 0))
    return pl.pallas_call(
        body,
        name="state_backward",
        out_shape=[
            jax.ShapeDtypeStruct((block, channels), HALF),
            jax.ShapeDtypeStruct((columns, block, 128), SINGLE),
            jax.ShapeDtypeStruct((columns, block, 128), SINGLE),
            jax.ShapeDtypeStruct((2, SEGMENTS, channels), SINGLE),
            jax.ShapeDtypeStruct((2, channels), SINGLE),
            jax.ShapeDtypeStruct((8, channels), SINGLE),
        ],
        grid=(block // tile,),
        in_specs=[SMEM] * 3
        + [pl.BlockSpec((tile, gate), lambda t: (t, 0)), narrow, whole(1, channels)]
        + [ANY] * 6,
        out_specs=[
            narrow,
            whole(columns, block, 128),
            whole(columns, block, 128),
            whole(2, SEGMENTS, channels),
            whole(2, channels),
            whole(8, channels),
        ],
        scratch_shapes=[
            pltpu.VMEM((1, channels, channels), HALF),
            pltpu.VMEM((groups, channels, width), HALF),
            pltpu.SemaphoreType.DMA((1,)),
            pltpu.SemaphoreType.DMA((groups,)),
        ],
        compiler_params=pltpu.CompilerParams(vmem_limit_bytes=40 * MIB),
        cost_estimate=pl.CostEstimate(
            flops=2 * block * channels * (gate + channels),
            bytes_accessed=16 * MIB,
            transcendentals=0,
        ),
    )(me, ends, base, expand_grad, act, decay, *small_parts, *parts)


def input_kernel(me, place, maps, spans, totals, products, act, prior, ssm_grad, slope, skip,
                 inflow, gain, tokens, cotangent, value_grad, small_parts, parts):
    block, width = tokens.shape
    channels = act.shape[1]
    gate = value_grad.shape[1]
    tile = 256
    groups = gate // width
    columns = channels // 128
    span = block // SEGMENTS

    def body(me, place_ref, maps_ref, span_ref, total_ref, product_ref, act_ref, prior_ref,
             ssm_ref, slope_ref, skip_ref, inflow_ref, gain_ref, x_ref, cot_ref, value_ref,
             s0, s1, p0, p1, p2, p3,
             reduce_ref, out_ref, channel_sums, norm_sums,
             carry_ref, small, weight, small_sems, sems):
        t = pl.program_id(0)

        @pl.when(t == 0)
        def _():
            load_weights(me[0], (s0, s1), small, REDUCE_PIECES, small_sems)
            load_weights(me[0], (p0, p1, p2, p3), weight, VALUE_PIECES, sems)
            entering = block_carry(place_ref[0], maps_ref, True)
            carries, _ = span_carries(span_ref[0], span_ref[1], entering, True)
            for s in range(SEGMENTS):
                carry_ref[s] = jnp.broadcast_to(carries[s], (8, channels))
            channel_sums[...] = jnp.zeros_like(channel_sums)
            norm_sums[...] = jnp.zeros_like(norm_sums)

        pieces = []
        for s in range(tile // span):
            rows = pl.ds(s * span, span)
            carry = carry_ref[t * (tile // span) + s][:1]
            pieces.append(
                lanes_joined(total_ref, rows) + lanes_joined(product_ref, rows) * carry
            )
        total = jnp.concatenate(pieces, axis=0)
        channel_sums[0] += fold(total * prior_ref[...].astype(SINGLE))
        channel_sums[1] += fold(total * act_ref[...])
        reduced = ssm_ref[...].astype(SINGLE) * skip_ref[...] + inflow_ref[...] * total
        reduced = reduced * slope_ref[...].astype(SINGLE)
        channel_sums[2] += fold(reduced)
        low = reduced.astype(HALF)
        reduce_ref[...] = low

        @pl.when(t == 0)
        def _():
            await_weights(small, 0, small_sems)
            for g in range(groups):
                await_weights(weight, g, sems)

        grad = dot(low, small[0], 1, 1)
        for g in range(groups):
            grad += dot(value_ref[:, g * width : (g + 1) * width], weight[g], 1, 1)
        n, inverse = norm_terms(x_ref[...].astype(SINGLE))
        norm_sums[0] += fold(grad * n)
        norm_sums[1] += fold(grad)
        h = grad * gain_ref[...]
        mean_h = jnp.mean(h, axis=-1, keepdims=True)
        mean_hn = jnp.mean(h * n, axis=-1, keepdims=True)
        back = inverse * (h - mean_h - n * mean_hn)
        out_ref[...] = (cot_ref[...].astype(SINGLE) + back).astype(HALF)

    tall = pl.BlockSpec((columns, tile, 128), lambda t: (0, t, 0))
    narrow = pl.BlockSpec((tile, channels), lambda t: (t, 0))
    full = pl.BlockSpec((tile, width), lambda t: (t, 0))
    wide = pl.BlockSpec((tile, gate), lambda t: (t, 0))
    return pl.pallas_call(
        body,
        name="input_backward",
        out_shape=[
            jax.ShapeDtypeStruct((block, channels), HALF),
            jax.ShapeDtypeStruct((block, width), HALF),
            jax.ShapeDtypeStruct((3, 8, channels), SINGLE),
            jax.ShapeDtypeStruct((2, 8, width), SINGLE),
        ],
        grid=(block // tile,),
        in_specs=[
            SMEM,
            SMEM,
            whole(*maps.shape),
            whole(*spans.shape),
            tall,
            tall,
            narrow,
            narrow,
            narrow,
            narrow,
            whole(1, channels),
            whole(1, channels),
            whole(1, width),
            full,
            full,
            wide,
        ]
        + [ANY] * 6,
        out_specs=[narrow, full, whole(3, 8, channels), whole(2, 8, width)],
        scratch_shapes=[
            pltpu.VMEM((SEGMENTS, 8, channels), SINGLE),
            pltpu.VMEM((1, width, channels), HALF),
            pltpu.VMEM((groups, width, width), HALF),
            pltpu.SemaphoreType.DMA((1,)),
            pltpu.SemaphoreType.DMA((groups,)),
        ],
        compiler_params=pltpu.CompilerParams(vmem_limit_bytes=40 * MIB),
        cost_estimate=pl.CostEstimate(
            flops=2 * block * width * (gate + channels),
            bytes_accessed=30 * MIB,
            transcendentals=0,
        ),
    )(me, place, maps, spans, totals, products, act, prior, ssm_grad, slope, skip, inflow, gain,
      tokens, cotangent, value_grad, *small_parts, *parts)


def weight_grad(left, right, shard_rows, column_block, row_block, me, name):
    tokens, height = left.shape
    width = right.shape[1]
    column_blocks, row_blocks = width // column_block, height // row_block
    per_block = row_block // shard_rows
    half = 1 << (MAIN - 1)

    def body(me_ref, left_ref, right_ref, send_ref, keep_ref):
        mine = me_ref[0]
        product = lax.dot_general(
            left_ref[...], right_ref[...], (((0,), (0,)), ((), ())), preferred_element_type=SINGLE
        ).astype(HALF)
        for s in range(per_block):
            shard = pl.program_id(1) * per_block + s
            core, k = spot(shard ^ mine, True)
            part = product[s * shard_rows : (s + 1) * shard_rows]

            @pl.when(core == 1)
            def _():
                send_ref[k] = part

            @pl.when(core == 0)
            def _():
                keep_ref[k] = part

    shape = jax.ShapeDtypeStruct((half, column_blocks * shard_rows, column_block), HALF)
    spec = pl.BlockSpec((half, shard_rows, column_block), lambda j, i: (0, j, 0))
    return pl.pallas_call(
        body,
        name=name,
        out_shape=[shape, shape],
        grid=(column_blocks, row_blocks),
        in_specs=[
            pl.BlockSpec(memory_space=pltpu.SMEM),
            pl.BlockSpec((tokens, row_block), lambda j, i: (0, i)),
            pl.BlockSpec((tokens, column_block), lambda j, i: (0, j)),
        ],
        out_specs=[spec, spec],
        compiler_params=pltpu.CompilerParams(vmem_limit_bytes=48 * MIB),
        cost_estimate=pl.CostEstimate(
            flops=2 * tokens * height * width,
            bytes_accessed=2 * tokens * (height + width) + 2 * height * width,
            transcendentals=0,
        ),
    )(me, left, right)


def add_low(first, second):
    return (first.astype(SINGLE) + second.astype(SINGLE)).astype(HALF)


def reduce_chunk(send, keep, split):
    base = low_bits()
    core, bit_x, bit_y, bit_z, bit_far = (base + i for i in range(MAIN))
    rows, width = send.shape[1:]
    total = add_low(keep, exchange(send, core)).reshape(2, 2, 4, rows, width)
    second = total[:, :, :, split:]
    if split:
        first = total[:, :, :, :split]
        from_x = exchange(first[1], bit_x)
        from_y = exchange(second[:, 1], bit_y)
        first, second = add_low(first[0], from_x), add_low(second[:, 0], from_y)
        from_y = exchange(first[1], bit_y)
        from_x = exchange(second[1], bit_x)
        first, second = add_low(first[0], from_y), add_low(second[0], from_x)
        total = jnp.concatenate([first, second], axis=1)
    else:
        second = add_low(second[0], exchange(second[1], bit_x))
        total = add_low(second[0], exchange(second[1], bit_y))
    total = add_low(total[:2], exchange(total[2:], bit_z))
    return total[0].astype(SINGLE) + exchange(total[1], bit_far).astype(SINGLE)


def keep_mask(ends_ref, first, shape, span):
    place = first + lax.broadcasted_iota(jnp.int32, shape, 0) * span
    start = place == 0
    for i in range(7):
        start = start | (place == ends_ref[i])
    return jnp.where(start, 0.0, 1.0)


def decay_terms(rates):
    return (jnp.exp(-rates), jnp.sqrt(-jnp.expm1(-2.0 * rates)))


def column_sum(values):
    return jnp.sum(values.astype(SINGLE), axis=0)


def column_blocks(shard, width):
    return jnp.concatenate(
        [shard[:, i : i + width] for i in range(0, shard.shape[1], width)], axis=0
    )


def from_column_blocks(rows, count):
    height = rows.shape[0] // count
    return jnp.concatenate([rows[i * height : (i + 1) * height] for i in range(count)], axis=1)


def on_device(
    tokens,
    lengths,
    cotangent,
    norm_gain,
    norm_shift,
    value_weight,
    value_bias,
    reduce_weight,
    reduce_bias,
    decay_rates,
    skip_gain,
    state_weight,
    expand_weight,
    expand_bias,
    out_weight,
    out_bias,
):
    half, single = HALF, SINGLE
    shards = 1 << MAIN
    me = (device_number() >> low_bits()).reshape(1).astype(jnp.int32)
    low = lambda a: gather_low(a.astype(half))
    vectors = [
        low(v)
        for v in (
            norm_gain,
            norm_shift,
            value_bias,
            reduce_bias,
            decay_rates,
            skip_gain,
            expand_bias,
            out_bias,
        )
    ]
    sizes = [v.shape[0] for v in vectors]
    used = sum(sizes)
    reduce_shard, state_shard = low(reduce_weight), low(state_weight)
    value_shard, expand_shard, out_shard = low(value_weight), low(expand_weight), low(out_weight)
    channels = state_shard.shape[1]
    width = tokens.shape[-1]
    gate = value_shard.shape[1]
    blocks = gate // width

    vector_rows = jnp.pad(jnp.concatenate(vectors)[None], ((0, 7), (0, channels - used)))
    small = jnp.concatenate([reduce_shard, state_shard, vector_rows], axis=0)
    small_parts = gather_chunk(small, 0)
    value_parts = gather_chunk(column_blocks(value_shard, width), 48)
    expand_parts = gather_chunk(column_blocks(expand_shard, width), 32)
    out_parts = gather_chunk(out_shard, 48)

    row_count, block, _ = tokens.shape
    place = lax.axis_index("seq").reshape(1).astype(jnp.int32)
    base = place * block
    positions = base + jnp.arange(block, dtype=jnp.int32)
    ends = jnp.cumsum(lengths, axis=-1).reshape(-1)
    live = ends[-1:]
    token_rows, cot_rows = tokens.reshape(block, width), cotangent.reshape(block, width)
    branch_grad = jnp.where((positions < live)[:, None], cot_rows, jnp.zeros_like(cot_rows))
    grad_out_add = column_sum(branch_grad)

    k = jnp.arange(shards, dtype=jnp.int32) ^ me
    spots = (k & 1) * 16 + spot(k, True)[1]
    table = jnp.concatenate([p[:, 48] for p in small_parts])[spots].astype(single)
    places = [sum(sizes[:i]) for i in range(len(sizes))]
    gain, shift, value_add, reduce_add, rates, skip, expand_add, out_add = [
        table[:, p : p + n].reshape(1, -1) for p, n in zip(places, sizes)
    ]
    decays, inflow = decay_terms(rates)

    normed, act, reduce_slope, states, products, spans, own_map = reduce_kernel(
        (me, ends, base), token_rows, gain, shift, reduce_add, decays, inflow, small_parts
    )
    maps = gather_maps(own_map)
    value_act, value_slope = value_kernel(me, normed, value_add, value_parts)
    gated, gate_slope, states_low, prior, ssm_low = expand_kernel(
        me, place, maps, spans, states, products, act, skip, inflow, expand_add, value_act,
        value_slope, small_parts, expand_parts
    )
    out_grads = weight_grad(gated, branch_grad, 96, width, 768, me, "grad_out")
    out_sum = reduce_chunk(*out_grads, 48)

    expand_grad, value_grad, expand_fold, value_fold = gate_kernel(
        me, branch_grad, value_act, gate_slope, out_parts
    )
    value_grads = weight_grad(normed, value_grad, 32, width, 512, me, "grad_value")
    value_sum = reduce_chunk(*value_grads, 48)
    expand_grads = weight_grad(ssm_low, expand_grad, 16, width, 512, me, "grad_expand")
    expand_sum = reduce_chunk(*expand_grads, 32)
    ssm_grad, totals, suffixes, back_spans, back_map, skip_fold = state_kernel(
        me, ends, base, expand_grad, act, decays, small_parts, expand_parts
    )
    back_maps = gather_maps(back_map)
    state_send, state_keep = weight_grad(states_low, ssm_grad, 16, channels, 512, me, "grad_state")
    reduce_grad, grad_tokens, channel_folds, norm_folds = input_kernel(
        me, place, back_maps, back_spans, totals, suffixes, act, prior, ssm_grad, reduce_slope,
        skip, inflow, gain, token_rows, cot_rows, value_grad, small_parts, value_parts
    )
    reduce_send, reduce_keep = weight_grad(
        normed, reduce_grad, 32, channels, 512, me, "grad_reduce"
    )
    output = out_kernel(me, live, base, gated, token_rows, out_add, out_parts)

    decay_sum, inflow_sum, grad_reduce_add = jnp.sum(channel_folds, axis=1)
    grad_scale, grad_offset = jnp.sum(norm_folds, axis=1)
    inflow_pull = jnp.exp(-2.0 * rates[0]) / inflow[0]
    grad_rates = inflow_pull * inflow_sum - decay_sum
    grad_skip = jnp.sum(skip_fold, axis=0)
    grad_expand_add, grad_value_add = jnp.sum(expand_fold, axis=0), jnp.sum(value_fold, axis=0)

    sums = (
        grad_scale,
        grad_offset,
        grad_value_add,
        grad_reduce_add,
        grad_rates,
        grad_skip,
        grad_expand_add,
        grad_out_add,
    )
    table = jnp.concatenate([v.reshape(shards, -1) for v in sums], axis=1).astype(half)
    table = jnp.pad(table[:, None], ((0, 0), (0, 7), (0, channels - used)))
    k = jnp.arange(shards // 2, dtype=jnp.int32)
    rel = ((k >> 3) & 1) * 2 + ((k >> 2) & 1) * 4 + ((k >> 1) & 1) * 8 + (k & 1) * 16
    small_sum = reduce_chunk(
        jnp.concatenate([reduce_send, state_send, table[(rel + 1) ^ me]], axis=1),
        jnp.concatenate([reduce_keep, state_keep, table[rel ^ me]], axis=1),
        0,
    )
    vector_sum = small_sum[48]
    vector_sums = [reduce_low(vector_sum[p : p + n]) for p, n in zip(places, sizes)]
    return (
        output.reshape(tokens.shape),
        grad_tokens.reshape(tokens.shape),
        vector_sums[0],
        vector_sums[1],
        reduce_low(from_column_blocks(value_sum, blocks)),
        vector_sums[2],
        reduce_low(small_sum[:32]),
        vector_sums[3],
        vector_sums[4],
        vector_sums[5],
        reduce_low(small_sum[32:48]),
        reduce_low(from_column_blocks(expand_sum, blocks)),
        vector_sums[6],
        reduce_low(out_sum),
        vector_sums[7],
    )


def solution(mesh):
    rows, vector, matrix = P("dp", "seq", None), P(("dp", "seq")), P(("dp", "seq"), None)
    return jax.shard_map(
        on_device,
        mesh=mesh,
        in_specs=(
            rows,
            P("dp", None),
            rows,
            vector,
            vector,
            matrix,
            vector,
            matrix,
            vector,
            vector,
            vector,
            matrix,
            matrix,
            vector,
            matrix,
            vector,
        ),
        out_specs=(
            rows,
            rows,
            vector,
            vector,
            matrix,
            vector,
            matrix,
            vector,
            vector,
            vector,
            matrix,
            matrix,
            vector,
            matrix,
            vector,
        ),
        check_vma=False,
    )
```

```python
import jax
import jax.numpy as jnp
from jax import lax
from jax.experimental import pallas as pl
from jax.experimental.pallas import tpu as pltpu
from jax.sharding import PartitionSpec as P

EPSILON = 1e-05
HALF = jnp.bfloat16
SINGLE = jnp.float32
MAIN = 5
SEGMENTS = 8
MIB = 1 << 20


def log2(n):
    return n.bit_length() - 1


def device_number():
    return lax.axis_index("dp") * lax.axis_size("seq") + lax.axis_index("seq")


def low_bits():
    return log2(lax.axis_size("dp") * lax.axis_size("seq")) - MAIN


def exchange(values, *bits):
    inner = log2(lax.axis_size("seq"))
    axis, first = ("seq", 0) if bits[0] < inner else ("dp", inner)
    flip = sum(1 << (bit - first) for bit in bits)
    return lax.ppermute(values, axis, [(i, i ^ flip) for i in range(lax.axis_size(axis))])


def gather_low(values):
    for bit in range(low_bits()):
        other = exchange(values, bit)
        upper = (device_number() >> bit) & 1
        values = jnp.where(
            upper == 1, jnp.concatenate([other, values]), jnp.concatenate([values, other])
        )
    return values


def reduce_low(values):
    for bit in reversed(range(low_bits())):
        upper = (device_number() >> bit) & 1
        halves = values.reshape((2, values.shape[0] // 2) + values.shape[1:])
        mine = lax.dynamic_index_in_dim(halves, upper, 0, False)
        theirs = lax.dynamic_index_in_dim(halves, 1 - upper, 0, False)
        values = mine + exchange(theirs, bit)
    return values


def join(own, other):
    return jnp.concatenate([own, other])


def gather_steps(rows, split):
    core, bit_x, bit_y, bit_z, bit_far = (low_bits() + i for i in range(MAIN))
    held = rows[None]
    if not split:
        others = yield [exchange(held, *bits) for bits in ((bit_far,), (bit_z,), (bit_z, bit_far))]
        held = jnp.concatenate([held, *others])
        (other,) = yield [exchange(held, bit_y)]
        held = join(held, other)
        other, held_core = yield [exchange(held, bit_x), exchange(held, core)]
        (other_core,) = yield [exchange(other, core)]
        return [held, other, held_core, other_core]
    (other,) = yield [exchange(held, bit_far)]
    held = join(held, other)
    (other,) = yield [exchange(held, bit_z)]
    held = join(held, other)
    first, second = held[:, :split], held[:, split:]
    from_y, from_x = yield [exchange(first, bit_y), exchange(second, bit_x)]
    first, second = join(first, from_y), join(second, from_x)
    from_x, from_y, *near = yield [
        exchange(first, bit_x),
        exchange(second, bit_y),
        exchange(first, core),
        exchange(second, core),
    ]
    far = yield [exchange(from_x, core), exchange(from_y, core)]
    return [first, from_x, near[0], far[0], second, from_y, near[1], far[1]]


def spot(rel, x_first):
    core = rel & 1
    bit_x, bit_y = (rel >> 1) & 1, (rel >> 2) & 1
    bit_z, bit_far = (rel >> 3) & 1, (rel >> 4) & 1
    if x_first:
        return core, bit_x * 8 + bit_y * 4 + bit_z * 2 + bit_far
    return core, bit_y * 8 + bit_x * 4 + bit_z * 2 + bit_far


def load_weights(mine, parts, target, pieces, sems):
    def one(k, carry):
        bits = ((k >> 2) & 1, ((k >> 1) & 1) * 8 + (k & 1) * 16)
        for four, row, rows, group, held, to_row in pieces:
            lead_bit, other_bit = (2, 4) if four == 0 else (4, 2)
            for side in range(4):
                rel = (side >> 1) + (side & 1) * lead_bit + bits[0] * other_bit + bits[1]
                shard = rel ^ mine
                to = group
                if group is None:
                    per_group = target.shape[1] // held
                    to, shard = shard // per_group, shard % per_group
                at = pl.multiple_of(shard * held + to_row, 16)
                source = parts[4 * four + side].at[k, pl.ds(row, rows)]
                pltpu.make_async_copy(source, target.at[to, pl.ds(at, rows)], sems.at[to]).start()
        return carry

    lax.fori_loop(0, 8, one, 0)


def await_weights(target, group, sems):
    pltpu.make_async_copy(target.at[group], target.at[group], sems.at[group]).wait()


REDUCE_PIECES = [(0, 0, 32, 0, 32, 0)]
STATE_PIECES = [(0, 32, 16, 0, 16, 0)]
EXPAND_PIECES = [(g // 2, 16 * (g % 2), 16, g, 16, 0) for g in range(4)]
OUT_PIECES = [(0, 0, 48, None, 96, 0), (1, 0, 48, None, 96, 48)]

SMEM = pl.BlockSpec(memory_space=pltpu.SMEM)
FAR = pl.BlockSpec(memory_space=pltpu.HBM)


def cost(micros):
    return pl.CostEstimate(flops=int(micros * 1e9), bytes_accessed=MIB, transcendentals=0)

ROOM = pltpu.CompilerParams(vmem_limit_bytes=60 * MIB)


def whole(*shape):
    return pl.BlockSpec(shape, lambda *_: (0,) * len(shape))


def dot(left, right, left_dim=1, right_dim=0):
    return lax.dot_general(
        left, right, (((left_dim,), (right_dim,)), ((), ())), preferred_element_type=SINGLE
    )


def gelu_pair(v):
    c, d = 0.7978845608028654, 0.7978845608028654 * 0.044715
    square = v * v
    h = 0.5 + 0.5 * jnp.tanh(v * (c + d * square))
    act = v * h
    return act, h + 2.0 * act * (1.0 - h) * (c + 3.0 * d * square)


def norm_terms(x):
    center = x - jnp.mean(x, axis=-1, keepdims=True)
    inverse = lax.rsqrt(jnp.mean(center * center, axis=-1, keepdims=True) + EPSILON)
    return center * inverse, inverse


def lanes_joined(ref, rows):
    return jnp.concatenate([ref[c, rows, :] for c in range(ref.shape[0])], axis=1)


def powers(decay, count, rows):
    power, out = decay, jnp.ones((rows, decay.shape[1]), SINGLE)
    for bit in range(8):
        out = jnp.where((count >> bit) & 1 == 1, out * power, out)
        power = power * power
    return out


def starts_near(ends_ref, places, reverse):
    far = jnp.full(places.shape, 1 << 20, jnp.int32)
    for i in range(7):
        away = ends_ref[i] - places if reverse else places - ends_ref[i]
        far = jnp.where(away >= (1 if reverse else 0), jnp.minimum(far, away), far)
    return far


def scan_block(ends_ref, first, decay, value_ref, reverse):
    columns, block, lanes = value_ref.shape
    span = block // SEGMENTS
    row = lax.broadcasted_iota(jnp.int32, (8, lanes), 0)
    order = 7 - row if reverse else row
    factors = []
    for c in range(columns):
        one = jnp.broadcast_to(decay[:, c * lanes : (c + 1) * lanes], (8, lanes))
        two = one * one
        steps = [jnp.where(order >= d, f, 0.0) for d, f in ((1, one), (2, two), (4, two * two))]
        factors.append(steps + [powers(one, order + 1, 8)])

    def tile(lap, carry):
        k = span // 8 - 1 - lap if reverse else lap
        out = []
        for s in range(SEGMENTS):
            at = pl.multiple_of(s * span + k * 8, 8)
            near = starts_near(ends_ref, first + at + row, reverse) + (0 if reverse else 1)
            for c in range(columns):
                x = value_ref[c, pl.ds(at, 8), :]
                for step, d in enumerate((1, 2, 4)):
                    moved = pltpu.roll(x, 8 - d if reverse else d, 0)
                    x = x + jnp.where(near > d, factors[c][step], 0.0) * moved
                whole_way = jnp.where(near > order + 1, factors[c][3], 0.0)
                x = x + whole_way * carry[s * columns + c]
                value_ref[c, pl.ds(at, 8), :] = x
                edge = x[:1] if reverse else x[7:]
                out.append(jnp.broadcast_to(edge, (8, lanes)))
        return out

    zero = [jnp.zeros((8, lanes), SINGLE)] * (columns * SEGMENTS)
    ends = lax.fori_loop(0, span // 8, tile, zero)
    states, products = [], []
    power = decay
    for _ in range(log2(span)):
        power = power * power
    for s in range(SEGMENTS):
        states.append(
            jnp.concatenate([ends[s * columns + c][:1] for c in range(columns)], axis=1)
        )
        low = first + s * span + (1 if reverse else 0)
        broken = jnp.int32(0)
        for i in range(7):
            inside = (ends_ref[i] >= low) & (ends_ref[i] < low + span)
            broken = jnp.where(inside, 1, broken)
        products.append(jnp.where(broken == 1, 0.0, power))
    return jnp.concatenate(products, axis=0), jnp.concatenate(states, axis=0)


def span_products(ends_ref, first, table, lanes, reverse):
    span, channels = table.shape
    row = lax.broadcasted_iota(jnp.int32, (span, lanes), 0)
    near = starts_near(ends_ref, first + row, reverse)
    kept = near > (span - row if reverse else row)
    return jnp.where(jnp.concatenate([kept] * (channels // lanes), axis=1), table, 0.0)


def span_table(decay, span, reverse):
    row = lax.broadcasted_iota(jnp.int32, (span, decay.shape[1]), 0)
    return powers(decay, span - row if reverse else row + 1, span)


def span_carries(product, state, carry, reverse):
    carries = [None] * SEGMENTS
    for s in range(SEGMENTS)[::-1] if reverse else range(SEGMENTS):
        carries[s] = carry
        carry = product[s : s + 1] * carry + state[s : s + 1]
    return carries, carry


def block_carry(place, maps_ref, reverse):
    count = maps_ref.shape[0]
    carry = jnp.zeros((1, maps_ref.shape[2]), SINGLE)
    for s in range(count)[::-1] if reverse else range(count):
        rel = s ^ place
        inside = s > place if reverse else s < place
        moved = maps_ref[rel, 0:1, :] * carry + maps_ref[rel, 1:2, :]
        carry = jnp.where(inside, moved, carry)
    return carry


def whole_map(product, state, reverse):
    zero = jnp.zeros((1, product.shape[1]), SINGLE)
    _, ending = span_carries(product, state, zero, reverse)
    through = zero + 1.0
    for s in range(SEGMENTS):
        through = through * product[s : s + 1]
    return through, ending


def gather_maps(maps):
    held = maps[None]
    for bit in range(log2(lax.axis_size("seq"))):
        held = join(held, exchange(held, bit))
    return held


def reduce_kernel(scalars, tokens, gain, shift, bias, decay, inflow, parts):
    block, width = tokens.shape
    channels = bias.shape[1]
    tile = 256
    columns = channels // 128

    def body(me, ends, base, x_ref, gain_ref, shift_ref, bias_ref, decay_ref, inflow_ref, s0, s1, s2, s3,
             normed_ref, act_ref, slope_ref, state_ref, span_ref, map_ref,
             weight, sems):
        load_weights(me[0], (s0, s1, s2, s3), weight, REDUCE_PIECES, sems)

        def norm(t, carry):
            rows = pl.ds(pl.multiple_of(t * tile, tile), tile)
            n, _ = norm_terms(x_ref[rows, :].astype(SINGLE))
            normed_ref[rows, :] = (n * gain_ref[...] + shift_ref[...]).astype(HALF)
            return carry

        lax.fori_loop(0, block // tile, norm, 0)
        await_weights(weight, 0, sems)

        def reduce(t, carry):
            rows = pl.ds(pl.multiple_of(t * tile, tile), tile)
            act, slope = gelu_pair(dot(normed_ref[rows, :], weight[0]) + bias_ref[...])
            act_ref[rows, :] = act
            slope_ref[rows, :] = slope.astype(HALF)
            flow = act * inflow_ref[...]
            for c in range(columns):
                state_ref[c, rows, :] = flow[:, c * 128 : (c + 1) * 128]
            return carry

        lax.fori_loop(0, block // tile, reduce, 0)
        product, state = scan_block(ends, base[0], decay_ref[...], state_ref, False)
        span_ref[0], span_ref[1] = product, state
        map_ref[0:1, :], map_ref[1:2, :] = whole_map(product, state, False)

    vm = pl.BlockSpec(memory_space=pltpu.VMEM)
    return pl.pallas_call(
        body,
        name="reduce_forward",
        out_shape=[
            jax.ShapeDtypeStruct((block, width), HALF),
            jax.ShapeDtypeStruct((block, channels), SINGLE),
            jax.ShapeDtypeStruct((block, channels), HALF),
            jax.ShapeDtypeStruct((columns, block, 128), SINGLE),
            jax.ShapeDtypeStruct((2, SEGMENTS, channels), SINGLE),
            jax.ShapeDtypeStruct((2, channels), SINGLE),
        ],
        in_specs=[SMEM] * 3 + [vm] * 6 + [FAR] * 4,
        out_specs=[vm] * 6,
        scratch_shapes=[
            pltpu.VMEM((1, width, channels), HALF),
            pltpu.SemaphoreType.DMA((1,)),
        ],
        compiler_params=ROOM,
        cost_estimate=cost(8),
    )(*scalars[:3], tokens, gain, shift, bias, decay, inflow, *parts)


def staged(count, product, finish):
    ahead = product(0)
    for c in range(count):
        now = ahead
        if c + 1 < count:
            ahead = product(c + 1)
        finish(c, now)


def once(*shape):
    return pl.BlockSpec(shape, lambda *_: (0,) * len(shape), pipeline_mode=pl.Buffered(1))


def states_kernel(me, place, ends, base, maps, spans, states, act, skip, inflow, decay, parts):
    columns, block, lanes = states.shape
    channels = act.shape[1]
    span = block // SEGMENTS

    def body(me, place_ref, ends_ref, base_ref, maps_ref, span_ref, state_ref, act_ref, skip_ref,
             inflow_ref, decay_ref, s0, s1, s2, s3, low_ref, prior_ref, ssm_ref,
             carry_ref, weight, sems):
        load_weights(me[0], (s0, s1, s2, s3), weight, STATE_PIECES, sems)
        entering = block_carry(place_ref[0], maps_ref, False)
        carries, _ = span_carries(span_ref[0], span_ref[1], entering, False)
        table = span_table(decay_ref[...], span, False)
        for s in range(SEGMENTS):
            carry_ref[s] = jnp.broadcast_to(carries[s], (8, channels))

        def one_span(s, done):
            rows = pl.ds(pl.multiple_of(s * span, span), span)
            product = span_products(ends_ref, base_ref[0] + s * span, table, lanes, False)
            state = lanes_joined(state_ref, rows) + product * carry_ref[s][:1]
            low_ref[rows, :] = state.astype(HALF)
            prior_ref[rows, :] = (state - inflow_ref[...] * act_ref[rows, :]).astype(HALF)
            return done

        lax.fori_loop(0, SEGMENTS, one_span, 0)
        await_weights(weight, 0, sems)
        ssm = dot(low_ref[...], weight[0]) + skip_ref[...] * act_ref[...]
        ssm_ref[...] = ssm.astype(HALF)

    vm = pl.BlockSpec(memory_space=pltpu.VMEM)
    return pl.pallas_call(
        body,
        name="states_forward",
        out_shape=[jax.ShapeDtypeStruct((block, channels), HALF)] * 3,
        in_specs=[SMEM] * 4 + [vm] * 7 + [FAR] * 4,
        out_specs=[vm] * 3,
        scratch_shapes=[
            pltpu.VMEM((SEGMENTS, 8, channels), SINGLE),
            pltpu.VMEM((1, channels, channels), HALF), pltpu.SemaphoreType.DMA((1,))],
        compiler_params=ROOM,
        cost_estimate=cost(3),
    )(me, place, ends, base, maps, spans, states, act, skip, inflow, decay, *parts)


def forward_kernel(me, normed, ssm, branch_grad, value_bias, expand_bias, value_weight,
                   expand_parts):
    block, width = normed.shape
    channels = ssm.shape[1]
    gate = value_bias.shape[1]
    groups, sub = 4, 256
    depth = gate // groups

    def body(me, x_ref, ssm_ref, grad_ref, value_bias_ref, expand_bias_ref, value,
             q0, q1, q2, q3, q4, q5, q6, q7, act_ref, gated_ref, slope_ref, sum_ref,
             expand, expand_sems):
        j = pl.program_id(0)

        @pl.when(j == 0)
        def _():
            load_weights(
                me[0], (q0, q1, q2, q3, q4, q5, q6, q7), expand, EXPAND_PIECES, expand_sems
            )

        for g in range(groups):

            @pl.when(j == g)
            def _():
                await_weights(expand, g, expand_sems)

        for c in range(depth // sub):
            cols = pl.ds(c * sub, sub)
            pre = dot(x_ref[...], value[:, cols]) + value_bias_ref[:, cols]
            act, slope = gelu_pair(pre)
            pre = dot(ssm_ref[...], expand[j, :, cols]) + expand_bias_ref[:, cols]
            act_ref[:, cols] = act.astype(HALF)
            gated_ref[:, cols] = (act * pre).astype(HALF)
            slope_ref[:, cols] = (slope * pre).astype(HALF)
        for c in range(width // sub):
            cols = pl.ds(c * sub, sub)
            sum_ref[:, cols] = dot(gated_ref[...], grad_ref[:, cols], 0, 0).astype(HALF)

    wide = pl.BlockSpec((block, depth), lambda j: (0, j))
    bias = pl.BlockSpec((1, depth), lambda j: (0, j))
    return pl.pallas_call(
        body,
        name="gate_forward",
        out_shape=[jax.ShapeDtypeStruct((block, gate), HALF)] * 3
        + [jax.ShapeDtypeStruct((gate, width), HALF)],
        grid=(groups,),
        in_specs=[
            SMEM,
            once(block, width),
            once(block, channels),
            once(block, width),
            bias,
            bias,
            pl.BlockSpec((width, depth), lambda j: (0, j)),
        ]
        + [FAR] * 8,
        out_specs=[wide] * 3 + [pl.BlockSpec((depth, width), lambda j: (j, 0))],
        scratch_shapes=[
            pltpu.VMEM((groups, channels, depth), HALF),
            pltpu.SemaphoreType.DMA((groups,)),
        ],
        compiler_params=ROOM,
        cost_estimate=cost(16),
    )(me, normed, ssm, branch_grad, value_bias, expand_bias, value_weight,
      *expand_parts)


def fold(values):
    return jnp.sum(values.reshape(values.shape[0] // 8, 8, values.shape[1]), axis=0)


def out_kernel(me, live, base, gated, tokens, bias, parts):
    block, gate = gated.shape
    width = tokens.shape[1]
    tile, sub, groups = block // 2, 256, 4
    depth = gate // groups

    def body(me, live_ref, base_ref, gated_ref, x_ref, bias_ref, p0, p1, p2, p3, p4, p5, p6, p7,
             out_ref, weight, sems):
        t = pl.program_id(0)

        @pl.when(t == 0)
        def _():
            load_weights(me[0], (p0, p1, p2, p3, p4, p5, p6, p7), weight, OUT_PIECES, sems)
            await_weights(weight, 0, sems)

        place = base_ref[0] + t * tile + lax.broadcasted_iota(jnp.int32, (tile, 1), 0)

        def column(c, carry):
            cols = pl.ds(pl.multiple_of(c * sub, sub), sub)
            branch = dot(gated_ref[...], weight[0, :, cols]) + bias_ref[:, cols]
            branch = jnp.where(place < live_ref[0], branch, 0.0)
            out_ref[:, cols] = (x_ref[:, cols].astype(SINGLE) + branch).astype(HALF)
            return carry

        lax.fori_loop(0, width // sub, column, 0)

    return pl.pallas_call(
        body,
        name="out_forward",
        out_shape=jax.ShapeDtypeStruct((block, width), HALF),
        grid=(block // tile,),
        in_specs=[
            SMEM,
            SMEM,
            SMEM,
            pl.BlockSpec((tile, gate), lambda t: (t, 0)),
            pl.BlockSpec((tile, width), lambda t: (t, 0)),
            whole(1, width),
        ]
        + [FAR] * 8,
        out_specs=pl.BlockSpec((tile, width), lambda t: (t, 0)),
        scratch_shapes=[pltpu.VMEM((1, gate, width), HALF), pltpu.SemaphoreType.DMA((1,))],
        compiler_params=ROOM,
        cost_estimate=cost(6),
    )(me, live, base, gated, tokens, bias, *parts)


def put_halves(mine, made, send_ref, keep_ref):
    half, rows, _ = send_ref.shape
    for k in range(half):
        rel = ((k >> 3) & 1) * 2 + ((k >> 2) & 1) * 4 + ((k >> 1) & 1) * 8 + (k & 1) * 16
        for side, ref in ((0, keep_ref), (1, send_ref)):
            ref[k] = made[pl.ds(pl.multiple_of(((rel + side) ^ mine) * rows, rows), rows), :]


def gate_kernel(me, branch_grad, normed, ssm, act, slope, parts, expand_parts):
    block, width = branch_grad.shape
    gate, channels = act.shape[1], ssm.shape[1]
    groups, sub = 4, 256
    depth = gate // groups
    half = 1 << (MAIN - 1)
    value_rows, expand_rows = width // (2 * half), channels // (2 * half)

    def body(me, grad_ref, x_ref, ssm_ref, act_ref, slope_ref, p0, p1, p2, p3, p4, p5, p6, p7,
             q0, q1, q2, q3, q4, q5, q6, q7, value_ref, expand_sum, value_sum, state_ref,
             value_send, value_keep, expand_send, expand_keep,
             expand_ref, made, made_low, weight, expand_weight, sems, expand_sems):
        j = pl.program_id(0)

        @pl.when(j == 0)
        def _():
            load_weights(me[0], (p0, p1, p2, p3, p4, p5, p6, p7), weight, OUT_PIECES, sems)
            load_weights(
                me[0], (q0, q1, q2, q3, q4, q5, q6, q7), expand_weight, EXPAND_PIECES, expand_sems
            )
            state_ref[...] = jnp.zeros_like(state_ref)

        for g in range(groups):

            @pl.when(j == g)
            def _():
                await_weights(weight, g, sems)
                await_weights(expand_weight, g, expand_sems)

        for c in range(depth // sub):
            cols = pl.ds(c * sub, sub)
            gated_grad = dot(grad_ref[...], weight[j, cols, :], 1, 1)
            expand = gated_grad * act_ref[:, cols].astype(SINGLE)
            value = gated_grad * slope_ref[:, cols].astype(SINGLE)
            expand_ref[:, cols] = expand.astype(HALF)
            value_ref[:, cols] = value.astype(HALF)
            expand_sum[:, cols] = fold(expand)
            value_sum[:, cols] = fold(value)
        for c in range(depth // sub):
            cols = pl.ds(c * sub, sub)
            made[:, cols] = dot(x_ref[...], value_ref[:, cols], 0, 0).astype(HALF)
            made_low[:, cols] = dot(ssm_ref[...], expand_ref[:, cols], 0, 0).astype(HALF)
        state_ref[...] += dot(expand_ref[...], expand_weight[j], 1, 1)
        put_halves(me[0], made, value_send, value_keep)
        put_halves(me[0], made_low, expand_send, expand_keep)

    wide = pl.BlockSpec((block, depth), lambda j: (0, j))
    sums = pl.BlockSpec((8, depth), lambda j: (0, j))
    halves = [
        (jax.ShapeDtypeStruct((half, groups * rows, depth), HALF),
         pl.BlockSpec((half, rows, depth), lambda j: (0, j, 0)))
        for rows in (value_rows, value_rows, expand_rows, expand_rows)
    ]
    return pl.pallas_call(
        body,
        name="gate_backward",
        out_shape=[jax.ShapeDtypeStruct((block, gate), HALF)]
        + [jax.ShapeDtypeStruct((8, gate), SINGLE)] * 2
        + [jax.ShapeDtypeStruct((block, channels), SINGLE)]
        + [h[0] for h in halves],
        grid=(groups,),
        in_specs=[
            SMEM,
            once(block, width),
            once(block, width),
            once(block, channels),
            wide,
            wide,
        ]
        + [FAR] * 16,
        out_specs=[wide, sums, sums, once(block, channels)] + [h[1] for h in halves],
        scratch_shapes=[
            pltpu.VMEM((block, depth), HALF),
            pltpu.VMEM((width, depth), HALF),
            pltpu.VMEM((channels, depth), HALF),
            pltpu.VMEM((groups, depth, width), HALF),
            pltpu.VMEM((groups, channels, depth), HALF),
            pltpu.SemaphoreType.DMA((groups,)),
            pltpu.SemaphoreType.DMA((groups,)),
        ],
        compiler_params=ROOM,
        cost_estimate=cost(16),
    )(me, branch_grad, normed, ssm, act, slope, *parts, *expand_parts)


def state_kernel(me, ends, base, ssm_grad, act, decay, parts):
    block, channels = ssm_grad.shape
    columns, tile = channels // 128, 256

    def body(me, ends_ref, base_ref, grad_ref, act_ref, decay_ref, s0, s1, s2, s3,
             ssm_ref, total_ref, span_ref, map_ref, skip_sum, weight, sems):
        load_weights(me[0], (s0, s1, s2, s3), weight, STATE_PIECES, sems)
        sums = jnp.zeros((8, channels), SINGLE)
        for t in range(block // tile):
            rows = pl.ds(t * tile, tile)
            grad = grad_ref[rows, :]
            ssm_ref[rows, :] = grad.astype(HALF)
            sums += fold(grad * act_ref[rows, :])
        skip_sum[...] = sums
        await_weights(weight, 0, sems)
        for c in range(channels // 256):
            state = dot(ssm_ref[...], weight[0, c * 256 : (c + 1) * 256, :], 1, 1)
            total_ref[2 * c], total_ref[2 * c + 1] = state[:, :128], state[:, 128:]
        product, ending = scan_block(ends_ref, base_ref[0], decay_ref[...], total_ref, True)
        span_ref[0], span_ref[1] = product, ending
        map_ref[0:1, :], map_ref[1:2, :] = whole_map(product, ending, True)

    vm = pl.BlockSpec(memory_space=pltpu.VMEM)
    return pl.pallas_call(
        body,
        name="state_backward",
        out_shape=[
            jax.ShapeDtypeStruct((block, channels), HALF),
            jax.ShapeDtypeStruct((columns, block, 128), SINGLE),
            jax.ShapeDtypeStruct((2, SEGMENTS, channels), SINGLE),
            jax.ShapeDtypeStruct((2, channels), SINGLE),
            jax.ShapeDtypeStruct((8, channels), SINGLE),
        ],
        in_specs=[SMEM] * 3 + [vm] * 3 + [FAR] * 4,
        out_specs=[vm] * 5,
        scratch_shapes=[pltpu.VMEM((1, channels, channels), HALF), pltpu.SemaphoreType.DMA((1,))],
        compiler_params=ROOM,
        cost_estimate=cost(4),
    )(me, ends, base, ssm_grad, act, decay, *parts)


def input_kernel(me, place, ends, base, maps, spans, totals, act, prior, ssm_grad, slope, skip,
                 inflow, decay, gain, tokens, cotangent, value_grad, weight,
                 small_parts):
    block, width = tokens.shape
    channels = act.shape[1]
    gate = value_grad.shape[1]
    tile, sub = 256, 256
    columns = channels // 128
    span = block // SEGMENTS

    def body(me, place_ref, ends_ref, base_ref, maps_ref, span_ref, total_ref, act_ref,
             prior_ref, ssm_ref, slope_ref, skip_ref, inflow_ref, decay_ref, gain_ref,
             weight_ref, x_far, cot_far, value_far, s0, s1, s2, s3,
             reduce_ref, out_ref, channel_sums, norm_sums, carry_ref, grads, small,
             x_ref, cot_ref, value_ref, small_sems, sems):
        j = pl.program_id(0)
        value_copy = pltpu.make_async_copy(value_far, value_ref, sems.at[0])
        x_copy = pltpu.make_async_copy(x_far, x_ref, sems.at[1])
        cot_copy = pltpu.make_async_copy(cot_far, cot_ref, sems.at[2])

        @pl.when(j == 0)
        def _():
            load_weights(me[0], (s0, s1, s2, s3), small, REDUCE_PIECES, small_sems)
            value_copy.start()
            x_copy.start()
            cot_copy.start()
            entering = block_carry(place_ref[0], maps_ref, True)
            carries, _ = span_carries(span_ref[0], span_ref[1], entering, True)
            table = span_table(decay_ref[...], span, True)
            for s in range(SEGMENTS):
                carry_ref[s] = jnp.broadcast_to(carries[s], (8, channels))

            def one_span(s, sums):
                rows = pl.ds(pl.multiple_of(s * span, span), span)
                product = span_products(ends_ref, base_ref[0] + s * span, table, 128, True)
                total = lanes_joined(total_ref, rows) + product * carry_ref[s][:1]
                reduced = ssm_ref[rows, :].astype(SINGLE) * skip_ref[...] + inflow_ref[...] * total
                reduced = reduced * slope_ref[rows, :].astype(SINGLE)
                reduce_ref[rows, :] = reduced.astype(HALF)
                terms = (total * prior_ref[rows, :].astype(SINGLE), total * act_ref[rows, :], reduced)
                return [old + fold(new) for old, new in zip(sums, terms)]

            sums = [jnp.zeros((8, channels), SINGLE)] * 3
            sums = lax.fori_loop(0, SEGMENTS, one_span, sums)
            for i in range(3):
                channel_sums[i] = sums[i]
            await_weights(small, 0, small_sems)
            value_copy.wait()

        at = pl.ds(pl.multiple_of(j * sub, sub), sub)
        grads[j] = dot(value_ref[...], weight_ref[...], 1, 1) + dot(
            reduce_ref[...], small[0, at, :], 1, 1
        )

        @pl.when(j == width // sub - 1)
        def _():
            x_copy.wait()
            cot_copy.wait()
            norm_sums[...] = jnp.zeros_like(norm_sums)

            def norm_back(t, carry):
                rows = pl.ds(pl.multiple_of(t * tile, tile), tile)
                grad = lanes_joined(grads, rows)
                n, inverse = norm_terms(x_ref[rows, :].astype(SINGLE))
                norm_sums[0] += fold(grad * n)
                norm_sums[1] += fold(grad)
                h = grad * gain_ref[...]
                mean_h = jnp.mean(h, axis=-1, keepdims=True)
                mean_hn = jnp.mean(h * n, axis=-1, keepdims=True)
                back = inverse * (h - mean_h - n * mean_hn)
                out_ref[rows, :] = (cot_ref[rows, :].astype(SINGLE) + back).astype(HALF)
                return carry

            lax.fori_loop(0, block // tile, norm_back, 0)

    tall = once(columns, block, 128)
    narrow = once(block, channels)
    return pl.pallas_call(
        body,
        name="input_backward",
        out_shape=[
            jax.ShapeDtypeStruct((block, channels), HALF),
            jax.ShapeDtypeStruct((block, width), HALF),
            jax.ShapeDtypeStruct((3, 8, channels), SINGLE),
            jax.ShapeDtypeStruct((2, 8, width), SINGLE),
        ],
        grid=(width // sub,),
        in_specs=[
            SMEM,
            SMEM,
            SMEM,
            SMEM,
            whole(*maps.shape),
            whole(*spans.shape),
            tall,
            narrow,
            narrow,
            narrow,
            narrow,
            whole(1, channels),
            whole(1, channels),
            whole(1, channels),
            whole(1, width),
            pl.BlockSpec((sub, gate), lambda j: (j, 0)),
        ]
        + [FAR] * 7,
        out_specs=[narrow, once(block, width), whole(3, 8, channels), whole(2, 8, width)],
        scratch_shapes=[
            pltpu.VMEM((SEGMENTS, 8, channels), SINGLE),
            pltpu.VMEM((width // sub, block, sub), SINGLE),
            pltpu.VMEM((1, width, channels), HALF),
            pltpu.VMEM((block, width), HALF),
            pltpu.VMEM((block, width), HALF),
            pltpu.VMEM((block, gate), HALF),
            pltpu.SemaphoreType.DMA((1,)),
            pltpu.SemaphoreType.DMA((3,)),
        ],
        compiler_params=ROOM,
        cost_estimate=cost(10),
    )(me, place, ends, base, maps, spans, totals, act, prior, ssm_grad, slope, skip, inflow, decay,
      gain, weight, tokens, cotangent, value_grad, *small_parts)


def unpack_kernel(me, sizes, parts):
    shards = 1 << MAIN
    lanes = 128
    rates_at = 4

    def body(me, *refs):
        ins, outs, table = refs[:4], refs[4:-1], refs[-1]
        for side in range(4):
            for k in range(8):
                rel = (side >> 1) + (side & 1) * 2 + ((k >> 2) & 1) * 4
                rel += ((k >> 1) & 1) * 8 + (k & 1) * 16
                table[rel ^ me[0]] = ins[side][k, :, :lanes].astype(SINGLE)
        for i, n in enumerate(sizes):
            for shard in range(shards):
                outs[i][:, shard * n : (shard + 1) * n] = table[shard, i : i + 1, :n]
        rates = outs[rates_at][...]
        decay_ref, inflow_ref, pull_ref = outs[len(sizes) :]
        inflow = jnp.sqrt(one_less_exp(2.0 * rates))
        decay_ref[...] = jnp.exp(-rates)
        inflow_ref[...] = inflow
        pull_ref[...] = jnp.exp(-2.0 * rates) / inflow

    channels = parts[0].shape[2]
    rows = parts[0].shape[1]
    widths = [n * shards for n in sizes] + [sizes[rates_at] * shards] * 3
    return pl.pallas_call(
        body,
        name="unpack",
        out_shape=[jax.ShapeDtypeStruct((1, n), SINGLE) for n in widths],
        grid=(1,),
        in_specs=[SMEM]
        + [pl.BlockSpec((8, 8, channels), lambda i: (0, rows // 8 - 1, 0))] * 4,
        out_specs=[whole(1, n) for n in widths],
        scratch_shapes=[pltpu.VMEM((shards, 8, lanes), SINGLE)],
        compiler_params=ROOM,
        cost_estimate=cost(1),
    )(me, *parts)


def sums_kernel(me, sizes, norm_folds, value_fold, channel_folds, pull, skip_fold, expand_fold,
                out_fold):
    shards = 1 << MAIN
    half = shards // 2
    channels = skip_fold.shape[1]
    lanes = 128

    def body(me, norm_ref, value_ref, channel_ref, pull_ref, skip_ref, expand_ref, out_ref,
             send_ref, keep_ref, table):
        def total(values):
            return jnp.sum(values, axis=0, keepdims=True)

        rates = pull_ref[...] * total(channel_ref[1]) - total(channel_ref[0])
        rows = (
            total(norm_ref[0]),
            total(norm_ref[1]),
            total(value_ref[...]),
            total(channel_ref[2]),
            rates,
            total(skip_ref[...]),
            total(expand_ref[...]),
            total(out_ref[...]),
        )
        table[...] = jnp.zeros_like(table)
        for i, (n, row) in enumerate(zip(sizes, rows)):
            for shard in range(shards):
                table[shard, i : i + 1, :n] = row[:, shard * n : (shard + 1) * n]
        send_ref[...] = jnp.zeros_like(send_ref)
        keep_ref[...] = jnp.zeros_like(keep_ref)
        for k in range(half):
            rel = ((k >> 3) & 1) * 2 + ((k >> 2) & 1) * 4 + ((k >> 1) & 1) * 8 + (k & 1) * 16
            keep_ref[k, :, :lanes] = table[rel ^ me[0]].astype(HALF)
            send_ref[k, :, :lanes] = table[(rel + 1) ^ me[0]].astype(HALF)

    vm = pl.BlockSpec(memory_space=pltpu.VMEM)
    shape = jax.ShapeDtypeStruct((half, 8, channels), HALF)
    return pl.pallas_call(
        body,
        name="vector_sums",
        out_shape=[shape, shape],
        in_specs=[SMEM] + [vm] * 7,
        out_specs=[vm] * 2,
        scratch_shapes=[pltpu.VMEM((shards, 8, lanes), SINGLE)],
        compiler_params=ROOM,
        cost_estimate=cost(0.1),
    )(me, norm_folds, value_fold, channel_folds, pull, skip_fold, expand_fold, out_fold)


def finish_kernel(sizes, wide, small, high, low, gate):
    groups = gate // wide[0].shape[1]

    def body(w0, w1, w2, s0, s1, s2, *outs):
        def total(refs, rows):
            first, second, third = (ref[rows, :].astype(SINGLE) for ref in refs)
            return first + second + third

        width = w0.shape[1]
        value_ref, expand_ref, reduce_ref, state_ref = outs[:4]
        for g in range(groups):
            cols = pl.ds(g * width, width)
            value_ref[:, cols] = total((w0, w1, w2), pl.ds(g * high, high))
            expand_ref[:, cols] = total((w0, w1, w2), pl.ds(groups * high + g * low, low))
        reduce_ref[...] = total((s0, s1, s2), pl.ds(0, high))
        state_ref[...] = total((s0, s1, s2), pl.ds(high, low))
        rows = total((s0, s1, s2), pl.ds(high + low, 8))
        for i, n in enumerate(sizes):
            outs[4 + i][...] = rows[i : i + 1, :n]

    channels = small[0].shape[1]
    vm = pl.BlockSpec(memory_space=pltpu.VMEM)
    shapes = [(high, gate), (low, gate), (high, channels), (low, channels)]
    shapes += [(1, n) for n in sizes]
    return pl.pallas_call(
        body,
        name="finish",
        out_shape=[jax.ShapeDtypeStruct(s, SINGLE) for s in shapes],
        in_specs=[vm] * 6,
        out_specs=[vm] * len(shapes),
        compiler_params=ROOM,
        cost_estimate=cost(1),
    )(*wide, *small)


def pack_kernel(vectors, reduce_shard, state_shard, expand_shard, out_shard):
    channels = state_shard.shape[1]
    high, low = reduce_shard.shape[0], state_shard.shape[0]
    groups, depth = 4, expand_shard.shape[1] // 4

    def body(*refs):
        vector_refs, refs = refs[: len(vectors)], refs[len(vectors) :]
        reduce_ref, state_ref, expand_ref, out_ref, small, expand, out, table = refs
        table[...] = jnp.zeros_like(table)
        for i, ref in enumerate(vector_refs):
            table[i : i + 1, : ref.shape[1]] = ref[...]
        small[:high, :] = reduce_ref[...].astype(HALF)
        small[high : high + low, :] = state_ref[...].astype(HALF)
        small[high + low :, :] = table[...].astype(HALF)
        for g in range(groups):
            cols = pl.ds(g * depth, depth)
            expand[g * low : (g + 1) * low, :] = expand_ref[:, cols].astype(HALF)
        out[...] = out_ref[...].astype(HALF)

    vm = pl.BlockSpec(memory_space=pltpu.VMEM)
    return pl.pallas_call(
        body,
        name="pack",
        out_shape=[
            jax.ShapeDtypeStruct((high + low + len(vectors), channels), HALF),
            jax.ShapeDtypeStruct((groups * low, depth), HALF),
            jax.ShapeDtypeStruct(out_shard.shape, HALF),
        ],
        in_specs=[vm] * (len(vectors) + 4),
        out_specs=[vm] * 3,
        scratch_shapes=[pltpu.VMEM((len(vectors), channels), SINGLE)],
        compiler_params=ROOM,
        cost_estimate=cost(1),
    )(*[v[None] for v in vectors], reduce_shard, state_shard, expand_shard, out_shard)


def weight_grad(left, right, column_block, me, name, micros):
    tokens, height = left.shape
    width = right.shape[1]
    blocks, sub = width // column_block, 256
    half = 1 << (MAIN - 1)
    shard_rows = height // (2 * half)

    def body(me_ref, left_ref, right_ref, send_ref, keep_ref, made):
        mine = me_ref[0]

        def product(c):
            return dot(left_ref[...], right_ref[:, c * sub : (c + 1) * sub], 0, 0)

        def finish(c, value):
            made[:, pl.ds(c * sub, sub)] = value.astype(HALF)

        staged(column_block // sub, product, finish)
        put_halves(mine, made, send_ref, keep_ref)

    shape = jax.ShapeDtypeStruct((half, blocks * shard_rows, column_block), HALF)
    spec = pl.BlockSpec((half, shard_rows, column_block), lambda j: (0, j, 0))
    return pl.pallas_call(
        body,
        name=name,
        out_shape=[shape, shape],
        grid=(blocks,),
        in_specs=[
            SMEM,
            once(tokens, height),
            pl.BlockSpec((tokens, column_block), lambda j: (0, j)),
        ],
        out_specs=[spec, spec],
        scratch_shapes=[pltpu.VMEM((height, column_block), HALF)],
        compiler_params=ROOM,
        cost_estimate=cost(micros),
    )(me, left, right)


def add_low(first, second):
    return (first.astype(SINGLE) + second.astype(SINGLE)).astype(HALF)


def core_exchange(values):
    return exchange(values, low_bits())


def reduce_steps(pairs, split):
    bit_x, bit_y, bit_z, bit_far = (low_bits() + i for i in range(1, MAIN))
    total = [[a.reshape((2, 2, 4) + a.shape[1:]) for a in pair] for pair in pairs]

    def added(x, y, first, last):
        parts, at = [], 0
        for keep, other in total:
            low, high = max(first - at, 0), min(last - at, keep.shape[3])
            if low < high:
                parts.append(add_low(keep[x, y, :, low:high], other[x, y, :, low:high]))
            at += keep.shape[3]
        return parts[0] if len(parts) == 1 else jnp.concatenate(parts, axis=-2)

    rows = sum(keep.shape[1] for keep, _ in pairs)
    every = slice(None)
    if split:
        from_x, from_y = yield [
            exchange(added(1, every, 0, split), bit_x),
            exchange(added(every, 1, split, rows), bit_y),
        ]
        kept_x, kept_y = added(0, every, 0, split), added(every, 0, split, rows)
        last_y, last_x = yield [
            exchange(add_low(kept_x[1], from_x[1]), bit_y),
            exchange(add_low(kept_y[1], from_y[1]), bit_x),
        ]
        first = add_low(add_low(kept_x[0], from_x[0]), last_y)
        second = add_low(add_low(kept_y[0], from_y[0]), last_x)
        total = jnp.concatenate([first, second], axis=1)
    else:
        (other,) = yield [exchange(added(1, every, 0, rows), bit_x)]
        kept = added(0, every, 0, rows)
        (last,) = yield [exchange(add_low(kept[1], other[1]), bit_y)]
        total = add_low(add_low(kept[0], other[0]), last)
    (other,) = yield [exchange(total[2:], bit_z)]
    (last,) = yield [exchange(add_low(total[1], other[1]), bit_far)]
    return total[0], other[0], last


class Run:
    def __init__(self, steps):
        self.steps, self.result = steps, None
        self.pending = next(steps)

    def step(self):
        try:
            self.pending = self.steps.send(self.pending)
        except StopIteration as stop:
            self.pending, self.result = None, stop.value


def tie(values):
    return lax.optimization_barrier(values)


def one_less_exp(y):
    series = jnp.ones_like(y)
    for n in range(9, 1, -1):
        series = 1.0 - series * y * (1.0 / n)
    return jnp.where(y < 0.5, y * series, 1.0 - jnp.exp(-y))


def on_device(
    tokens,
    lengths,
    cotangent,
    norm_gain,
    norm_shift,
    value_weight,
    value_bias,
    reduce_weight,
    reduce_bias,
    decay_rates,
    skip_gain,
    state_weight,
    expand_weight,
    expand_bias,
    out_weight,
    out_bias,
):
    half, single = HALF, SINGLE
    shards = 1 << MAIN
    me = (device_number() >> low_bits()).reshape(1).astype(jnp.int32)
    value_mat = lax.all_gather(value_weight.astype(half), ("dp", "seq"), axis=0, tiled=True)
    vectors = [
        gather_low(v)
        for v in (
            norm_gain,
            norm_shift,
            value_bias,
            reduce_bias,
            decay_rates,
            skip_gain,
            expand_bias,
            out_bias,
        )
    ]
    sizes = [v.shape[0] for v in vectors]
    small, expand_rows, out_rows = pack_kernel(
        vectors,
        gather_low(reduce_weight),
        gather_low(state_weight),
        gather_low(expand_weight),
        gather_low(out_weight),
    )
    channels = state_weight.shape[1]
    width = tokens.shape[-1]
    blocks = value_weight.shape[1] // width
    small_run = Run(gather_steps(small, 0))
    small_run.pending, expand_rows, out_rows = tie((small_run.pending, expand_rows, out_rows))
    small_run.step()
    expand_run = Run(gather_steps(expand_rows, 32))
    small_run.pending, expand_run.pending, out_rows = tie(
        (small_run.pending, expand_run.pending, out_rows)
    )
    small_run.step()
    expand_run.step()
    out_run = Run(gather_steps(out_rows, 48))
    small_run.pending, expand_run.pending, out_run.pending = tie(
        (small_run.pending, expand_run.pending, out_run.pending)
    )
    small_run.step()
    expand_run.step()
    out_run.step()
    small_run.step()
    small_parts = small_run.result

    row_count, block, _ = tokens.shape
    place = lax.axis_index("seq").reshape(1).astype(jnp.int32)
    base = place * block
    positions = base + jnp.arange(block, dtype=jnp.int32)
    ends = jnp.cumsum(lengths, axis=-1).reshape(-1)
    live = ends[-1:]
    token_rows, cot_rows = tokens.reshape(block, width), cotangent.reshape(block, width)
    branch_grad = jnp.where((positions < live)[:, None], cot_rows, jnp.zeros_like(cot_rows))
    out_fold = fold(branch_grad.astype(single))

    vectors = unpack_kernel(me, sizes, small_parts)
    gain, shift, value_add, reduce_add, _, skip, expand_add, out_add = vectors[:8]
    decays, inflow, inflow_pull = vectors[8:]
    expand_run.pending, out_run.pending, me = tie(
        (expand_run.pending, out_run.pending, me)
    )
    expand_run.step()
    out_run.step()

    normed, act, reduce_slope, states, spans, own_map = reduce_kernel(
        (me, ends, base), token_rows, gain, shift, reduce_add, decays, inflow, small_parts
    )
    own_map, me = tie((own_map, me))
    maps = gather_maps(own_map)
    states_low, prior, ssm_low = states_kernel(
        me, place, ends, base, maps, spans, states, act, skip, inflow, decays, small_parts
    )
    expand_run.pending, out_run.pending, ssm_low, me = tie(
        (expand_run.pending, out_run.pending, ssm_low, me)
    )
    expand_run.step()
    expand_run.pending, me = tie((expand_run.pending, me))
    expand_run.step()
    expand_parts = expand_run.result
    out_run.step()

    value_act, gated, gate_slope, out_grads = forward_kernel(
        me, normed, ssm_low, branch_grad, value_add, expand_add, value_mat, expand_parts
    )
    out_run.pending, gated, me = tie((out_run.pending, gated, me))
    out_run.step()
    out_run.pending, me = tie((out_run.pending, me))
    out_run.step()
    out_parts = out_run.result
    out_sum = lax.psum_scatter(out_grads, ("dp", "seq"), scatter_dimension=0, tiled=True)
    value_grad, expand_fold, value_fold, ssm_grad, *halves = gate_kernel(
        me, branch_grad, normed, ssm_low, value_act, gate_slope, out_parts, expand_parts
    )
    halves, me = tie((halves, me))

    others = [core_exchange(halves[0]), core_exchange(halves[2])]
    ssm_grad, totals, back_spans, back_map, skip_fold = state_kernel(
        me, ends, base, ssm_grad, act, decays, small_parts
    )
    state_halves = weight_grad(states_low, ssm_grad, channels, me, "grad_state", 1)
    others, state_halves, back_map, me = tie((others, state_halves, back_map, me))

    wide_run = Run(reduce_steps([(halves[1], others[0]), (halves[3], others[1])], 96))
    back_maps = gather_maps(back_map)
    reduce_grad, grad_tokens, channel_folds, norm_folds = input_kernel(
        me, place, ends, base, back_maps, back_spans, totals, act, prior, ssm_grad, reduce_slope,
        skip, inflow, decays, gain, token_rows, cot_rows, value_grad, value_mat, small_parts
    )
    wide_run.pending, reduce_grad, norm_folds, me = tie(
        (wide_run.pending, reduce_grad, norm_folds, me)
    )

    wide_run.step()
    reduce_halves = weight_grad(normed, reduce_grad, channels, me, "grad_reduce", 2)
    table_halves = sums_kernel(
        me, sizes, norm_folds, value_fold, channel_folds, inflow_pull, skip_fold, expand_fold,
        out_fold
    )
    small_others = [core_exchange(h[0]) for h in (reduce_halves, state_halves, table_halves)]
    small_run = Run(
        reduce_steps(
            [
                (halves[1], other)
                for halves, other in zip((reduce_halves, state_halves, table_halves), small_others)
            ],
            0,
        )
    )
    output = out_kernel(me, live, base, gated, token_rows, out_add, out_parts)
    wide_run.pending, small_run.pending, output, out_sum = tie(
        (wide_run.pending, small_run.pending, output, out_sum)
    )

    wide_run.step()
    small_run.step()
    wide_run.pending, small_run.pending = tie((wide_run.pending, small_run.pending))

    for run in (small_run, wide_run):
        while run.result is None:
            run.step()
    value_sum, expand_sum, reduce_sum, state_sum, *vector_sums = finish_kernel(
        sizes, wide_run.result, small_run.result, width // shards, channels // shards, width * blocks
    )
    vector_sums = [reduce_low(v[0]) for v in vector_sums]
    return (
        output.reshape(tokens.shape),
        grad_tokens.reshape(tokens.shape),
        vector_sums[0],
        vector_sums[1],
        reduce_low(value_sum),
        vector_sums[2],
        reduce_low(reduce_sum),
        vector_sums[3],
        vector_sums[4],
        vector_sums[5],
        reduce_low(state_sum),
        reduce_low(expand_sum),
        vector_sums[6],
        out_sum.astype(single),
        vector_sums[7],
    )


def solution(mesh):
    rows, vector, matrix = P("dp", "seq", None), P(("dp", "seq")), P(("dp", "seq"), None)
    return jax.shard_map(
        on_device,
        mesh=mesh,
        in_specs=(
            rows,
            P("dp", None),
            rows,
            vector,
            vector,
            matrix,
            vector,
            matrix,
            vector,
            vector,
            vector,
            matrix,
            matrix,
            vector,
            matrix,
            vector,
        ),
        out_specs=(
            rows,
            rows,
            vector,
            vector,
            matrix,
            vector,
            matrix,
            vector,
            vector,
            vector,
            matrix,
            matrix,
            vector,
            matrix,
            vector,
        ),
        check_vma=False,
    )
```

```python
import jax
import jax.numpy as jnp
from jax import lax
from jax.experimental import pallas as pl
from jax.experimental.pallas import tpu as pltpu
from jax.sharding import PartitionSpec as P

EPSILON = 1e-05
HALF = jnp.bfloat16
SINGLE = jnp.float32
MAIN = 5
SEGMENTS = 8
MIB = 1 << 20


def log2(n):
    return n.bit_length() - 1


def device_number():
    return lax.axis_index("dp") * lax.axis_size("seq") + lax.axis_index("seq")


def low_bits():
    return log2(lax.axis_size("dp") * lax.axis_size("seq")) - MAIN


def exchange(values, *bits):
    axes = ("dp", "seq")
    base = low_bits()

    def other(i):
        for bit in bits:
            i ^= 1 << (bit[(i >> base) & 1] if isinstance(bit, tuple) else bit)
        return i

    count = lax.axis_size("dp") * lax.axis_size("seq")
    return lax.ppermute(values, axes, [(i, other(i)) for i in range(count)])


def gather_low(values):
    for bit in range(low_bits()):
        other = exchange(values, bit)
        upper = (device_number() >> bit) & 1
        values = jnp.where(
            upper == 1, jnp.concatenate([other, values]), jnp.concatenate([values, other])
        )
    return values


def reduce_low(values):
    for bit in reversed(range(low_bits())):
        upper = (device_number() >> bit) & 1
        halves = values.reshape((2, values.shape[0] // 2) + values.shape[1:])
        mine = lax.dynamic_index_in_dim(halves, upper, 0, False)
        theirs = lax.dynamic_index_in_dim(halves, 1 - upper, 0, False)
        values = mine + exchange(theirs, bit)
    return values


def join(own, other):
    return jnp.concatenate([own, other])


def stage_bits():
    core, bit_x, bit_y, near, far = (low_bits() + i for i in range(MAIN))
    return core, (bit_x, bit_y), (bit_y, bit_x), near, far


def gather_steps(rows, direct=False, early=False):
    core, lead, second, near, far = stage_bits()
    held = rows[None]
    if direct:
        others = yield [(held, far), (held, near), (held, near, far)]
        held = jnp.concatenate([held, *others])
    else:
        (other,) = yield [(held, far)]
        held = join(held, other)
        (other,) = yield [(held, near)]
        held = join(held, other)
    (other,) = yield [(held, second)]
    held = join(held, other)
    if early:
        other, held_there = yield [(held, lead), (held, core)]
        (other_there,) = yield [(other, core)]
    else:
        (other,) = yield [(held, lead)]
        held_there, other_there = yield [(held, core), (other, core)]
    return [held, other, held_there, other_there]


def shard_at(mine, side, lead, k):
    own = 2 + 2 * (mine & 1)
    first, second = (own, 6 - own) if side == 0 else (6 - own, own)
    rel = side + lead * first + ((k >> 2) & 1) * second + ((k >> 1) & 1) * 8 + (k & 1) * 16
    return rel ^ mine


def load_weights(mine, parts, target, pieces, sems):
    def one(k, carry):
        for row, rows, group, held, to_row in pieces:
            for side in range(4):
                shard = shard_at(mine, side >> 1, side & 1, k)
                to = group
                if group is None:
                    per_group = target.shape[1] // held
                    to, shard = shard // per_group, shard % per_group
                at = pl.multiple_of(shard * held + to_row, 16)
                source = parts[side].at[k, pl.ds(row, rows)]
                pltpu.make_async_copy(source, target.at[to, pl.ds(at, rows)], sems.at[to]).start()
        return carry

    lax.fori_loop(0, 8, one, 0)


def await_weights(target, group, sems):
    pltpu.make_async_copy(target.at[group], target.at[group], sems.at[group]).wait()


REDUCE_PIECES = [(0, 32, 0, 32, 0)]
STATE_PIECES = [(32, 16, 0, 16, 0)]
EXPAND_PIECES = [(16 * g, 16, g, 16, 0) for g in range(4)]
OUT_PIECES = [(0, 96, None, 96, 0)]

SMEM = pl.BlockSpec(memory_space=pltpu.SMEM)
FAR = pl.BlockSpec(memory_space=pltpu.HBM)


def cost(micros):
    return pl.CostEstimate(flops=int(micros * 1e9), bytes_accessed=MIB, transcendentals=0)


def room(mib):
    return pltpu.CompilerParams(vmem_limit_bytes=mib * MIB)


def whole(*shape):
    return pl.BlockSpec(shape, lambda *_: (0,) * len(shape))


def dot(left, right, left_dim=1, right_dim=0):
    return lax.dot_general(
        left, right, (((left_dim,), (right_dim,)), ((), ())), preferred_element_type=SINGLE
    )


def gelu_pair(v):
    c, d = 0.7978845608028654, 0.7978845608028654 * 0.044715
    square = v * v
    h = 0.5 + 0.5 * jnp.tanh(v * (c + d * square))
    act = v * h
    return act, h + 2.0 * act * (1.0 - h) * (c + 3.0 * d * square)


def norm_terms(x):
    center = x - jnp.mean(x, axis=-1, keepdims=True)
    inverse = lax.rsqrt(jnp.mean(center * center, axis=-1, keepdims=True) + EPSILON)
    return center * inverse, inverse


def lanes_joined(ref, rows):
    return jnp.concatenate([ref[c, rows, :] for c in range(ref.shape[0])], axis=1)


def powers(decay, count, rows):
    power, out = decay, jnp.ones((rows, decay.shape[1]), SINGLE)
    for bit in range(8):
        out = jnp.where((count >> bit) & 1 == 1, out * power, out)
        power = power * power
    return out


def starts_near(ends_ref, places, reverse):
    far = jnp.full(places.shape, 1 << 20, jnp.int32)
    for i in range(7):
        away = ends_ref[i] - places if reverse else places - ends_ref[i]
        far = jnp.where(away >= (1 if reverse else 0), jnp.minimum(far, away), far)
    return far


def scan_block(ends_ref, first, decay, source_ref, value_ref, reverse):
    columns, block, lanes = value_ref.shape
    span = block // SEGMENTS
    row = lax.broadcasted_iota(jnp.int32, (8, lanes), 0)
    order = 7 - row if reverse else row
    factors = []
    for c in range(columns):
        one = jnp.broadcast_to(decay[:, c * lanes : (c + 1) * lanes], (8, lanes))
        two = one * one
        steps = [jnp.where(order >= d, f, 0.0) for d, f in ((1, one), (2, two), (4, two * two))]
        factors.append(steps + [powers(one, order + 1, 8)])

    def tile(lap, carry):
        k = span // 8 - 1 - lap if reverse else lap
        out = []
        for s in range(SEGMENTS):
            at = pl.multiple_of(s * span + k * 8, 8)
            near = starts_near(ends_ref, first + at + row, reverse) + (0 if reverse else 1)
            for c in range(columns):
                x = source_ref[c, pl.ds(at, 8), :]
                for step, d in enumerate((1, 2, 4)):
                    moved = pltpu.roll(x, 8 - d if reverse else d, 0)
                    x = x + jnp.where(near > d, factors[c][step], 0.0) * moved
                whole_way = jnp.where(near > order + 1, factors[c][3], 0.0)
                x = x + whole_way * carry[s * columns + c]
                value_ref[c, pl.ds(at, 8), :] = x
                edge = x[:1] if reverse else x[7:]
                out.append(jnp.broadcast_to(edge, (8, lanes)))
        return out

    zero = [jnp.zeros((8, lanes), SINGLE)] * (columns * SEGMENTS)
    ends = lax.fori_loop(0, span // 8, tile, zero)
    states, products = [], []
    power = decay
    for _ in range(log2(span)):
        power = power * power
    for s in range(SEGMENTS):
        states.append(
            jnp.concatenate([ends[s * columns + c][:1] for c in range(columns)], axis=1)
        )
        low = first + s * span + (1 if reverse else 0)
        broken = jnp.int32(0)
        for i in range(7):
            inside = (ends_ref[i] >= low) & (ends_ref[i] < low + span)
            broken = jnp.where(inside, 1, broken)
        products.append(jnp.where(broken == 1, 0.0, power))
    return jnp.concatenate(products, axis=0), jnp.concatenate(states, axis=0)


def span_products(ends_ref, first, table, lanes, reverse):
    span, channels = table.shape
    row = lax.broadcasted_iota(jnp.int32, (span, lanes), 0)
    near = starts_near(ends_ref, first + row, reverse)
    kept = near > (span - row if reverse else row)
    return jnp.where(jnp.concatenate([kept] * (channels // lanes), axis=1), table, 0.0)


def span_table(decay, span, reverse):
    row = lax.broadcasted_iota(jnp.int32, (span, decay.shape[1]), 0)
    return powers(decay, span - row if reverse else row + 1, span)


def span_carries(product, state, carry, reverse):
    carries = [None] * SEGMENTS
    for s in range(SEGMENTS)[::-1] if reverse else range(SEGMENTS):
        carries[s] = carry
        carry = product[s : s + 1] * carry + state[s : s + 1]
    return carries, carry


def block_carry(place, maps_ref, reverse):
    count = maps_ref.shape[0]
    carry = jnp.zeros((1, maps_ref.shape[2]), SINGLE)
    for s in range(count)[::-1] if reverse else range(count):
        rel = s ^ place
        inside = s > place if reverse else s < place
        moved = maps_ref[rel, 0:1, :] * carry + maps_ref[rel, 1:2, :]
        carry = jnp.where(inside, moved, carry)
    return carry


def whole_map(product, state, reverse):
    zero = jnp.zeros((1, product.shape[1]), SINGLE)
    _, ending = span_carries(product, state, zero, reverse)
    through = zero + 1.0
    for s in range(SEGMENTS):
        through = through * product[s : s + 1]
    return through, ending


def gather_maps(maps):
    held = maps[None]
    for bit in range(log2(lax.axis_size("seq"))):
        held = join(held, exchange(held, bit))
    return held


def reduce_kernel(me, tokens, gain, shift, bias, inflow, parts):
    block, width = tokens.shape
    channels = bias.shape[1]
    tile = 256
    columns = channels // 128

    def body(me, x_ref, gain_ref, shift_ref, bias_ref, inflow_ref, s0, s1, s2, s3,
             normed_ref, act_ref, slope_ref, state_ref, weight, sems):
        load_weights(me[0], (s0, s1, s2, s3), weight, REDUCE_PIECES, sems)

        def norm(t, carry):
            rows = pl.ds(pl.multiple_of(t * tile, tile), tile)
            n, _ = norm_terms(x_ref[rows, :].astype(SINGLE))
            normed_ref[rows, :] = (n * gain_ref[...] + shift_ref[...]).astype(HALF)
            return carry

        lax.fori_loop(0, block // tile, norm, 0)
        await_weights(weight, 0, sems)

        def reduce(t, carry):
            rows = pl.ds(pl.multiple_of(t * tile, tile), tile)
            act, slope = gelu_pair(dot(normed_ref[rows, :], weight[0]) + bias_ref[...])
            act_ref[rows, :] = act
            slope_ref[rows, :] = slope.astype(HALF)
            flow = act * inflow_ref[...]
            for c in range(columns):
                state_ref[c, rows, :] = flow[:, c * 128 : (c + 1) * 128]
            return carry

        lax.fori_loop(0, block // tile, reduce, 0)

    vm = pl.BlockSpec(memory_space=pltpu.VMEM)
    return pl.pallas_call(
        body,
        name="reduce_forward",
        out_shape=[
            jax.ShapeDtypeStruct((block, width), HALF),
            jax.ShapeDtypeStruct((block, channels), SINGLE),
            jax.ShapeDtypeStruct((block, channels), HALF),
            jax.ShapeDtypeStruct((columns, block, 128), SINGLE),
        ],
        in_specs=[SMEM] + [vm] * 5 + [FAR] * 4,
        out_specs=[vm] * 4,
        scratch_shapes=[
            pltpu.VMEM((1, width, channels), HALF),
            pltpu.SemaphoreType.DMA((1,)),
        ],
        compiler_params=room(60),
        cost_estimate=cost(8),
    )(me, tokens, gain, shift, bias, inflow, *parts)


def scan_kernel(order, ends, base, flow, decay):
    channels = decay.shape[1]

    def body(order, ends_ref, base_ref, flow_ref, decay_ref, state_ref, span_ref, map_ref):
        product, state = scan_block(
            ends_ref, base_ref[0], decay_ref[...], flow_ref, state_ref, False
        )
        span_ref[0], span_ref[1] = product, state
        map_ref[0:1, :], map_ref[1:2, :] = whole_map(product, state, False)

    vm = pl.BlockSpec(memory_space=pltpu.VMEM)
    return pl.pallas_call(
        body,
        name="state_scan",
        out_shape=[
            jax.ShapeDtypeStruct(flow.shape, SINGLE),
            jax.ShapeDtypeStruct((2, SEGMENTS, channels), SINGLE),
            jax.ShapeDtypeStruct((2, channels), SINGLE),
        ],
        in_specs=[SMEM] * 3 + [vm] * 2,
        out_specs=[vm] * 3,
        compiler_params=room(20),
        cost_estimate=cost(12),
    )(order, ends, base, flow, decay)


def staged(count, product, finish):
    ahead = product(0)
    for c in range(count):
        now = ahead
        if c + 1 < count:
            ahead = product(c + 1)
        finish(c, now)


def once(*shape):
    return pl.BlockSpec(shape, lambda *_: (0,) * len(shape), pipeline_mode=pl.Buffered(1))


def states_kernel(me, place, ends, base, maps, spans, states, act, skip, inflow, decay, parts):
    columns, block, lanes = states.shape
    channels = act.shape[1]
    span = block // SEGMENTS

    def body(me, place_ref, ends_ref, base_ref, maps_ref, span_ref, state_ref, act_ref, skip_ref,
             inflow_ref, decay_ref, s0, s1, s2, s3, low_ref, prior_ref, ssm_ref,
             carry_ref, weight, sems):
        load_weights(me[0], (s0, s1, s2, s3), weight, STATE_PIECES, sems)
        entering = block_carry(place_ref[0], maps_ref, False)
        carries, _ = span_carries(span_ref[0], span_ref[1], entering, False)
        table = span_table(decay_ref[...], span, False)
        for s in range(SEGMENTS):
            carry_ref[s] = jnp.broadcast_to(carries[s], (8, channels))

        def one_span(s, done):
            rows = pl.ds(pl.multiple_of(s * span, span), span)
            product = span_products(ends_ref, base_ref[0] + s * span, table, lanes, False)
            state = lanes_joined(state_ref, rows) + product * carry_ref[s][:1]
            low_ref[rows, :] = state.astype(HALF)
            prior_ref[rows, :] = (state - inflow_ref[...] * act_ref[rows, :]).astype(HALF)
            return done

        lax.fori_loop(0, SEGMENTS, one_span, 0)
        await_weights(weight, 0, sems)
        ssm = dot(low_ref[...], weight[0]) + skip_ref[...] * act_ref[...]
        ssm_ref[...] = ssm.astype(HALF)

    vm = pl.BlockSpec(memory_space=pltpu.VMEM)
    return pl.pallas_call(
        body,
        name="states_forward",
        out_shape=[jax.ShapeDtypeStruct((block, channels), HALF)] * 3,
        in_specs=[SMEM] * 4 + [vm] * 7 + [FAR] * 4,
        out_specs=[vm] * 3,
        scratch_shapes=[
            pltpu.VMEM((SEGMENTS, 8, channels), SINGLE),
            pltpu.VMEM((1, channels, channels), HALF), pltpu.SemaphoreType.DMA((1,))],
        compiler_params=room(20),
        cost_estimate=cost(4),
    )(me, place, ends, base, maps, spans, states, act, skip, inflow, decay, *parts)


def forward_kernel(me, normed, ssm, branch_grad, value_bias, expand_bias, value_weight,
                   expand_parts):
    block, width = normed.shape
    channels = ssm.shape[1]
    gate = value_bias.shape[1]
    groups, sub = 4, 256
    depth = gate // groups
    rows = gate >> MAIN

    def body(me, x_ref, ssm_ref, grad_ref, value_bias_ref, expand_bias_ref, value,
             q0, q1, q2, q3, act_ref, gated_ref, slope_ref, send_ref, keep_ref,
             made, expand, expand_sems):
        j = pl.program_id(0)

        @pl.when(j == 0)
        def _():
            load_weights(
                me[0], (q0, q1, q2, q3), expand, EXPAND_PIECES, expand_sems
            )

        for g in range(groups):

            @pl.when(j == g)
            def _():
                await_weights(expand, g, expand_sems)

        for c in range(depth // sub):
            cols = pl.ds(c * sub, sub)
            pre = dot(x_ref[...], value[:, cols]) + value_bias_ref[:, cols]
            act, slope = gelu_pair(pre)
            pre = dot(ssm_ref[...], expand[j, :, cols]) + expand_bias_ref[:, cols]
            act_ref[:, cols] = act.astype(HALF)
            gated_ref[:, cols] = (act * pre).astype(HALF)
            slope_ref[:, cols] = (slope * pre).astype(HALF)
        for c in range(width // sub):
            cols = pl.ds(c * sub, sub)
            made[:, cols] = dot(gated_ref[...], grad_ref[:, cols], 0, 0).astype(HALF)
        rel_z = j ^ (me[0] >> 3)
        place = (rel_z & 1) * 2 + (rel_z >> 1)
        for k in range(0, 16, 4):
            for side, ref in ((0, keep_ref), (1, send_ref)):
                at = pl.multiple_of((shard_at(me[0], side, k >> 3, k & 7) & 7) * rows, 16)
                ref[k + place] = made[pl.ds(at, rows), :]

    wide = pl.BlockSpec((block, depth), lambda j: (0, j))
    bias = pl.BlockSpec((1, depth), lambda j: (0, j))
    return pl.pallas_call(
        body,
        name="gate_forward",
        out_shape=[jax.ShapeDtypeStruct((block, gate), HALF)] * 3
        + [jax.ShapeDtypeStruct((16, rows, width), HALF)] * 2,
        grid=(groups,),
        in_specs=[
            SMEM,
            once(block, width),
            once(block, channels),
            once(block, width),
            bias,
            bias,
            pl.BlockSpec((width, depth), lambda j: (0, j)),
        ]
        + [FAR] * 4,
        out_specs=[wide] * 3 + [once(16, rows, width)] * 2,
        scratch_shapes=[
            pltpu.VMEM((depth, width), HALF),
            pltpu.VMEM((groups, channels, depth), HALF),
            pltpu.SemaphoreType.DMA((groups,)),
        ],
        compiler_params=room(60),
        cost_estimate=cost(16),
    )(me, normed, ssm, branch_grad, value_bias, expand_bias, value_weight,
      *expand_parts)


def fold(values):
    return jnp.sum(values.reshape(values.shape[0] // 8, 8, values.shape[1]), axis=0)


def out_kernel(me, live, base, gated, tokens, bias, parts):
    block, gate = gated.shape
    width = tokens.shape[1]
    tile, sub, groups = block // 2, 256, 4
    depth = gate // groups

    def body(me, live_ref, base_ref, gated_ref, x_ref, bias_ref, p0, p1, p2, p3,
             out_ref, weight, sems):
        t = pl.program_id(0)

        @pl.when(t == 0)
        def _():
            load_weights(me[0], (p0, p1, p2, p3), weight, OUT_PIECES, sems)
            await_weights(weight, 0, sems)

        place = base_ref[0] + t * tile + lax.broadcasted_iota(jnp.int32, (tile, 1), 0)

        def column(c, carry):
            cols = pl.ds(pl.multiple_of(c * sub, sub), sub)
            branch = dot(gated_ref[...], weight[0, :, cols]) + bias_ref[:, cols]
            branch = jnp.where(place < live_ref[0], branch, 0.0)
            out_ref[:, cols] = (x_ref[:, cols].astype(SINGLE) + branch).astype(HALF)
            return carry

        lax.fori_loop(0, width // sub, column, 0)

    return pl.pallas_call(
        body,
        name="out_forward",
        out_shape=jax.ShapeDtypeStruct((block, width), HALF),
        grid=(block // tile,),
        in_specs=[
            SMEM,
            SMEM,
            SMEM,
            pl.BlockSpec((tile, gate), lambda t: (t, 0)),
            pl.BlockSpec((tile, width), lambda t: (t, 0)),
            whole(1, width),
        ]
        + [FAR] * 4,
        out_specs=pl.BlockSpec((tile, width), lambda t: (t, 0)),
        scratch_shapes=[pltpu.VMEM((1, gate, width), HALF), pltpu.SemaphoreType.DMA((1,))],
        compiler_params=room(24),
        cost_estimate=cost(12),
    )(me, live, base, gated, tokens, bias, *parts)


def put_halves(mine, made, send_ref, keep_ref):
    half, rows, _ = send_ref.shape
    for k in range(half):
        for side, ref in ((0, keep_ref), (1, send_ref)):
            at = shard_at(mine, side, k >> 3, k & 7) * rows
            ref[k] = made[pl.ds(pl.multiple_of(at, rows), rows), :]


def gate_kernel(me, branch_grad, normed, ssm, act, slope, parts, expand_parts):
    block, width = branch_grad.shape
    gate, channels = act.shape[1], ssm.shape[1]
    groups, sub = 4, 256
    depth = gate // groups
    half = 1 << (MAIN - 1)
    value_rows, expand_rows = width // (2 * half), channels // (2 * half)

    def body(me, grad_ref, x_ref, ssm_ref, act_ref, slope_ref, p0, p1, p2, p3,
             q0, q1, q2, q3, value_ref, expand_sum, value_sum, state_ref,
             value_send, value_keep, expand_send, expand_keep,
             expand_ref, made, made_low, weight, expand_weight, sems, expand_sems):
        j = pl.program_id(0)

        @pl.when(j == 0)
        def _():
            load_weights(me[0], (p0, p1, p2, p3), weight, OUT_PIECES, sems)
            load_weights(
                me[0], (q0, q1, q2, q3), expand_weight, EXPAND_PIECES, expand_sems
            )
            state_ref[...] = jnp.zeros_like(state_ref)

        for g in range(groups):

            @pl.when(j == g)
            def _():
                await_weights(weight, g, sems)
                await_weights(expand_weight, g, expand_sems)

        for c in range(depth // sub):
            cols = pl.ds(c * sub, sub)
            gated_grad = dot(grad_ref[...], weight[j, cols, :], 1, 1)
            expand = gated_grad * act_ref[:, cols].astype(SINGLE)
            value = gated_grad * slope_ref[:, cols].astype(SINGLE)
            expand_ref[:, cols] = expand.astype(HALF)
            value_ref[:, cols] = value.astype(HALF)
            expand_sum[:, cols] = fold(expand)
            value_sum[:, cols] = fold(value)
        for c in range(depth // sub):
            cols = pl.ds(c * sub, sub)
            made[:, cols] = dot(x_ref[...], value_ref[:, cols], 0, 0).astype(HALF)
            made_low[:, cols] = dot(ssm_ref[...], expand_ref[:, cols], 0, 0).astype(HALF)
        state_ref[...] += dot(expand_ref[...], expand_weight[j], 1, 1)
        put_halves(me[0], made, value_send, value_keep)
        put_halves(me[0], made_low, expand_send, expand_keep)

    wide = pl.BlockSpec((block, depth), lambda j: (0, j))
    sums = pl.BlockSpec((8, depth), lambda j: (0, j))
    halves = [
        (jax.ShapeDtypeStruct((half, groups * rows, depth), HALF),
         pl.BlockSpec((half, rows, depth), lambda j: (0, j, 0)))
        for rows in (value_rows, value_rows, expand_rows, expand_rows)
    ]
    return pl.pallas_call(
        body,
        name="gate_backward",
        out_shape=[jax.ShapeDtypeStruct((block, gate), HALF)]
        + [jax.ShapeDtypeStruct((8, gate), SINGLE)] * 2
        + [jax.ShapeDtypeStruct((block, channels), SINGLE)]
        + [h[0] for h in halves],
        grid=(groups,),
        in_specs=[
            SMEM,
            once(block, width),
            once(block, width),
            once(block, channels),
            wide,
            wide,
        ]
        + [FAR] * 8,
        out_specs=[wide, sums, sums, once(block, channels)] + [h[1] for h in halves],
        scratch_shapes=[
            pltpu.VMEM((block, depth), HALF),
            pltpu.VMEM((width, depth), HALF),
            pltpu.VMEM((channels, depth), HALF),
            pltpu.VMEM((groups, depth, width), HALF),
            pltpu.VMEM((groups, channels, depth), HALF),
            pltpu.SemaphoreType.DMA((groups,)),
            pltpu.SemaphoreType.DMA((groups,)),
        ],
        compiler_params=room(60),
        cost_estimate=cost(20),
    )(me, branch_grad, normed, ssm, act, slope, *parts, *expand_parts)


def state_kernel(me, ends, base, ssm_grad, act, decay, parts):
    block, channels = ssm_grad.shape
    columns, tile = channels // 128, 256

    def body(me, ends_ref, base_ref, grad_ref, act_ref, decay_ref, s0, s1, s2, s3,
             ssm_ref, total_ref, span_ref, map_ref, skip_sum, weight, sems):
        load_weights(me[0], (s0, s1, s2, s3), weight, STATE_PIECES, sems)
        sums = jnp.zeros((8, channels), SINGLE)
        for t in range(block // tile):
            rows = pl.ds(t * tile, tile)
            grad = grad_ref[rows, :]
            ssm_ref[rows, :] = grad.astype(HALF)
            sums += fold(grad * act_ref[rows, :])
        skip_sum[...] = sums
        await_weights(weight, 0, sems)
        for c in range(channels // 256):
            state = dot(ssm_ref[...], weight[0, c * 256 : (c + 1) * 256, :], 1, 1)
            total_ref[2 * c], total_ref[2 * c + 1] = state[:, :128], state[:, 128:]
        product, ending = scan_block(
            ends_ref, base_ref[0], decay_ref[...], total_ref, total_ref, True
        )
        span_ref[0], span_ref[1] = product, ending
        map_ref[0:1, :], map_ref[1:2, :] = whole_map(product, ending, True)

    vm = pl.BlockSpec(memory_space=pltpu.VMEM)
    return pl.pallas_call(
        body,
        name="state_backward",
        out_shape=[
            jax.ShapeDtypeStruct((block, channels), HALF),
            jax.ShapeDtypeStruct((columns, block, 128), SINGLE),
            jax.ShapeDtypeStruct((2, SEGMENTS, channels), SINGLE),
            jax.ShapeDtypeStruct((2, channels), SINGLE),
            jax.ShapeDtypeStruct((8, channels), SINGLE),
        ],
        in_specs=[SMEM] * 3 + [vm] * 3 + [FAR] * 4,
        out_specs=[vm] * 5,
        scratch_shapes=[pltpu.VMEM((1, channels, channels), HALF), pltpu.SemaphoreType.DMA((1,))],
        compiler_params=room(20),
        cost_estimate=cost(6),
    )(me, ends, base, ssm_grad, act, decay, *parts)


def input_kernel(me, place, ends, base, maps, spans, totals, act, prior, ssm_grad, slope, skip,
                 inflow, decay, gain, tokens, cotangent, value_grad, weight,
                 small_parts):
    block, width = tokens.shape
    channels = act.shape[1]
    gate = value_grad.shape[1]
    tile, sub = 256, 256
    columns = channels // 128
    span = block // SEGMENTS

    def body(me, place_ref, ends_ref, base_ref, maps_ref, span_ref, total_ref, act_ref,
             prior_ref, ssm_ref, slope_ref, skip_ref, inflow_ref, decay_ref, gain_ref,
             weight_ref, x_far, cot_far, value_far, s0, s1, s2, s3,
             reduce_ref, out_ref, channel_sums, norm_sums, carry_ref, grads, small,
             x_ref, cot_ref, value_ref, small_sems, sems):
        j = pl.program_id(0)
        value_copy = pltpu.make_async_copy(value_far, value_ref, sems.at[0])
        x_copy = pltpu.make_async_copy(x_far, x_ref, sems.at[1])
        cot_copy = pltpu.make_async_copy(cot_far, cot_ref, sems.at[2])

        @pl.when(j == 0)
        def _():
            load_weights(me[0], (s0, s1, s2, s3), small, REDUCE_PIECES, small_sems)
            value_copy.start()
            x_copy.start()
            cot_copy.start()
            entering = block_carry(place_ref[0], maps_ref, True)
            carries, _ = span_carries(span_ref[0], span_ref[1], entering, True)
            table = span_table(decay_ref[...], span, True)
            for s in range(SEGMENTS):
                carry_ref[s] = jnp.broadcast_to(carries[s], (8, channels))

            def one_span(s, sums):
                rows = pl.ds(pl.multiple_of(s * span, span), span)
                product = span_products(ends_ref, base_ref[0] + s * span, table, 128, True)
                total = lanes_joined(total_ref, rows) + product * carry_ref[s][:1]
                reduced = ssm_ref[rows, :].astype(SINGLE) * skip_ref[...] + inflow_ref[...] * total
                reduced = reduced * slope_ref[rows, :].astype(SINGLE)
                reduce_ref[rows, :] = reduced.astype(HALF)
                terms = (total * prior_ref[rows, :].astype(SINGLE), total * act_ref[rows, :], reduced)
                return [old + fold(new) for old, new in zip(sums, terms)]

            sums = [jnp.zeros((8, channels), SINGLE)] * 3
            sums = lax.fori_loop(0, SEGMENTS, one_span, sums)
            for i in range(3):
                channel_sums[i] = sums[i]
            await_weights(small, 0, small_sems)
            value_copy.wait()

        at = pl.ds(pl.multiple_of(j * sub, sub), sub)
        grads[j] = dot(value_ref[...], weight_ref[...], 1, 1) + dot(
            reduce_ref[...], small[0, at, :], 1, 1
        )

        @pl.when(j == width // sub - 1)
        def _():
            x_copy.wait()
            cot_copy.wait()
            norm_sums[...] = jnp.zeros_like(norm_sums)

            def norm_back(t, carry):
                rows = pl.ds(pl.multiple_of(t * tile, tile), tile)
                grad = lanes_joined(grads, rows)
                n, inverse = norm_terms(x_ref[rows, :].astype(SINGLE))
                norm_sums[0] += fold(grad * n)
                norm_sums[1] += fold(grad)
                h = grad * gain_ref[...]
                mean_h = jnp.mean(h, axis=-1, keepdims=True)
                mean_hn = jnp.mean(h * n, axis=-1, keepdims=True)
                back = inverse * (h - mean_h - n * mean_hn)
                out_ref[rows, :] = (cot_ref[rows, :].astype(SINGLE) + back).astype(HALF)
                return carry

            lax.fori_loop(0, block // tile, norm_back, 0)

    tall = once(columns, block, 128)
    narrow = once(block, channels)
    return pl.pallas_call(
        body,
        name="input_backward",
        out_shape=[
            jax.ShapeDtypeStruct((block, channels), HALF),
            jax.ShapeDtypeStruct((block, width), HALF),
            jax.ShapeDtypeStruct((3, 8, channels), SINGLE),
            jax.ShapeDtypeStruct((2, 8, width), SINGLE),
        ],
        grid=(width // sub,),
        in_specs=[
            SMEM,
            SMEM,
            SMEM,
            SMEM,
            whole(*maps.shape),
            whole(*spans.shape),
            tall,
            narrow,
            narrow,
            narrow,
            narrow,
            whole(1, channels),
            whole(1, channels),
            whole(1, channels),
            whole(1, width),
            pl.BlockSpec((sub, gate), lambda j: (j, 0)),
        ]
        + [FAR] * 7,
        out_specs=[narrow, once(block, width), whole(3, 8, channels), whole(2, 8, width)],
        scratch_shapes=[
            pltpu.VMEM((SEGMENTS, 8, channels), SINGLE),
            pltpu.VMEM((width // sub, block, sub), SINGLE),
            pltpu.VMEM((1, width, channels), HALF),
            pltpu.VMEM((block, width), HALF),
            pltpu.VMEM((block, width), HALF),
            pltpu.VMEM((block, gate), HALF),
            pltpu.SemaphoreType.DMA((1,)),
            pltpu.SemaphoreType.DMA((3,)),
        ],
        compiler_params=room(40),
        cost_estimate=cost(16),
    )(me, place, ends, base, maps, spans, totals, act, prior, ssm_grad, slope, skip, inflow, decay,
      gain, weight, tokens, cotangent, value_grad, *small_parts)


def unpack_kernel(me, sizes, parts):
    shards = 1 << MAIN
    lanes = 128
    rates_at = 4

    def body(me, *refs):
        ins, outs, table = refs[:4], refs[4:-1], refs[-1]
        for side in range(4):
            for k in range(8):
                table[shard_at(me[0], side >> 1, side & 1, k)] = ins[side][k, :, :lanes].astype(SINGLE)
        for i, n in enumerate(sizes):
            for shard in range(shards):
                outs[i][:, shard * n : (shard + 1) * n] = table[shard, i : i + 1, :n]
        rates = outs[rates_at][...]
        decay_ref, inflow_ref, pull_ref = outs[len(sizes) :]
        inflow = jnp.sqrt(one_less_exp(2.0 * rates))
        decay_ref[...] = jnp.exp(-rates)
        inflow_ref[...] = inflow
        pull_ref[...] = jnp.exp(-2.0 * rates) / inflow

    channels = parts[0].shape[2]
    rows = parts[0].shape[1]
    widths = [n * shards for n in sizes] + [sizes[rates_at] * shards] * 3
    return pl.pallas_call(
        body,
        name="unpack",
        out_shape=[jax.ShapeDtypeStruct((1, n), SINGLE) for n in widths],
        grid=(1,),
        in_specs=[SMEM]
        + [pl.BlockSpec((8, 8, channels), lambda i: (0, rows // 8 - 1, 0))] * 4,
        out_specs=[whole(1, n) for n in widths],
        scratch_shapes=[pltpu.VMEM((shards, 8, lanes), SINGLE)],
        compiler_params=room(60),
        cost_estimate=cost(1),
    )(me, *parts)


def sums_kernel(me, sizes, norm_folds, value_fold, channel_folds, pull, skip_fold, expand_fold,
                out_fold):
    shards = 1 << MAIN
    half = shards // 2
    channels = skip_fold.shape[1]
    lanes = 128

    def body(me, norm_ref, value_ref, channel_ref, pull_ref, skip_ref, expand_ref, out_ref,
             send_ref, keep_ref, table):
        def total(values):
            return jnp.sum(values, axis=0, keepdims=True)

        rates = pull_ref[...] * total(channel_ref[1]) - total(channel_ref[0])
        rows = (
            total(norm_ref[0]),
            total(norm_ref[1]),
            total(value_ref[...]),
            total(channel_ref[2]),
            rates,
            total(skip_ref[...]),
            total(expand_ref[...]),
            total(out_ref[...]),
        )
        table[...] = jnp.zeros_like(table)
        for i, (n, row) in enumerate(zip(sizes, rows)):
            for shard in range(shards):
                table[shard, i : i + 1, :n] = row[:, shard * n : (shard + 1) * n]
        send_ref[...] = jnp.zeros_like(send_ref)
        keep_ref[...] = jnp.zeros_like(keep_ref)
        for k in range(half):
            for side, ref in ((0, keep_ref), (1, send_ref)):
                ref[k, :, :lanes] = table[shard_at(me[0], side, k >> 3, k & 7)].astype(HALF)

    vm = pl.BlockSpec(memory_space=pltpu.VMEM)
    shape = jax.ShapeDtypeStruct((half, 8, channels), HALF)
    return pl.pallas_call(
        body,
        name="vector_sums",
        out_shape=[shape, shape],
        in_specs=[SMEM] + [vm] * 7,
        out_specs=[vm] * 2,
        scratch_shapes=[pltpu.VMEM((shards, 8, lanes), SINGLE)],
        compiler_params=room(16),
        cost_estimate=cost(12),
    )(me, norm_folds, value_fold, channel_folds, pull, skip_fold, expand_fold, out_fold)


def finish_kernel(sizes, value, expand, out, small, high, low, gate):
    groups = gate // value[0].shape[1]

    def body(*refs):
        value, expand, out, small = refs[:3], refs[3:6], refs[6:9], refs[9:13]
        outs = refs[13:]

        def total(refs, rows):
            return sum(ref[rows, :].astype(SINGLE) for ref in refs)

        width = value[0].shape[1]
        value_ref, expand_ref, out_ref, reduce_ref, state_ref = outs[:5]
        out_ref[...] = total(out, pl.ds(0, out_ref.shape[0]))
        for g in range(groups):
            cols = pl.ds(g * width, width)
            value_ref[:, cols] = total(value, pl.ds(g * high, high))
            expand_ref[:, cols] = total(expand, pl.ds(g * low, low))
        reduce_ref[...] = total(small, pl.ds(0, high))
        state_ref[...] = total(small, pl.ds(high, low))
        rows = total(small, pl.ds(high + low, 8))
        for i, n in enumerate(sizes):
            outs[5 + i][...] = rows[i : i + 1, :n]

    channels = small[0].shape[1]
    vm = pl.BlockSpec(memory_space=pltpu.VMEM)
    shapes = [(high, gate), (low, gate), out[0].shape, (high, channels), (low, channels)]
    shapes += [(1, n) for n in sizes]
    return pl.pallas_call(
        body,
        name="finish",
        out_shape=[jax.ShapeDtypeStruct(s, SINGLE) for s in shapes],
        in_specs=[vm] * 13,
        out_specs=[vm] * len(shapes),
        compiler_params=room(16),
        cost_estimate=cost(1),
    )(*value, *expand, *out, *small)


def pack_kernel(vectors, reduce_shard, state_shard, expand_shard, out_shard):
    channels = state_shard.shape[1]
    high, low = reduce_shard.shape[0], state_shard.shape[0]
    groups, depth = 4, expand_shard.shape[1] // 4

    def body(*refs):
        vector_refs, refs = refs[: len(vectors)], refs[len(vectors) :]
        reduce_ref, state_ref, expand_ref, out_ref, small, expand, out, table = refs
        table[...] = jnp.zeros_like(table)
        for i, ref in enumerate(vector_refs):
            table[i : i + 1, : ref.shape[1]] = ref[...]
        small[:high, :] = reduce_ref[...].astype(HALF)
        small[high : high + low, :] = state_ref[...].astype(HALF)
        small[high + low :, :] = table[...].astype(HALF)
        for g in range(groups):
            cols = pl.ds(g * depth, depth)
            expand[g * low : (g + 1) * low, :] = expand_ref[:, cols].astype(HALF)
        out[...] = out_ref[...].astype(HALF)

    vm = pl.BlockSpec(memory_space=pltpu.VMEM)
    return pl.pallas_call(
        body,
        name="pack",
        out_shape=[
            jax.ShapeDtypeStruct((high + low + len(vectors), channels), HALF),
            jax.ShapeDtypeStruct((groups * low, depth), HALF),
            jax.ShapeDtypeStruct(out_shard.shape, HALF),
        ],
        in_specs=[vm] * (len(vectors) + 4),
        out_specs=[vm] * 3,
        scratch_shapes=[pltpu.VMEM((len(vectors), channels), SINGLE)],
        compiler_params=room(60),
        cost_estimate=cost(1),
    )(*[v[None] for v in vectors], reduce_shard, state_shard, expand_shard, out_shard)


def weight_grad(left, right, column_block, me, name, micros):
    tokens, height = left.shape
    width = right.shape[1]
    blocks, sub = width // column_block, 256
    half = 1 << (MAIN - 1)
    shard_rows = height // (2 * half)

    def body(me_ref, left_ref, right_ref, send_ref, keep_ref, made):
        mine = me_ref[0]

        def product(c):
            return dot(left_ref[...], right_ref[:, c * sub : (c + 1) * sub], 0, 0)

        def finish(c, value):
            made[:, pl.ds(c * sub, sub)] = value.astype(HALF)

        staged(column_block // sub, product, finish)
        put_halves(mine, made, send_ref, keep_ref)

    shape = jax.ShapeDtypeStruct((half, blocks * shard_rows, column_block), HALF)
    spec = pl.BlockSpec((half, shard_rows, column_block), lambda j: (0, j, 0))
    return pl.pallas_call(
        body,
        name=name,
        out_shape=[shape, shape],
        grid=(blocks,),
        in_specs=[
            SMEM,
            once(tokens, height),
            pl.BlockSpec((tokens, column_block), lambda j: (0, j)),
        ],
        out_specs=[spec, spec],
        scratch_shapes=[pltpu.VMEM((height, column_block), HALF)],
        compiler_params=room(16),
        cost_estimate=cost(micros),
    )(me, left, right)


def add_low(first, second):
    return (first.astype(SINGLE) + second.astype(SINGLE)).astype(HALF)


def core_exchange(values):
    return exchange(values, low_bits())


def reduce_steps(pairs, direct=False):
    _, lead, second, near, far = stage_bits()

    def added(part):
        parts = [add_low(keep[part], other[part]) for keep, other in pairs]
        return parts[0] if len(parts) == 1 else jnp.concatenate(parts, axis=1)

    (other,) = yield [(added(slice(8, 16)), lead)]
    kept = added(slice(0, 8))
    (last,) = yield [(add_low(kept[4:], other[4:]), second)]
    total = add_low(add_low(kept[:4], other[:4]), last)
    if direct:
        others = yield [(total[1], far), (total[2], near), (total[3], near, far)]
        return [total[0], *others]
    (other,) = yield [(total[2:], near)]
    (last,) = yield [(add_low(total[1], other[1]), far)]
    return [total[0], other[0], last]


class Run:
    def __init__(self, steps):
        self.steps, self.pending, self.result = steps, None, None

    def step(self, token=None):
        try:
            wanted = self.steps.send(self.pending)
        except StopIteration as stop:
            self.pending, self.result = None, stop.value
            return token
        arrays, bits = [w[0] for w in wanted], [w[1:] for w in wanted]
        if token is not None:
            arrays, token = tie((arrays, token))
        self.pending = [exchange(array, *bit) for array, bit in zip(arrays, bits)]
        return token


def tie(values):
    return lax.optimization_barrier(values)


def one_less_exp(y):
    series = jnp.ones_like(y)
    for n in range(9, 1, -1):
        series = 1.0 - series * y * (1.0 / n)
    return jnp.where(y < 0.5, y * series, 1.0 - jnp.exp(-y))


def on_device(
    tokens,
    lengths,
    cotangent,
    norm_gain,
    norm_shift,
    value_weight,
    value_bias,
    reduce_weight,
    reduce_bias,
    decay_rates,
    skip_gain,
    state_weight,
    expand_weight,
    expand_bias,
    out_weight,
    out_bias,
):
    half, single = HALF, SINGLE
    shards = 1 << MAIN
    me = (device_number() >> low_bits()).reshape(1).astype(jnp.int32)
    value_mat = lax.all_gather(value_weight.astype(half), ("dp", "seq"), axis=0, tiled=True)
    vectors = [
        gather_low(v)
        for v in (
            norm_gain,
            norm_shift,
            value_bias,
            reduce_bias,
            decay_rates,
            skip_gain,
            expand_bias,
            out_bias,
        )
    ]
    sizes = [v.shape[0] for v in vectors]
    small, expand_rows, out_rows = pack_kernel(
        vectors,
        gather_low(reduce_weight),
        gather_low(state_weight),
        gather_low(expand_weight),
        gather_low(out_weight),
    )
    channels = state_weight.shape[1]
    width = tokens.shape[-1]
    blocks = value_weight.shape[1] // width
    row_count, block, _ = tokens.shape
    place = lax.axis_index("seq").reshape(1).astype(jnp.int32)
    base = place * block
    positions = base + jnp.arange(block, dtype=jnp.int32)
    ends = jnp.cumsum(lengths, axis=-1).reshape(-1)
    live = ends[-1:]
    token_rows, cot_rows = tokens.reshape(block, width), cotangent.reshape(block, width)
    branch_grad = jnp.where((positions < live)[:, None], cot_rows, jnp.zeros_like(cot_rows))
    out_fold = fold(branch_grad.astype(single))

    small_run = Run(gather_steps(small, True))
    small_run.step()
    small_run.pending, expand_rows, out_rows, branch_grad, out_fold, ends = tie(
        (small_run.pending, expand_rows, out_rows, branch_grad, out_fold, ends)
    )
    small_run.step()
    expand_run = Run(gather_steps(expand_rows))
    expand_run.step()
    small_run.pending, expand_run.pending, out_rows = tie(
        (small_run.pending, expand_run.pending, out_rows)
    )
    small_run.step()
    expand_run.step()
    out_run = Run(gather_steps(out_rows, early=True))
    out_run.step()
    small_run.pending, expand_run.pending, out_run.pending = tie(
        (small_run.pending, expand_run.pending, out_run.pending)
    )
    small_run.step()
    small_run.pending, expand_run.pending, out_run.pending = tie(
        (small_run.pending, expand_run.pending, out_run.pending)
    )
    small_run.step()
    small_parts = small_run.result
    me = expand_run.step(me)
    me = out_run.step(me)

    vectors = unpack_kernel(me, sizes, small_parts)
    gain, shift, value_add, reduce_add, _, skip, expand_add, out_add = vectors[:8]
    decays, inflow, inflow_pull = vectors[8:]
    normed, act, reduce_slope, flow = reduce_kernel(
        me, token_rows, gain, shift, reduce_add, inflow, small_parts
    )
    flow, expand_run.pending, me = tie((flow, expand_run.pending, me))
    me = expand_run.step(me)
    states, spans, own_map = scan_kernel(me, ends, base, flow, decays)
    own_map, out_run.pending, me = tie((own_map, out_run.pending, me))
    maps = gather_maps(own_map)
    maps, me = out_run.step((maps, me))
    states_low, prior, ssm_low = states_kernel(
        me, place, ends, base, maps, spans, states, act, skip, inflow, decays, small_parts
    )
    expand_run.pending, out_run.pending, ssm_low, me = tie(
        (expand_run.pending, out_run.pending, ssm_low, me)
    )
    expand_run.step()
    me = out_run.step(me)
    expand_run.pending, me = tie((expand_run.pending, me))
    expand_run.step()
    expand_parts = expand_run.result

    value_act, gated, gate_slope, out_send, out_keep = forward_kernel(
        me, normed, ssm_low, branch_grad, value_add, expand_add, value_mat, expand_parts
    )
    out_run.pending, gated, me = tie((out_run.pending, gated, me))
    out_run.step()
    out_run.pending, out_other, me = tie((out_run.pending, core_exchange(out_send), me))
    out_run.step()
    out_parts = out_run.result

    out_run = Run(reduce_steps([(out_keep, out_other)]))
    me = out_run.step(me)
    value_grad, expand_fold, value_fold, ssm_grad, *halves = gate_kernel(
        me, branch_grad, normed, ssm_low, value_act, gate_slope, out_parts, expand_parts
    )
    out_run.pending, halves, me = tie((out_run.pending, halves, me))

    others = [core_exchange(halves[0]), core_exchange(halves[2])]
    me = out_run.step(me)
    ssm_grad, totals, back_spans, back_map, skip_fold = state_kernel(
        me, ends, base, ssm_grad, act, decays, small_parts
    )
    out_run.pending, others, ssm_grad, back_map, me = tie(
        (out_run.pending, others, ssm_grad, back_map, me)
    )

    back_maps = gather_maps(back_map)
    value_run = Run(reduce_steps([(halves[1], others[0])]))
    expand_run = Run(reduce_steps([(halves[3], others[1])]))
    back_maps, me = value_run.step((back_maps, me))
    me = out_run.step(me)
    reduce_grad, grad_tokens, channel_folds, norm_folds = input_kernel(
        me, place, ends, base, back_maps, back_spans, totals, act, prior, ssm_grad, reduce_slope,
        skip, inflow, decays, gain, token_rows, cot_rows, value_grad, value_mat, small_parts
    )
    value_run.pending, out_run.pending, reduce_grad, norm_folds, me = tie(
        (value_run.pending, out_run.pending, reduce_grad, norm_folds, me)
    )

    me = value_run.step(me)
    me, norm_folds = expand_run.step((me, norm_folds))
    me = out_run.step(me)
    reduce_halves = weight_grad(normed, reduce_grad, channels, me, "grad_reduce", 6)
    table_halves = sums_kernel(
        me, sizes, norm_folds, value_fold, channel_folds, inflow_pull, skip_fold, expand_fold,
        out_fold
    )
    state_halves = weight_grad(states_low, ssm_grad, channels, me, "grad_state", 6)
    small_halves = (reduce_halves, state_halves, table_halves)
    reduce_halves, state_halves, table_halves, me = tie((*small_halves, me))
    small_halves = (reduce_halves, state_halves, table_halves)
    small_others = [core_exchange(h[0]) for h in small_halves]
    output = out_kernel(me, live, base, gated, token_rows, out_add, out_parts)
    value_run.pending, expand_run.pending, out_run.pending, small_others, output = tie(
        (value_run.pending, expand_run.pending, out_run.pending, small_others, output)
    )

    small_run = Run(reduce_steps([(h[1], other) for h, other in zip(small_halves, small_others)], True))
    small_run.step()
    value_run.step()
    expand_run.step()
    out_run.step()
    value_run.pending, expand_run.pending, small_run.pending = tie(
        (value_run.pending, expand_run.pending, small_run.pending)
    )

    small_run.step()
    value_run.step()
    expand_run.step()
    value_run.pending, expand_run.pending, small_run.pending = tie(
        (value_run.pending, expand_run.pending, small_run.pending)
    )
    for run in (value_run, expand_run, small_run, out_run):
        while run.result is None:
            run.step()
    value_sum, expand_sum, out_sum, reduce_sum, state_sum, *vector_sums = finish_kernel(
        sizes, value_run.result, expand_run.result, out_run.result, small_run.result, width // shards, channels // shards, width * blocks
    )
    vector_sums = [reduce_low(v[0]) for v in vector_sums]
    return (
        output.reshape(tokens.shape),
        grad_tokens.reshape(tokens.shape),
        vector_sums[0],
        vector_sums[1],
        reduce_low(value_sum),
        vector_sums[2],
        reduce_low(reduce_sum),
        vector_sums[3],
        vector_sums[4],
        vector_sums[5],
        reduce_low(state_sum),
        reduce_low(expand_sum),
        vector_sums[6],
        reduce_low(out_sum),
        vector_sums[7],
    )


def solution(mesh):
    rows, vector, matrix = P("dp", "seq", None), P(("dp", "seq")), P(("dp", "seq"), None)
    return jax.shard_map(
        on_device,
        mesh=mesh,
        in_specs=(
            rows,
            P("dp", None),
            rows,
            vector,
            vector,
            matrix,
            vector,
            matrix,
            vector,
            vector,
            vector,
            matrix,
            matrix,
            vector,
            matrix,
            vector,
        ),
        out_specs=(
            rows,
            rows,
            vector,
            vector,
            matrix,
            vector,
            matrix,
            vector,
            vector,
            vector,
            matrix,
            matrix,
            vector,
            matrix,
            vector,
        ),
        check_vma=False,
    )
```

```python
import jax
import jax.numpy as jnp
from jax import lax
from jax.experimental import pallas as pl
from jax.experimental.pallas import tpu as pltpu
from jax.sharding import PartitionSpec as P

EPSILON = 1e-05
HALF = jnp.bfloat16
SINGLE = jnp.float32
MAIN = 5
SEGMENTS = 8
MIB = 1 << 20


def log2(n):
    return n.bit_length() - 1


def device_number():
    return lax.axis_index("dp") * lax.axis_size("seq") + lax.axis_index("seq")


def low_bits():
    return log2(lax.axis_size("dp") * lax.axis_size("seq")) - MAIN


def exchange(values, *bits):
    axes = ("dp", "seq")
    base = low_bits()

    def other(i):
        for bit in bits:
            i ^= 1 << (bit[(i >> base) & 1] if isinstance(bit, tuple) else bit)
        return i

    count = lax.axis_size("dp") * lax.axis_size("seq")
    return lax.ppermute(values, axes, [(i, other(i)) for i in range(count)])


def gather_low(values):
    for bit in range(low_bits()):
        other = exchange(values, bit)
        upper = (device_number() >> bit) & 1
        values = jnp.where(
            upper == 1, jnp.concatenate([other, values]), jnp.concatenate([values, other])
        )
    return values


def reduce_low(values):
    for bit in reversed(range(low_bits())):
        upper = (device_number() >> bit) & 1
        halves = values.reshape((2, values.shape[0] // 2) + values.shape[1:])
        mine = lax.dynamic_index_in_dim(halves, upper, 0, False)
        theirs = lax.dynamic_index_in_dim(halves, 1 - upper, 0, False)
        values = mine + exchange(theirs, bit)
    return values


def join(own, other):
    return jnp.concatenate([own, other])


def stage_bits():
    core, bit_x, bit_y, near, far = (low_bits() + i for i in range(MAIN))
    return core, (bit_x, bit_y), (bit_y, bit_x), near, far


def gather_steps(rows, direct=False, early=False):
    core, lead, second, near, far = stage_bits()
    held = rows[None]
    if direct:
        others = yield [(held, far), (held, near), (held, near, far)]
        held = jnp.concatenate([held, *others])
    else:
        (other,) = yield [(held, far)]
        held = join(held, other)
        (other,) = yield [(held, near)]
        held = join(held, other)
    (other,) = yield [(held, second)]
    held = join(held, other)
    if early:
        other, held_there = yield [(held, lead), (held, core)]
        (other_there,) = yield [(other, core)]
    else:
        (other,) = yield [(held, lead)]
        held_there, other_there = yield [(held, core), (other, core)]
    return [held, other, held_there, other_there]


def shard_at(mine, side, lead, k):
    own = 2 + 2 * (mine & 1)
    first, second = (own, 6 - own) if side == 0 else (6 - own, own)
    rel = side + lead * first + ((k >> 2) & 1) * second + ((k >> 1) & 1) * 8 + (k & 1) * 16
    return rel ^ mine


def load_weights(mine, parts, target, pieces, sems):
    def one(k, carry):
        for row, rows, group, held, to_row in pieces:
            for side in range(4):
                shard = shard_at(mine, side >> 1, side & 1, k)
                to = group
                if group is None:
                    per_group = target.shape[1] // held
                    to, shard = shard // per_group, shard % per_group
                at = pl.multiple_of(shard * held + to_row, 16)
                source = parts[side].at[k, pl.ds(row, rows)]
                pltpu.make_async_copy(source, target.at[to, pl.ds(at, rows)], sems.at[to]).start()
        return carry

    lax.fori_loop(0, 8, one, 0)


def await_weights(target, group, sems):
    pltpu.make_async_copy(target.at[group], target.at[group], sems.at[group]).wait()


REDUCE_PIECES = [(0, 32, 0, 32, 0)]
STATE_PIECES = [(32, 16, 0, 16, 0)]
EXPAND_PIECES = [(16 * g, 16, g, 16, 0) for g in range(4)]
OUT_PIECES = [(0, 96, None, 96, 0)]

SMEM = pl.BlockSpec(memory_space=pltpu.SMEM)
FAR = pl.BlockSpec(memory_space=pltpu.HBM)


def cost(micros):
    return pl.CostEstimate(flops=int(micros * 1e9), bytes_accessed=MIB, transcendentals=0)


def room(mib):
    return pltpu.CompilerParams(vmem_limit_bytes=mib * MIB)


def whole(*shape):
    return pl.BlockSpec(shape, lambda *_: (0,) * len(shape))


def dot(left, right, left_dim=1, right_dim=0):
    return lax.dot_general(
        left, right, (((left_dim,), (right_dim,)), ((), ())), preferred_element_type=SINGLE
    )


def gelu_pair(v):
    c, d = 0.7978845608028654, 0.7978845608028654 * 0.044715
    square = v * v
    h = 0.5 + 0.5 * jnp.tanh(v * (c + d * square))
    act = v * h
    return act, h + 2.0 * act * (1.0 - h) * (c + 3.0 * d * square)


def norm_terms(x):
    center = x - jnp.mean(x, axis=-1, keepdims=True)
    inverse = lax.rsqrt(jnp.mean(center * center, axis=-1, keepdims=True) + EPSILON)
    return center * inverse, inverse


def lanes_joined(ref, rows):
    return jnp.concatenate([ref[c, rows, :] for c in range(ref.shape[0])], axis=1)


def powers(decay, count, rows):
    power, out = decay, jnp.ones((rows, decay.shape[1]), SINGLE)
    for bit in range(8):
        out = jnp.where((count >> bit) & 1 == 1, out * power, out)
        power = power * power
    return out


def starts_near(ends_ref, places, reverse):
    far = jnp.full(places.shape, 1 << 20, jnp.int32)
    for i in range(7):
        away = ends_ref[i] - places if reverse else places - ends_ref[i]
        far = jnp.where(away >= (1 if reverse else 0), jnp.minimum(far, away), far)
    return far


def scan_block(ends_ref, first, decay, source_ref, value_ref, reverse):
    columns, block, lanes = value_ref.shape
    span = block // SEGMENTS
    row = lax.broadcasted_iota(jnp.int32, (8, lanes), 0)
    order = 7 - row if reverse else row
    factors = []
    for c in range(columns):
        one = jnp.broadcast_to(decay[:, c * lanes : (c + 1) * lanes], (8, lanes))
        two = one * one
        steps = [jnp.where(order >= d, f, 0.0) for d, f in ((1, one), (2, two), (4, two * two))]
        factors.append(steps + [powers(one, order + 1, 8)])

    def tile(lap, carry):
        k = span // 8 - 1 - lap if reverse else lap
        out = []
        for s in range(SEGMENTS):
            at = pl.multiple_of(s * span + k * 8, 8)
            near = starts_near(ends_ref, first + at + row, reverse) + (0 if reverse else 1)
            for c in range(columns):
                x = source_ref[c, pl.ds(at, 8), :]
                for step, d in enumerate((1, 2, 4)):
                    moved = pltpu.roll(x, 8 - d if reverse else d, 0)
                    x = x + jnp.where(near > d, factors[c][step], 0.0) * moved
                whole_way = jnp.where(near > order + 1, factors[c][3], 0.0)
                x = x + whole_way * carry[s * columns + c]
                value_ref[c, pl.ds(at, 8), :] = x
                edge = x[:1] if reverse else x[7:]
                out.append(jnp.broadcast_to(edge, (8, lanes)))
        return out

    zero = [jnp.zeros((8, lanes), SINGLE)] * (columns * SEGMENTS)
    ends = lax.fori_loop(0, span // 8, tile, zero)
    states, products = [], []
    power = decay
    for _ in range(log2(span)):
        power = power * power
    for s in range(SEGMENTS):
        states.append(
            jnp.concatenate([ends[s * columns + c][:1] for c in range(columns)], axis=1)
        )
        low = first + s * span + (1 if reverse else 0)
        broken = jnp.int32(0)
        for i in range(7):
            inside = (ends_ref[i] >= low) & (ends_ref[i] < low + span)
            broken = jnp.where(inside, 1, broken)
        products.append(jnp.where(broken == 1, 0.0, power))
    return jnp.concatenate(products, axis=0), jnp.concatenate(states, axis=0)


def span_products(ends_ref, first, table, lanes, reverse):
    span, channels = table.shape
    row = lax.broadcasted_iota(jnp.int32, (span, lanes), 0)
    near = starts_near(ends_ref, first + row, reverse)
    kept = near > (span - row if reverse else row)
    return jnp.where(jnp.concatenate([kept] * (channels // lanes), axis=1), table, 0.0)


def span_table(decay, span, reverse):
    row = lax.broadcasted_iota(jnp.int32, (span, decay.shape[1]), 0)
    return powers(decay, span - row if reverse else row + 1, span)


def span_carries(product, state, carry, reverse):
    carries = [None] * SEGMENTS
    for s in range(SEGMENTS)[::-1] if reverse else range(SEGMENTS):
        carries[s] = carry
        carry = product[s : s + 1] * carry + state[s : s + 1]
    return carries, carry


def block_carry(place, maps_ref, reverse):
    count = maps_ref.shape[0]
    carry = jnp.zeros((1, maps_ref.shape[2]), SINGLE)
    for s in range(count)[::-1] if reverse else range(count):
        rel = s ^ place
        inside = s > place if reverse else s < place
        moved = maps_ref[rel, 0:1, :] * carry + maps_ref[rel, 1:2, :]
        carry = jnp.where(inside, moved, carry)
    return carry


def whole_map(product, state, reverse):
    zero = jnp.zeros((1, product.shape[1]), SINGLE)
    _, ending = span_carries(product, state, zero, reverse)
    through = zero + 1.0
    for s in range(SEGMENTS):
        through = through * product[s : s + 1]
    return through, ending


def gather_maps(maps):
    held = maps[None]
    for bit in range(log2(lax.axis_size("seq"))):
        held = join(held, exchange(held, bit))
    return held


def reduce_kernel(me, ends, base, tokens, gain, shift, bias, decay, inflow, parts):
    block, width = tokens.shape
    channels = bias.shape[1]
    tile = 256
    columns = channels // 128

    def body(me, ends_ref, base_ref, x_ref, gain_ref, shift_ref, bias_ref, decay_ref, inflow_ref,
             s0, s1, s2, s3, normed_ref, act_ref, slope_ref, state_ref, span_ref, map_ref,
             weight, sems):
        load_weights(me[0], (s0, s1, s2, s3), weight, REDUCE_PIECES, sems)

        def norm(t, carry):
            rows = pl.ds(pl.multiple_of(t * tile, tile), tile)
            n, _ = norm_terms(x_ref[rows, :].astype(SINGLE))
            normed_ref[rows, :] = (n * gain_ref[...] + shift_ref[...]).astype(HALF)
            return carry

        lax.fori_loop(0, block // tile, norm, 0)
        await_weights(weight, 0, sems)

        def reduce(t, carry):
            rows = pl.ds(pl.multiple_of(t * tile, tile), tile)
            act, slope = gelu_pair(dot(normed_ref[rows, :], weight[0]) + bias_ref[...])
            act_ref[rows, :] = act
            slope_ref[rows, :] = slope.astype(HALF)
            flow = act * inflow_ref[...]
            for c in range(columns):
                state_ref[c, rows, :] = flow[:, c * 128 : (c + 1) * 128]
            return carry

        lax.fori_loop(0, block // tile, reduce, 0)
        product, state = scan_block(
            ends_ref, base_ref[0], decay_ref[...], state_ref, state_ref, False
        )
        span_ref[0], span_ref[1] = product, state
        map_ref[0:1, :], map_ref[1:2, :] = whole_map(product, state, False)

    vm = pl.BlockSpec(memory_space=pltpu.VMEM)
    return pl.pallas_call(
        body,
        name="reduce_forward",
        out_shape=[
            jax.ShapeDtypeStruct((block, width), HALF),
            jax.ShapeDtypeStruct((block, channels), SINGLE),
            jax.ShapeDtypeStruct((block, channels), HALF),
            jax.ShapeDtypeStruct((columns, block, 128), SINGLE),
            jax.ShapeDtypeStruct((2, SEGMENTS, channels), SINGLE),
            jax.ShapeDtypeStruct((2, channels), SINGLE),
        ],
        in_specs=[SMEM] * 3 + [vm] * 6 + [FAR] * 4,
        out_specs=[vm] * 6,
        scratch_shapes=[
            pltpu.VMEM((1, width, channels), HALF),
            pltpu.SemaphoreType.DMA((1,)),
        ],
        compiler_params=room(60),
        cost_estimate=cost(8),
    )(me, ends, base, tokens, gain, shift, bias, decay, inflow, *parts)


def staged(count, product, finish):
    ahead = product(0)
    for c in range(count):
        now = ahead
        if c + 1 < count:
            ahead = product(c + 1)
        finish(c, now)


def once(*shape):
    return pl.BlockSpec(shape, lambda *_: (0,) * len(shape), pipeline_mode=pl.Buffered(1))


def states_kernel(me, place, ends, base, maps, spans, states, act, skip, inflow, decay, parts):
    columns, block, lanes = states.shape
    channels = act.shape[1]
    span = block // SEGMENTS

    def body(me, place_ref, ends_ref, base_ref, maps_ref, span_ref, state_ref, act_ref, skip_ref,
             inflow_ref, decay_ref, s0, s1, s2, s3, low_ref, prior_ref, ssm_ref,
             carry_ref, weight, sems):
        load_weights(me[0], (s0, s1, s2, s3), weight, STATE_PIECES, sems)
        entering = block_carry(place_ref[0], maps_ref, False)
        carries, _ = span_carries(span_ref[0], span_ref[1], entering, False)
        table = span_table(decay_ref[...], span, False)
        for s in range(SEGMENTS):
            carry_ref[s] = jnp.broadcast_to(carries[s], (8, channels))

        def one_span(s, done):
            rows = pl.ds(pl.multiple_of(s * span, span), span)
            product = span_products(ends_ref, base_ref[0] + s * span, table, lanes, False)
            state = lanes_joined(state_ref, rows) + product * carry_ref[s][:1]
            low_ref[rows, :] = state.astype(HALF)
            prior_ref[rows, :] = (state - inflow_ref[...] * act_ref[rows, :]).astype(HALF)
            return done

        lax.fori_loop(0, SEGMENTS, one_span, 0)
        await_weights(weight, 0, sems)
        ssm = dot(low_ref[...], weight[0]) + skip_ref[...] * act_ref[...]
        ssm_ref[...] = ssm.astype(HALF)

    vm = pl.BlockSpec(memory_space=pltpu.VMEM)
    return pl.pallas_call(
        body,
        name="states_forward",
        out_shape=[jax.ShapeDtypeStruct((block, channels), HALF)] * 3,
        in_specs=[SMEM] * 4 + [vm] * 7 + [FAR] * 4,
        out_specs=[vm] * 3,
        scratch_shapes=[
            pltpu.VMEM((SEGMENTS, 8, channels), SINGLE),
            pltpu.VMEM((1, channels, channels), HALF), pltpu.SemaphoreType.DMA((1,))],
        compiler_params=room(20),
        cost_estimate=cost(4),
    )(me, place, ends, base, maps, spans, states, act, skip, inflow, decay, *parts)


def forward_kernel(me, normed, ssm, branch_grad, value_bias, expand_bias, value_weight,
                   expand_parts):
    block, width = normed.shape
    channels = ssm.shape[1]
    gate = value_bias.shape[1]
    groups, sub = 4, 256
    depth = gate // groups
    rows = gate >> MAIN

    def body(me, x_ref, ssm_ref, grad_ref, value_bias_ref, expand_bias_ref, value,
             q0, q1, q2, q3, act_ref, gated_ref, slope_ref, send_ref, keep_ref,
             made, expand, expand_sems):
        j = pl.program_id(0)

        @pl.when(j == 0)
        def _():
            load_weights(
                me[0], (q0, q1, q2, q3), expand, EXPAND_PIECES, expand_sems
            )

        for g in range(groups):

            @pl.when(j == g)
            def _():
                await_weights(expand, g, expand_sems)

        for c in range(depth // sub):
            cols = pl.ds(c * sub, sub)
            pre = dot(x_ref[...], value[:, cols]) + value_bias_ref[:, cols]
            act, slope = gelu_pair(pre)
            pre = dot(ssm_ref[...], expand[j, :, cols]) + expand_bias_ref[:, cols]
            act_ref[:, cols] = act.astype(HALF)
            gated_ref[:, cols] = (act * pre).astype(HALF)
            slope_ref[:, cols] = (slope * pre).astype(HALF)
        for c in range(width // sub):
            cols = pl.ds(c * sub, sub)
            made[:, cols] = dot(gated_ref[...], grad_ref[:, cols], 0, 0).astype(HALF)
        rel_z = j ^ (me[0] >> 3)
        place = (rel_z & 1) * 2 + (rel_z >> 1)
        for k in range(0, 16, 4):
            for side, ref in ((0, keep_ref), (1, send_ref)):
                at = pl.multiple_of((shard_at(me[0], side, k >> 3, k & 7) & 7) * rows, 16)
                ref[k + place] = made[pl.ds(at, rows), :]

    wide = pl.BlockSpec((block, depth), lambda j: (0, j))
    bias = pl.BlockSpec((1, depth), lambda j: (0, j))
    return pl.pallas_call(
        body,
        name="gate_forward",
        out_shape=[jax.ShapeDtypeStruct((block, gate), HALF)] * 3
        + [jax.ShapeDtypeStruct((16, rows, width), HALF)] * 2,
        grid=(groups,),
        in_specs=[
            SMEM,
            once(block, width),
            once(block, channels),
            once(block, width),
            bias,
            bias,
            pl.BlockSpec((width, depth), lambda j: (0, j)),
        ]
        + [FAR] * 4,
        out_specs=[wide] * 3 + [once(16, rows, width)] * 2,
        scratch_shapes=[
            pltpu.VMEM((depth, width), HALF),
            pltpu.VMEM((groups, channels, depth), HALF),
            pltpu.SemaphoreType.DMA((groups,)),
        ],
        compiler_params=room(60),
        cost_estimate=cost(16),
    )(me, normed, ssm, branch_grad, value_bias, expand_bias, value_weight,
      *expand_parts)


def fold(values):
    return jnp.sum(values.reshape(values.shape[0] // 8, 8, values.shape[1]), axis=0)


def out_kernel(me, live, base, gated, tokens, bias, parts):
    block, gate = gated.shape
    width = tokens.shape[1]
    tile, sub, groups = block // 2, 256, 4
    depth = gate // groups

    def body(me, live_ref, base_ref, gated_ref, x_ref, bias_ref, p0, p1, p2, p3,
             out_ref, weight, sems):
        t = pl.program_id(0)

        @pl.when(t == 0)
        def _():
            load_weights(me[0], (p0, p1, p2, p3), weight, OUT_PIECES, sems)
            await_weights(weight, 0, sems)

        place = base_ref[0] + t * tile + lax.broadcasted_iota(jnp.int32, (tile, 1), 0)

        def column(c, carry):
            cols = pl.ds(pl.multiple_of(c * sub, sub), sub)
            branch = dot(gated_ref[...], weight[0, :, cols]) + bias_ref[:, cols]
            branch = jnp.where(place < live_ref[0], branch, 0.0)
            out_ref[:, cols] = (x_ref[:, cols].astype(SINGLE) + branch).astype(HALF)
            return carry

        lax.fori_loop(0, width // sub, column, 0)

    return pl.pallas_call(
        body,
        name="out_forward",
        out_shape=jax.ShapeDtypeStruct((block, width), HALF),
        grid=(block // tile,),
        in_specs=[
            SMEM,
            SMEM,
            SMEM,
            pl.BlockSpec((tile, gate), lambda t: (t, 0)),
            pl.BlockSpec((tile, width), lambda t: (t, 0)),
            whole(1, width),
        ]
        + [FAR] * 4,
        out_specs=pl.BlockSpec((tile, width), lambda t: (t, 0)),
        scratch_shapes=[pltpu.VMEM((1, gate, width), HALF), pltpu.SemaphoreType.DMA((1,))],
        compiler_params=room(24),
        cost_estimate=cost(12),
    )(me, live, base, gated, tokens, bias, *parts)


def put_halves(mine, made, send_ref, keep_ref):
    half, rows, _ = send_ref.shape
    for k in range(half):
        for side, ref in ((0, keep_ref), (1, send_ref)):
            at = shard_at(mine, side, k >> 3, k & 7) * rows
            ref[k] = made[pl.ds(pl.multiple_of(at, rows), rows), :]


def gate_kernel(me, branch_grad, normed, ssm, act, slope, parts, expand_parts):
    block, width = branch_grad.shape
    gate, channels = act.shape[1], ssm.shape[1]
    groups, sub = 4, 256
    depth = gate // groups
    half = 1 << (MAIN - 1)
    value_rows, expand_rows = width // (2 * half), channels // (2 * half)

    def body(me, grad_ref, x_ref, ssm_ref, act_ref, slope_ref, p0, p1, p2, p3,
             q0, q1, q2, q3, value_ref, expand_sum, value_sum, state_ref,
             value_send, value_keep, expand_send, expand_keep,
             expand_ref, made, made_low, weight, expand_weight, sems, expand_sems):
        j = pl.program_id(0)

        @pl.when(j == 0)
        def _():
            load_weights(me[0], (p0, p1, p2, p3), weight, OUT_PIECES, sems)
            load_weights(
                me[0], (q0, q1, q2, q3), expand_weight, EXPAND_PIECES, expand_sems
            )
            state_ref[...] = jnp.zeros_like(state_ref)

        for g in range(groups):

            @pl.when(j == g)
            def _():
                await_weights(weight, g, sems)
                await_weights(expand_weight, g, expand_sems)

        for c in range(depth // sub):
            cols = pl.ds(c * sub, sub)
            gated_grad = dot(grad_ref[...], weight[j, cols, :], 1, 1)
            expand = gated_grad * act_ref[:, cols].astype(SINGLE)
            value = gated_grad * slope_ref[:, cols].astype(SINGLE)
            expand_ref[:, cols] = expand.astype(HALF)
            value_ref[:, cols] = value.astype(HALF)
            expand_sum[:, cols] = fold(expand)
            value_sum[:, cols] = fold(value)
        for c in range(depth // sub):
            cols = pl.ds(c * sub, sub)
            made[:, cols] = dot(x_ref[...], value_ref[:, cols], 0, 0).astype(HALF)
            made_low[:, cols] = dot(ssm_ref[...], expand_ref[:, cols], 0, 0).astype(HALF)
        state_ref[...] += dot(expand_ref[...], expand_weight[j], 1, 1)
        put_halves(me[0], made, value_send, value_keep)
        put_halves(me[0], made_low, expand_send, expand_keep)

    wide = pl.BlockSpec((block, depth), lambda j: (0, j))
    sums = pl.BlockSpec((8, depth), lambda j: (0, j))
    halves = [
        (jax.ShapeDtypeStruct((half, groups * rows, depth), HALF),
         pl.BlockSpec((half, rows, depth), lambda j: (0, j, 0)))
        for rows in (value_rows, value_rows, expand_rows, expand_rows)
    ]
    return pl.pallas_call(
        body,
        name="gate_backward",
        out_shape=[jax.ShapeDtypeStruct((block, gate), HALF)]
        + [jax.ShapeDtypeStruct((8, gate), SINGLE)] * 2
        + [jax.ShapeDtypeStruct((block, channels), SINGLE)]
        + [h[0] for h in halves],
        grid=(groups,),
        in_specs=[
            SMEM,
            once(block, width),
            once(block, width),
            once(block, channels),
            wide,
            wide,
        ]
        + [FAR] * 8,
        out_specs=[wide, sums, sums, once(block, channels)] + [h[1] for h in halves],
        scratch_shapes=[
            pltpu.VMEM((block, depth), HALF),
            pltpu.VMEM((width, depth), HALF),
            pltpu.VMEM((channels, depth), HALF),
            pltpu.VMEM((groups, depth, width), HALF),
            pltpu.VMEM((groups, channels, depth), HALF),
            pltpu.SemaphoreType.DMA((groups,)),
            pltpu.SemaphoreType.DMA((groups,)),
        ],
        compiler_params=room(60),
        cost_estimate=cost(20),
    )(me, branch_grad, normed, ssm, act, slope, *parts, *expand_parts)


def state_kernel(me, ends, base, ssm_grad, act, decay, parts):
    block, channels = ssm_grad.shape
    columns, tile = channels // 128, 256

    def body(me, ends_ref, base_ref, grad_ref, act_ref, decay_ref, s0, s1, s2, s3,
             ssm_ref, total_ref, span_ref, map_ref, skip_sum, weight, sems):
        load_weights(me[0], (s0, s1, s2, s3), weight, STATE_PIECES, sems)
        sums = jnp.zeros((8, channels), SINGLE)
        for t in range(block // tile):
            rows = pl.ds(t * tile, tile)
            grad = grad_ref[rows, :]
            ssm_ref[rows, :] = grad.astype(HALF)
            sums += fold(grad * act_ref[rows, :])
        skip_sum[...] = sums
        await_weights(weight, 0, sems)
        for c in range(channels // 256):
            state = dot(ssm_ref[...], weight[0, c * 256 : (c + 1) * 256, :], 1, 1)
            total_ref[2 * c], total_ref[2 * c + 1] = state[:, :128], state[:, 128:]
        product, ending = scan_block(
            ends_ref, base_ref[0], decay_ref[...], total_ref, total_ref, True
        )
        span_ref[0], span_ref[1] = product, ending
        map_ref[0:1, :], map_ref[1:2, :] = whole_map(product, ending, True)

    vm = pl.BlockSpec(memory_space=pltpu.VMEM)
    return pl.pallas_call(
        body,
        name="state_backward",
        out_shape=[
            jax.ShapeDtypeStruct((block, channels), HALF),
            jax.ShapeDtypeStruct((columns, block, 128), SINGLE),
            jax.ShapeDtypeStruct((2, SEGMENTS, channels), SINGLE),
            jax.ShapeDtypeStruct((2, channels), SINGLE),
            jax.ShapeDtypeStruct((8, channels), SINGLE),
        ],
        in_specs=[SMEM] * 3 + [vm] * 3 + [FAR] * 4,
        out_specs=[vm] * 5,
        scratch_shapes=[pltpu.VMEM((1, channels, channels), HALF), pltpu.SemaphoreType.DMA((1,))],
        compiler_params=room(20),
        cost_estimate=cost(6),
    )(me, ends, base, ssm_grad, act, decay, *parts)


def input_kernel(me, place, ends, base, maps, spans, totals, act, prior, ssm_grad, slope, skip,
                 inflow, decay, gain, tokens, cotangent, value_grad, weight,
                 small_parts):
    block, width = tokens.shape
    channels = act.shape[1]
    gate = value_grad.shape[1]
    tile, sub = 256, 256
    columns = channels // 128
    span = block // SEGMENTS

    def body(me, place_ref, ends_ref, base_ref, maps_ref, span_ref, total_ref, act_ref,
             prior_ref, ssm_ref, slope_ref, skip_ref, inflow_ref, decay_ref, gain_ref,
             weight_ref, x_far, cot_far, value_far, s0, s1, s2, s3,
             reduce_ref, out_ref, channel_sums, norm_sums, carry_ref, grads, small,
             x_ref, cot_ref, value_ref, small_sems, sems):
        j = pl.program_id(0)
        value_copy = pltpu.make_async_copy(value_far, value_ref, sems.at[0])
        x_copy = pltpu.make_async_copy(x_far, x_ref, sems.at[1])
        cot_copy = pltpu.make_async_copy(cot_far, cot_ref, sems.at[2])

        @pl.when(j == 0)
        def _():
            load_weights(me[0], (s0, s1, s2, s3), small, REDUCE_PIECES, small_sems)
            value_copy.start()
            x_copy.start()
            cot_copy.start()
            entering = block_carry(place_ref[0], maps_ref, True)
            carries, _ = span_carries(span_ref[0], span_ref[1], entering, True)
            table = span_table(decay_ref[...], span, True)
            for s in range(SEGMENTS):
                carry_ref[s] = jnp.broadcast_to(carries[s], (8, channels))

            def one_span(s, sums):
                rows = pl.ds(pl.multiple_of(s * span, span), span)
                product = span_products(ends_ref, base_ref[0] + s * span, table, 128, True)
                total = lanes_joined(total_ref, rows) + product * carry_ref[s][:1]
                reduced = ssm_ref[rows, :].astype(SINGLE) * skip_ref[...] + inflow_ref[...] * total
                reduced = reduced * slope_ref[rows, :].astype(SINGLE)
                reduce_ref[rows, :] = reduced.astype(HALF)
                terms = (total * prior_ref[rows, :].astype(SINGLE), total * act_ref[rows, :], reduced)
                return [old + fold(new) for old, new in zip(sums, terms)]

            sums = [jnp.zeros((8, channels), SINGLE)] * 3
            sums = lax.fori_loop(0, SEGMENTS, one_span, sums)
            for i in range(3):
                channel_sums[i] = sums[i]
            await_weights(small, 0, small_sems)
            value_copy.wait()

        at = pl.ds(pl.multiple_of(j * sub, sub), sub)
        grads[j] = dot(value_ref[...], weight_ref[...], 1, 1) + dot(
            reduce_ref[...], small[0, at, :], 1, 1
        )

        @pl.when(j == width // sub - 1)
        def _():
            x_copy.wait()
            cot_copy.wait()
            norm_sums[...] = jnp.zeros_like(norm_sums)

            def norm_back(t, carry):
                rows = pl.ds(pl.multiple_of(t * tile, tile), tile)
                grad = lanes_joined(grads, rows)
                n, inverse = norm_terms(x_ref[rows, :].astype(SINGLE))
                norm_sums[0] += fold(grad * n)
                norm_sums[1] += fold(grad)
                h = grad * gain_ref[...]
                mean_h = jnp.mean(h, axis=-1, keepdims=True)
                mean_hn = jnp.mean(h * n, axis=-1, keepdims=True)
                back = inverse * (h - mean_h - n * mean_hn)
                out_ref[rows, :] = (cot_ref[rows, :].astype(SINGLE) + back).astype(HALF)
                return carry

            lax.fori_loop(0, block // tile, norm_back, 0)

    tall = once(columns, block, 128)
    narrow = once(block, channels)
    return pl.pallas_call(
        body,
        name="input_backward",
        out_shape=[
            jax.ShapeDtypeStruct((block, channels), HALF),
            jax.ShapeDtypeStruct((block, width), HALF),
            jax.ShapeDtypeStruct((3, 8, channels), SINGLE),
            jax.ShapeDtypeStruct((2, 8, width), SINGLE),
        ],
        grid=(width // sub,),
        in_specs=[
            SMEM,
            SMEM,
            SMEM,
            SMEM,
            whole(*maps.shape),
            whole(*spans.shape),
            tall,
            narrow,
            narrow,
            narrow,
            narrow,
            whole(1, channels),
            whole(1, channels),
            whole(1, channels),
            whole(1, width),
            pl.BlockSpec((sub, gate), lambda j: (j, 0)),
        ]
        + [FAR] * 7,
        out_specs=[narrow, once(block, width), whole(3, 8, channels), whole(2, 8, width)],
        scratch_shapes=[
            pltpu.VMEM((SEGMENTS, 8, channels), SINGLE),
            pltpu.VMEM((width // sub, block, sub), SINGLE),
            pltpu.VMEM((1, width, channels), HALF),
            pltpu.VMEM((block, width), HALF),
            pltpu.VMEM((block, width), HALF),
            pltpu.VMEM((block, gate), HALF),
            pltpu.SemaphoreType.DMA((1,)),
            pltpu.SemaphoreType.DMA((3,)),
        ],
        compiler_params=room(40),
        cost_estimate=cost(16),
    )(me, place, ends, base, maps, spans, totals, act, prior, ssm_grad, slope, skip, inflow, decay,
      gain, weight, tokens, cotangent, value_grad, *small_parts)


def unpack_kernel(me, sizes, parts):
    shards = 1 << MAIN
    lanes = 128
    rates_at = 4

    def body(me, *refs):
        ins, outs, table = refs[:4], refs[4:-1], refs[-1]
        for side in range(4):
            for k in range(8):
                table[shard_at(me[0], side >> 1, side & 1, k)] = ins[side][k, :, :lanes].astype(SINGLE)
        for i, n in enumerate(sizes):
            for shard in range(shards):
                outs[i][:, shard * n : (shard + 1) * n] = table[shard, i : i + 1, :n]
        rates = outs[rates_at][...]
        decay_ref, inflow_ref, pull_ref = outs[len(sizes) :]
        inflow = jnp.sqrt(one_less_exp(2.0 * rates))
        decay_ref[...] = jnp.exp(-rates)
        inflow_ref[...] = inflow
        pull_ref[...] = jnp.exp(-2.0 * rates) / inflow

    channels = parts[0].shape[2]
    rows = parts[0].shape[1]
    widths = [n * shards for n in sizes] + [sizes[rates_at] * shards] * 3
    return pl.pallas_call(
        body,
        name="unpack",
        out_shape=[jax.ShapeDtypeStruct((1, n), SINGLE) for n in widths],
        grid=(1,),
        in_specs=[SMEM]
        + [pl.BlockSpec((8, 8, channels), lambda i: (0, rows // 8 - 1, 0))] * 4,
        out_specs=[whole(1, n) for n in widths],
        scratch_shapes=[pltpu.VMEM((shards, 8, lanes), SINGLE)],
        compiler_params=room(60),
        cost_estimate=cost(1),
    )(me, *parts)


def sums_kernel(me, sizes, norm_folds, value_fold, channel_folds, pull, skip_fold, expand_fold,
                out_fold):
    shards = 1 << MAIN
    half = shards // 2
    channels = skip_fold.shape[1]
    lanes = 128

    def body(me, norm_ref, value_ref, channel_ref, pull_ref, skip_ref, expand_ref, out_ref,
             send_ref, keep_ref, table):
        def total(values):
            return jnp.sum(values, axis=0, keepdims=True)

        rates = pull_ref[...] * total(channel_ref[1]) - total(channel_ref[0])
        rows = (
            total(norm_ref[0]),
            total(norm_ref[1]),
            total(value_ref[...]),
            total(channel_ref[2]),
            rates,
            total(skip_ref[...]),
            total(expand_ref[...]),
            total(out_ref[...]),
        )
        table[...] = jnp.zeros_like(table)
        for i, (n, row) in enumerate(zip(sizes, rows)):
            for shard in range(shards):
                table[shard, i : i + 1, :n] = row[:, shard * n : (shard + 1) * n]
        send_ref[...] = jnp.zeros_like(send_ref)
        keep_ref[...] = jnp.zeros_like(keep_ref)
        for k in range(half):
            for side, ref in ((0, keep_ref), (1, send_ref)):
                ref[k, :, :lanes] = table[shard_at(me[0], side, k >> 3, k & 7)].astype(HALF)

    vm = pl.BlockSpec(memory_space=pltpu.VMEM)
    shape = jax.ShapeDtypeStruct((half, 8, channels), HALF)
    return pl.pallas_call(
        body,
        name="vector_sums",
        out_shape=[shape, shape],
        in_specs=[SMEM] + [vm] * 7,
        out_specs=[vm] * 2,
        scratch_shapes=[pltpu.VMEM((shards, 8, lanes), SINGLE)],
        compiler_params=room(16),
        cost_estimate=cost(12),
    )(me, norm_folds, value_fold, channel_folds, pull, skip_fold, expand_fold, out_fold)


def finish_kernel(sizes, value, expand, out, small, high, low, gate):
    groups = gate // value[0].shape[1]

    def body(*refs):
        value, expand, out, small = refs[:3], refs[3:6], refs[6:9], refs[9:13]
        outs = refs[13:]

        def total(refs, rows):
            return sum(ref[rows, :].astype(SINGLE) for ref in refs)

        width = value[0].shape[1]
        value_ref, expand_ref, out_ref, reduce_ref, state_ref = outs[:5]
        out_ref[...] = total(out, pl.ds(0, out_ref.shape[0]))
        for g in range(groups):
            cols = pl.ds(g * width, width)
            value_ref[:, cols] = total(value, pl.ds(g * high, high))
            expand_ref[:, cols] = total(expand, pl.ds(g * low, low))
        reduce_ref[...] = total(small, pl.ds(0, high))
        state_ref[...] = total(small, pl.ds(high, low))
        rows = total(small, pl.ds(high + low, 8))
        for i, n in enumerate(sizes):
            outs[5 + i][...] = rows[i : i + 1, :n]

    channels = small[0].shape[1]
    vm = pl.BlockSpec(memory_space=pltpu.VMEM)
    shapes = [(high, gate), (low, gate), out[0].shape, (high, channels), (low, channels)]
    shapes += [(1, n) for n in sizes]
    return pl.pallas_call(
        body,
        name="finish",
        out_shape=[jax.ShapeDtypeStruct(s, SINGLE) for s in shapes],
        in_specs=[vm] * 13,
        out_specs=[vm] * len(shapes),
        compiler_params=room(16),
        cost_estimate=cost(1),
    )(*value, *expand, *out, *small)


def pack_kernel(vectors, reduce_shard, state_shard, expand_shard, out_shard):
    channels = state_shard.shape[1]
    high, low = reduce_shard.shape[0], state_shard.shape[0]
    groups, depth = 4, expand_shard.shape[1] // 4

    def body(*refs):
        vector_refs, refs = refs[: len(vectors)], refs[len(vectors) :]
        reduce_ref, state_ref, expand_ref, out_ref, small, expand, out, table = refs
        table[...] = jnp.zeros_like(table)
        for i, ref in enumerate(vector_refs):
            table[i : i + 1, : ref.shape[1]] = ref[...]
        small[:high, :] = reduce_ref[...].astype(HALF)
        small[high : high + low, :] = state_ref[...].astype(HALF)
        small[high + low :, :] = table[...].astype(HALF)
        for g in range(groups):
            cols = pl.ds(g * depth, depth)
            expand[g * low : (g + 1) * low, :] = expand_ref[:, cols].astype(HALF)
        out[...] = out_ref[...].astype(HALF)

    vm = pl.BlockSpec(memory_space=pltpu.VMEM)
    return pl.pallas_call(
        body,
        name="pack",
        out_shape=[
            jax.ShapeDtypeStruct((high + low + len(vectors), channels), HALF),
            jax.ShapeDtypeStruct((groups * low, depth), HALF),
            jax.ShapeDtypeStruct(out_shard.shape, HALF),
        ],
        in_specs=[vm] * (len(vectors) + 4),
        out_specs=[vm] * 3,
        scratch_shapes=[pltpu.VMEM((len(vectors), channels), SINGLE)],
        compiler_params=room(60),
        cost_estimate=cost(1),
    )(*[v[None] for v in vectors], reduce_shard, state_shard, expand_shard, out_shard)


def weight_grad(left, right, column_block, me, name, micros):
    tokens, height = left.shape
    width = right.shape[1]
    blocks, sub = width // column_block, 256
    half = 1 << (MAIN - 1)
    shard_rows = height // (2 * half)

    def body(me_ref, left_ref, right_ref, send_ref, keep_ref, made):
        mine = me_ref[0]

        def product(c):
            return dot(left_ref[...], right_ref[:, c * sub : (c + 1) * sub], 0, 0)

        def finish(c, value):
            made[:, pl.ds(c * sub, sub)] = value.astype(HALF)

        staged(column_block // sub, product, finish)
        put_halves(mine, made, send_ref, keep_ref)

    shape = jax.ShapeDtypeStruct((half, blocks * shard_rows, column_block), HALF)
    spec = pl.BlockSpec((half, shard_rows, column_block), lambda j: (0, j, 0))
    return pl.pallas_call(
        body,
        name=name,
        out_shape=[shape, shape],
        grid=(blocks,),
        in_specs=[
            SMEM,
            once(tokens, height),
            pl.BlockSpec((tokens, column_block), lambda j: (0, j)),
        ],
        out_specs=[spec, spec],
        scratch_shapes=[pltpu.VMEM((height, column_block), HALF)],
        compiler_params=room(16),
        cost_estimate=cost(micros),
    )(me, left, right)


def add_low(first, second):
    return (first.astype(SINGLE) + second.astype(SINGLE)).astype(HALF)


def core_exchange(values):
    return exchange(values, low_bits())


def reduce_steps(pairs, direct=False):
    _, lead, second, near, far = stage_bits()

    def added(part):
        parts = [add_low(keep[part], other[part]) for keep, other in pairs]
        return parts[0] if len(parts) == 1 else jnp.concatenate(parts, axis=1)

    (other,) = yield [(added(slice(8, 16)), lead)]
    kept = added(slice(0, 8))
    (last,) = yield [(add_low(kept[4:], other[4:]), second)]
    total = add_low(add_low(kept[:4], other[:4]), last)
    if direct:
        others = yield [(total[1], far), (total[2], near), (total[3], near, far)]
        return [total[0], *others]
    (other,) = yield [(total[2:], near)]
    (last,) = yield [(add_low(total[1], other[1]), far)]
    return [total[0], other[0], last]


class Run:
    def __init__(self, steps):
        self.steps, self.pending, self.result = steps, None, None

    def step(self, token=None):
        try:
            wanted = self.steps.send(self.pending)
        except StopIteration as stop:
            self.pending, self.result = None, stop.value
            return token
        arrays, bits = [w[0] for w in wanted], [w[1:] for w in wanted]
        if token is not None:
            arrays, token = tie((arrays, token))
        self.pending = [exchange(array, *bit) for array, bit in zip(arrays, bits)]
        return token


def tie(values):
    return lax.optimization_barrier(values)


def one_less_exp(y):
    series = jnp.ones_like(y)
    for n in range(9, 1, -1):
        series = 1.0 - series * y * (1.0 / n)
    return jnp.where(y < 0.5, y * series, 1.0 - jnp.exp(-y))


def on_device(
    tokens,
    lengths,
    cotangent,
    norm_gain,
    norm_shift,
    value_weight,
    value_bias,
    reduce_weight,
    reduce_bias,
    decay_rates,
    skip_gain,
    state_weight,
    expand_weight,
    expand_bias,
    out_weight,
    out_bias,
):
    half, single = HALF, SINGLE
    shards = 1 << MAIN
    me = (device_number() >> low_bits()).reshape(1).astype(jnp.int32)
    vectors = [
        gather_low(v)
        for v in (
            norm_gain,
            norm_shift,
            value_bias,
            reduce_bias,
            decay_rates,
            skip_gain,
            expand_bias,
            out_bias,
        )
    ]
    sizes = [v.shape[0] for v in vectors]
    small, expand_rows, out_rows = pack_kernel(
        vectors,
        gather_low(reduce_weight),
        gather_low(state_weight),
        gather_low(expand_weight),
        gather_low(out_weight),
    )
    value_part, small = tie((value_weight, small))
    value_mat = lax.all_gather(value_part.astype(half), ("dp", "seq"), axis=0, tiled=True)
    channels = state_weight.shape[1]
    width = tokens.shape[-1]
    blocks = value_weight.shape[1] // width
    row_count, block, _ = tokens.shape
    place = lax.axis_index("seq").reshape(1).astype(jnp.int32)
    base = place * block
    positions = base + jnp.arange(block, dtype=jnp.int32)
    ends = jnp.cumsum(lengths, axis=-1).reshape(-1)
    live = ends[-1:]
    token_rows, cot_rows = tokens.reshape(block, width), cotangent.reshape(block, width)
    branch_grad = jnp.where((positions < live)[:, None], cot_rows, jnp.zeros_like(cot_rows))
    out_fold = fold(branch_grad.astype(single))

    small_run = Run(gather_steps(small, True))
    small_run.step()
    small_run.pending, expand_rows, out_rows, branch_grad, out_fold, ends = tie(
        (small_run.pending, expand_rows, out_rows, branch_grad, out_fold, ends)
    )
    small_run.step()
    expand_run = Run(gather_steps(expand_rows))
    expand_run.step()
    small_run.pending, expand_run.pending, out_rows = tie(
        (small_run.pending, expand_run.pending, out_rows)
    )
    small_run.step()
    expand_run.step()
    out_run = Run(gather_steps(out_rows, early=True))
    out_run.step()
    small_run.pending, expand_run.pending, out_run.pending = tie(
        (small_run.pending, expand_run.pending, out_run.pending)
    )
    small_run.step()
    small_run.pending, expand_run.pending, out_run.pending = tie(
        (small_run.pending, expand_run.pending, out_run.pending)
    )
    small_run.step()
    small_parts = small_run.result
    me = expand_run.step(me)
    me = out_run.step(me)

    vectors = unpack_kernel(me, sizes, small_parts)
    gain, shift, value_add, reduce_add, _, skip, expand_add, out_add = vectors[:8]
    decays, inflow, inflow_pull = vectors[8:]
    normed, act, reduce_slope, states, spans, own_map = reduce_kernel(
        me, ends, base, token_rows, gain, shift, reduce_add, decays, inflow, small_parts
    )
    own_map, expand_run.pending, out_run.pending, me = tie(
        (own_map, expand_run.pending, out_run.pending, me)
    )
    me = expand_run.step(me)
    maps = gather_maps(own_map)
    maps, me = out_run.step((maps, me))
    states_low, prior, ssm_low = states_kernel(
        me, place, ends, base, maps, spans, states, act, skip, inflow, decays, small_parts
    )
    expand_run.pending, out_run.pending, ssm_low, me = tie(
        (expand_run.pending, out_run.pending, ssm_low, me)
    )
    expand_run.step()
    me = out_run.step(me)
    expand_run.pending, me = tie((expand_run.pending, me))
    expand_run.step()
    expand_parts = expand_run.result

    value_act, gated, gate_slope, out_send, out_keep = forward_kernel(
        me, normed, ssm_low, branch_grad, value_add, expand_add, value_mat, expand_parts
    )
    out_run.pending, gated, me = tie((out_run.pending, gated, me))
    out_run.step()
    out_run.pending, out_other, me = tie((out_run.pending, core_exchange(out_send), me))
    out_run.step()
    out_parts = out_run.result

    out_run = Run(reduce_steps([(out_keep, out_other)]))
    me = out_run.step(me)
    value_grad, expand_fold, value_fold, ssm_grad, *halves = gate_kernel(
        me, branch_grad, normed, ssm_low, value_act, gate_slope, out_parts, expand_parts
    )
    out_run.pending, halves, me = tie((out_run.pending, halves, me))

    others = [core_exchange(halves[0]), core_exchange(halves[2])]
    me = out_run.step(me)
    ssm_grad, totals, back_spans, back_map, skip_fold = state_kernel(
        me, ends, base, ssm_grad, act, decays, small_parts
    )
    out_run.pending, others, ssm_grad, back_map, me = tie(
        (out_run.pending, others, ssm_grad, back_map, me)
    )

    back_maps = gather_maps(back_map)
    value_run = Run(reduce_steps([(halves[1], others[0])]))
    expand_run = Run(reduce_steps([(halves[3], others[1])]))
    back_maps, me = value_run.step((back_maps, me))
    me = out_run.step(me)
    reduce_grad, grad_tokens, channel_folds, norm_folds = input_kernel(
        me, place, ends, base, back_maps, back_spans, totals, act, prior, ssm_grad, reduce_slope,
        skip, inflow, decays, gain, token_rows, cot_rows, value_grad, value_mat, small_parts
    )
    value_run.pending, out_run.pending, reduce_grad, norm_folds, me = tie(
        (value_run.pending, out_run.pending, reduce_grad, norm_folds, me)
    )

    me = value_run.step(me)
    me, norm_folds = expand_run.step((me, norm_folds))
    me = out_run.step(me)
    reduce_halves = weight_grad(normed, reduce_grad, channels, me, "grad_reduce", 6)
    table_halves = sums_kernel(
        me, sizes, norm_folds, value_fold, channel_folds, inflow_pull, skip_fold, expand_fold,
        out_fold
    )
    state_halves = weight_grad(states_low, ssm_grad, channels, me, "grad_state", 6)
    small_halves = (reduce_halves, state_halves, table_halves)
    reduce_halves, state_halves, table_halves, me = tie((*small_halves, me))
    small_halves = (reduce_halves, state_halves, table_halves)
    small_other = core_exchange(jnp.concatenate([h[0] for h in small_halves], axis=1))
    output = out_kernel(me, live, base, gated, token_rows, out_add, out_parts)
    value_run.pending, expand_run.pending, out_run.pending, small_other, output = tie(
        (value_run.pending, expand_run.pending, out_run.pending, small_other, output)
    )

    small_pairs, at = [], 0
    for _, keep in small_halves:
        small_pairs.append((keep, small_other[:, at : at + keep.shape[1]]))
        at += keep.shape[1]
    small_run = Run(reduce_steps(small_pairs, True))
    small_run.step()
    value_run.step()
    expand_run.step()
    out_run.step()
    value_run.pending, expand_run.pending, small_run.pending = tie(
        (value_run.pending, expand_run.pending, small_run.pending)
    )

    small_run.step()
    value_run.step()
    expand_run.step()
    value_run.pending, expand_run.pending, small_run.pending = tie(
        (value_run.pending, expand_run.pending, small_run.pending)
    )
    for run in (value_run, expand_run, small_run, out_run):
        while run.result is None:
            run.step()
    value_sum, expand_sum, out_sum, reduce_sum, state_sum, *vector_sums = finish_kernel(
        sizes, value_run.result, expand_run.result, out_run.result, small_run.result, width // shards, channels // shards, width * blocks
    )
    vector_sums = [reduce_low(v[0]) for v in vector_sums]
    return (
        output.reshape(tokens.shape),
        grad_tokens.reshape(tokens.shape),
        vector_sums[0],
        vector_sums[1],
        reduce_low(value_sum),
        vector_sums[2],
        reduce_low(reduce_sum),
        vector_sums[3],
        vector_sums[4],
        vector_sums[5],
        reduce_low(state_sum),
        reduce_low(expand_sum),
        vector_sums[6],
        reduce_low(out_sum),
        vector_sums[7],
    )


def solution(mesh):
    rows, vector, matrix = P("dp", "seq", None), P(("dp", "seq")), P(("dp", "seq"), None)
    return jax.shard_map(
        on_device,
        mesh=mesh,
        in_specs=(
            rows,
            P("dp", None),
            rows,
            vector,
            vector,
            matrix,
            vector,
            matrix,
            vector,
            vector,
            vector,
            matrix,
            matrix,
            vector,
            matrix,
            vector,
        ),
        out_specs=(
            rows,
            rows,
            vector,
            vector,
            matrix,
            vector,
            matrix,
            vector,
            vector,
            vector,
            matrix,
            matrix,
            vector,
            matrix,
            vector,
        ),
        check_vma=False,
    )
```
